32 devices in a mesh: ctx: 16 (over z, y, core), fsdp: 2 (over x).
Axes of the slice: x: 2, y: 2, z: 4, core: 2. Of those that a mesh axis runs over, the one named last changes fastest.
Arguments:
- tokens: bfloat16 [2, 4096, 768], P('fsdp', 'ctx'), may hold values from -6 to 6
- lengths: int32 [2], P('fsdp'), may hold values from 1024 to 4096, as said below
- cotangent: bfloat16 [2, 4096, 768], P('fsdp', 'ctx'), may hold values from -6 to 6
- query_weight: bfloat16 [768, 768], P('ctx', 'fsdp'), may hold values from -0.21875 to 0.21875
- key_weight: bfloat16 [768, 768], P('ctx', 'fsdp'), may hold values from -0.21875 to 0.21875
- value_weight: bfloat16 [768, 768], P('ctx', 'fsdp'), may hold values from -0.21875 to 0.21875
- out_weight: bfloat16 [768, 768], P('ctx', 'fsdp'), may hold values from -6 to 6
- in_weight: bfloat16 [768, 3072], P('ctx', 'fsdp'), may hold values from -0.21875 to 0.21875
- down_weight: bfloat16 [3072, 768], P('ctx', 'fsdp'), may hold values from -0.109375 to 0.109375
- query_bias: bfloat16 [768], P('ctx'), may hold values from -3 to 3
- value_bias: bfloat16 [768], P('ctx'), may hold values from -0.119628906 to 0.119628906
- out_bias: bfloat16 [768], P('ctx'), may hold values from -3 to 3
- attn_norm_gain: bfloat16 [768], P('ctx'), may hold values from 0.5 to 1.5
- attn_norm_bias: bfloat16 [768], P('ctx'), may hold values from -2 to 2
- in_bias: bfloat16 [3072], P('ctx'), may hold values from -3 to 3
- down_bias: bfloat16 [768], P('ctx'), may hold values from -3 to 3
- ffn_norm_gain: bfloat16 [768], P('ctx'), may hold values from 0.5 to 1.5
- ffn_norm_bias: bfloat16 [768], P('ctx'), may hold values from -2 to 2
Outputs:
- layer_out: bfloat16 [2, 4096, 768], P('fsdp', 'ctx')
- tokens_grad: bfloat16 [2, 4096, 768], P('fsdp', 'ctx')
- grad_query_weight: float32 [768, 768], P('ctx', 'fsdp')
- grad_key_weight: float32 [768, 768], P('ctx', 'fsdp')
- grad_value_weight: float32 [768, 768], P('ctx', 'fsdp')
- grad_out_weight: float32 [768, 768], P('ctx', 'fsdp')
- grad_in_weight: float32 [768, 3072], P('ctx', 'fsdp')
- grad_down_weight: float32 [3072, 768], P('ctx', 'fsdp')
- grad_query_bias: float32 [768], P('ctx')
- grad_value_bias: float32 [768], P('ctx')
- grad_out_bias: float32 [768], P('ctx')
- grad_attn_norm_gain: float32 [768], P('ctx')
- grad_attn_norm_bias: float32 [768], P('ctx')
- grad_in_bias: float32 [3072], P('ctx')
- grad_down_bias: float32 [768], P('ctx')
- grad_ffn_norm_gain: float32 [768], P('ctx')
- grad_ffn_norm_bias: float32 [768], P('ctx')
- rms_values: float32 [3], replicated
The draws below stay inside these ranges and needn't reach their ends.
Inputs may be any that keep to these rules, and one draw needn't show every extreme that they name: `lengths`: each sequence has between 1024 and 4096 valid slots; some sequence has exactly 4096, another exactly 1024.
All inputs are finite; a program needn't handle non-finite values.
Results may differ from the reference program's by a relative error of at most 0.022.
Values may be sent and summed in bfloat16 or wider, within the bound.
No kernel may reach another device: no remote copies, remote signals or barrier semaphores. Data moves between devices by JAX's collectives and lax.ppermute only.
A program may use at most 192 MiB of HBM per device.

```python
import jax
import jax.numpy as jnp
from jax import lax

D = 768
HEADS = 12
HEAD_DIM = 64
FF = 3072
LENGTH = 4096
SEQS = 2


def draw_lengths(key, part):
    drawn = jax.random.randint(key, (SEQS,), LENGTH // 4, LENGTH + 1)
    longest = jax.random.randint(jax.random.fold_in(key, 1), (), 0, SEQS)
    drawn = drawn.at[longest].set(LENGTH)
    shortest = (longest + 1) % SEQS
    return drawn.at[shortest].set(LENGTH // 4).astype(jnp.int32)


def levels(rng, dims, cuts, least, top_value):
    gain, own = 1.0, jax.random.fold_in(rng, 6)
    for dim, blocks in cuts:
        draws = jnp.exp(jax.random.uniform(jax.random.fold_in(own, dim), (blocks,), jnp.float32, least / len(cuts), top_value / len(cuts)))
        gain = gain * jnp.repeat(draws, dims[dim] // blocks).reshape([-1 if axis == dim else 1 for axis in range(len(dims))])
    return gain


def gaussian(stream_key, extent, deviation, bound, split=(), held_as=jnp.bfloat16):
    values = jax.random.normal(stream_key, extent, jnp.float32) * deviation
    if len(split) > 0:
        values = levels(stream_key, extent, split, -0.22, 0.18) * values
    return jnp.clip(values, min=-bound, max=bound).astype(held_as)


def setup_inputs(seed: int = 0) -> dict:
    splits = jax.random.split(jax.random.key(seed), 19)
    return {
        "tokens": gaussian(splits[0], (SEQS, LENGTH, D), 1.0, 6.0, ((0, 2), (1, 16))),
        "lengths": draw_lengths(jax.random.fold_in(splits[18], 71), 0),
        "cotangent": gaussian(splits[2], (SEQS, LENGTH, D), 1.0, 6.0, ((0, 2), (1, 16))),
        "query_weight": gaussian(splits[3], (D, D), D ** -0.5, 0.21875, ((0, 16), (1, 2))),
        "key_weight": gaussian(splits[4], (D, D), D ** -0.5, 0.21875, ((0, 16), (1, 2))),
        "value_weight": gaussian(splits[5], (D, D), D ** -0.5, 0.21875, ((0, 16), (1, 2))),
        "out_weight": gaussian(splits[6], (D, D), (max(1, 4 * D // LENGTH)) ** -0.5, 6.0, ((0, 16), (1, 2))),
        "in_weight": gaussian(splits[7], (D, FF), D ** -0.5, 0.21875, ((0, 16), (1, 2))),
        "down_weight": gaussian(splits[8], (FF, D), FF ** -0.5, 0.109375, ((0, 16), (1, 2))),
        "query_bias": gaussian(splits[9], (D,), 0.5, 3.0, ((0, 16),)),
        "value_bias": gaussian(splits[10], (D,), 0.02, 0.119628906, ((0, 16),)),
        "out_bias": gaussian(splits[11], (D,), 0.5, 3.0, ((0, 16),)),
        "attn_norm_gain": jnp.clip(1.0 + 0.1 * jax.random.normal(splits[12], (D,), jnp.float32), 0.5, 1.5).astype(jnp.bfloat16),
        "attn_norm_bias": gaussian(splits[13], (D,), 0.3, 2.0, ((0, 16),)),
        "in_bias": gaussian(splits[14], (FF,), 0.5, 3.0, ((0, 16),)),
        "down_bias": gaussian(splits[15], (D,), 0.5, 3.0, ((0, 16),)),
        "ffn_norm_gain": jnp.clip(1.0 + 0.1 * jax.random.normal(splits[16], (D,), jnp.float32), 0.5, 1.5).astype(jnp.bfloat16),
        "ffn_norm_bias": gaussian(splits[17], (D,), 0.3, 2.0, ((0, 16),)),
    }


@jax.custom_vjp
def low(v):
    return lax.optimization_barrier(v.astype(jnp.bfloat16)).astype(jnp.float32)

@jax.custom_vjp
def low_back(v):
    return v

def low_keep(v):
    return (low(v), None)

def low_pass(kept, grad):
    return (grad,)

def back_keep(v):
    return (v, None)

def back_low(kept, grad):
    return (low(grad),)
low.defvjp(low_keep, low_pass)
low_back.defvjp(back_keep, back_low)
highest = lax.Precision.HIGHEST
norm_eps = 1e-12
score_scale = 0.125
masked_score = -1000000000.0

def layer_norm(stream, gain_vec, shift_vec):
    center = lax.optimization_barrier(jnp.mean(stream, axis=-1, keepdims=True))
    offset = stream - center
    spread = lax.optimization_barrier(jnp.mean(offset * offset, axis=-1, keepdims=True))
    return offset * lax.rsqrt(spread + norm_eps) * gain_vec + shift_vec

def product(left_side, right_side):
    return jnp.dot(left_side, right_side, precision=highest)

def forward(token_rows, weights, valid_rows, key_ok):
    query_weight, key_weight, value_weight, out_weight, in_weight, down_weight, query_bias, value_bias, out_bias, attn_norm_gain, attn_norm_bias, in_bias, down_bias, ffn_norm_gain, ffn_norm_bias = weights
    seq_length = token_rows.shape[0]
    queries = low(low_back(product(token_rows, query_weight) + query_bias))
    key_rows = low(low_back(product(token_rows, key_weight)))
    values = low(low_back(product(token_rows, value_weight) + value_bias))

    def split_heads(matrix):
        return matrix.reshape(seq_length, HEADS, HEAD_DIM).transpose(1, 0, 2)

    def one_head(triple):
        query_head, key_head, value_head = triple
        scores = low_back(product(query_head, key_head.T) * score_scale)
        scores = jnp.where(key_ok[None, :], scores, masked_score)
        row_peak = lax.optimization_barrier(jnp.max(scores, axis=-1, keepdims=True))
        row_expo = jnp.exp(scores - row_peak)
        attn_probs = row_expo / lax.optimization_barrier(jnp.sum(row_expo, axis=-1, keepdims=True))
        return product(low(attn_probs), value_head)
    heads_out = lax.map(jax.checkpoint(one_head), (split_heads(queries), split_heads(key_rows), split_heads(values)))
    mixed_out = low(low_back(heads_out.transpose(1, 0, 2).reshape(seq_length, HEADS * HEAD_DIM)))
    attn_branch = low_back(product(mixed_out, out_weight) + out_bias)
    stream = token_rows + attn_branch
    norm_one = layer_norm(stream, attn_norm_gain, attn_norm_bias)
    inner_pre = low_back(product(low(norm_one), in_weight) + in_bias)
    act_out = low(jax.nn.gelu(inner_pre, approximate=False))
    ffn_branch = low_back(product(act_out, down_weight) + down_bias)
    column = valid_rows[:, None]
    final_out = column * layer_norm(norm_one + ffn_branch, ffn_norm_gain, ffn_norm_bias)
    moments = jnp.stack([jnp.sum(column * stream * stream), jnp.sum(column * attn_branch * attn_branch), jnp.sum(column * ffn_branch * ffn_branch)])
    return (final_out, moments)

def reference(tokens, lengths, cotangent, query_weight, key_weight, value_weight, out_weight, in_weight, down_weight, query_bias, value_bias, out_bias, attn_norm_gain, attn_norm_bias, in_bias, down_bias, ffn_norm_gain, ffn_norm_bias):
    weights = tuple((entry.astype(jnp.float32) for entry in (query_weight, key_weight, value_weight, out_weight, in_weight, down_weight, query_bias, value_bias, out_bias, attn_norm_gain, attn_norm_bias, in_bias, down_bias, ffn_norm_gain, ffn_norm_bias)))
    positions = jnp.arange(LENGTH)

    def one_sequence(loop_state, seq_item):
        seq_tokens, seq_length, seq_grad = seq_item
        key_ok = positions < seq_length
        valid_rows = key_ok.astype(jnp.float32)

        def apply_layer(stream, params):
            return forward(stream, params, valid_rows, key_ok)
        final_out, pullback, moments = jax.vjp(apply_layer, seq_tokens.astype(jnp.float32), weights, has_aux=True)
        grad_tokens, grad_weights = pullback(seq_grad.astype(jnp.float32))
        running, moment_sums = loop_state
        running = jax.tree.map(jnp.add, running, grad_weights)
        return ((running, moment_sums + moments), (final_out.astype(jnp.bfloat16), grad_tokens.astype(jnp.bfloat16)))
    zeros_grads = tuple((jnp.zeros_like(entry) for entry in weights))
    (grads, moment_sums), (layer_out, tokens_grad) = lax.scan(one_sequence, (zeros_grads, jnp.zeros((3,), jnp.float32)), (tokens, lengths, cotangent))
    valid_count = jnp.sum(lengths).astype(jnp.float32) * D
    rms_values = jnp.sqrt(moment_sums / valid_count)
    return (layer_out, tokens_grad, grads[0], grads[1], grads[2], grads[3], grads[4], grads[5], grads[6], grads[7], grads[8], grads[9], grads[10], grads[11], grads[12], grads[13], grads[14], rms_values)
```

```python
import functools

import jax
import jax.numpy as jnp
from jax import lax
from jax.experimental import pallas as pl
from jax.experimental.pallas import tpu as pltpu
from jax.sharding import PartitionSpec as P

HEAD_DIM = 64


norm_eps = 1e-12
score_scale = 0.125
masked_score = -1000000000.0
rows_contract = (((0,), (0,)), ((), ()))
columns_contract = (((1,), (1,)), ((), ()))


def layer_norm(stream, gain_vec, shift_vec):
    center = jnp.mean(stream, axis=-1, keepdims=True)
    offset = stream - center
    spread = jnp.mean(offset * offset, axis=-1, keepdims=True)
    return offset * lax.rsqrt(spread + norm_eps) * gain_vec + shift_vec


def gelu_exact(inner_pre):
    return jax.nn.gelu(inner_pre, approximate=False)


def plain_product(left_side, right_side):
    return jnp.dot(left_side, right_side, preferred_element_type=jnp.float32)


def row_product(left_side, right_side):
    return lax.dot_general(left_side, right_side, rows_contract, preferred_element_type=jnp.float32)


def column_product(left_side, right_side):
    return lax.dot_general(
        left_side, right_side, columns_contract, preferred_element_type=jnp.float32
    )


def head_scores(query_head, key_head, key_ok):
    scores = (
        jnp.einsum("sqd,skd->sqk", query_head, key_head, preferred_element_type=jnp.float32)
        * score_scale
    )
    return jnp.where(key_ok[:, None, :], scores, masked_score)


def attend(query_seq, pair_all, key_ok):
    seq_count, slot_count, model_width = query_seq.shape
    heads_count = model_width // HEAD_DIM

    def one_head(head_index, loop_state):
        mixed_out, log_totals = loop_state
        head_start = head_index * HEAD_DIM
        query_head = lax.dynamic_slice_in_dim(query_seq, head_start, HEAD_DIM, 2)
        key_head = lax.dynamic_slice_in_dim(pair_all, head_start, HEAD_DIM, 2)
        value_head = lax.dynamic_slice_in_dim(pair_all, model_width + head_start, HEAD_DIM, 2)
        scores = head_scores(query_head, key_head, key_ok)
        row_peak = jnp.max(scores, axis=-1, keepdims=True)
        row_expo = jnp.exp(scores - row_peak)
        row_total = jnp.sum(row_expo, axis=-1, keepdims=True)
        attn_probs = (row_expo / row_total).astype(jnp.bfloat16)
        head_out = jnp.einsum(
            "sqk,skd->sqd", attn_probs, value_head, preferred_element_type=jnp.float32
        )
        mixed_out = lax.dynamic_update_slice_in_dim(mixed_out, head_out, head_start, 2)
        log_row = row_peak[..., 0] + jnp.log(row_total[..., 0])
        log_totals = lax.dynamic_update_index_in_dim(log_totals, log_row, head_index, 0)
        return (mixed_out, log_totals)

    start_state = (
        jnp.zeros((seq_count, slot_count, model_width), jnp.float32),
        jnp.zeros((heads_count, seq_count, slot_count), jnp.float32),
    )
    return lax.fori_loop(0, heads_count, one_head, start_state)


def attend_back(query_seq, pair_all, key_ok, log_totals, grad_mixed):
    seq_count, slot_count, model_width = query_seq.shape
    heads_count = model_width // HEAD_DIM

    def one_head(head_index, loop_state):
        grad_query, grad_pair = loop_state
        head_start = head_index * HEAD_DIM
        query_head = lax.dynamic_slice_in_dim(query_seq, head_start, HEAD_DIM, 2)
        key_head = lax.dynamic_slice_in_dim(pair_all, head_start, HEAD_DIM, 2)
        value_head = lax.dynamic_slice_in_dim(pair_all, model_width + head_start, HEAD_DIM, 2)
        grad_head = lax.dynamic_slice_in_dim(grad_mixed, head_start, HEAD_DIM, 2)
        scores = head_scores(query_head, key_head, key_ok)
        log_row = lax.dynamic_index_in_dim(log_totals, head_index, 0, keepdims=False)
        attn_probs = jnp.exp(scores - log_row[..., None])
        probs_b = attn_probs.astype(jnp.bfloat16)
        grad_probs = jnp.einsum(
            "sqd,skd->sqk", grad_head, value_head, preferred_element_type=jnp.float32
        )
        row_inner = jnp.sum(attn_probs * grad_probs, axis=-1, keepdims=True)
        grad_scores = (attn_probs * (grad_probs - row_inner)).astype(jnp.bfloat16)
        grad_query_head = (
            jnp.einsum("sqk,skd->sqd", grad_scores, key_head, preferred_element_type=jnp.float32)
            * score_scale
        )
        grad_key_head = (
            jnp.einsum("sqk,sqd->skd", grad_scores, query_head, preferred_element_type=jnp.float32)
            * score_scale
        )
        grad_value_head = jnp.einsum(
            "sqk,sqd->skd", probs_b, grad_head, preferred_element_type=jnp.float32
        )
        grad_query = lax.dynamic_update_slice_in_dim(grad_query, grad_query_head, head_start, 2)
        grad_pair = lax.dynamic_update_slice_in_dim(grad_pair, grad_key_head, head_start, 2)
        grad_pair = lax.dynamic_update_slice_in_dim(
            grad_pair, grad_value_head, model_width + head_start, 2
        )
        return (grad_query, grad_pair)

    start_state = (jnp.zeros(query_seq.shape, jnp.float32), jnp.zeros(pair_all.shape, jnp.float32))
    return lax.fori_loop(0, heads_count, one_head, start_state)


def column_sums(matrix_b):
    return jnp.sum(matrix_b.astype(jnp.float32), axis=0)


def body(
    tokens,
    lengths,
    cotangent,
    query_weight,
    key_weight,
    value_weight,
    out_weight,
    in_weight,
    down_weight,
    query_bias,
    value_bias,
    out_bias,
    attn_norm_gain,
    attn_norm_bias,
    in_bias,
    down_bias,
    ffn_norm_gain,
    ffn_norm_bias,
):
    seq_count, slot_count, model_width = tokens.shape
    row_count = seq_count * slot_count
    ctx_size = lax.axis_size("ctx")
    ctx_index = lax.axis_index("ctx")
    row_parts = (
        lax.all_gather(query_weight, "ctx", axis=0, tiled=True),
        lax.all_gather(key_weight, "ctx", axis=0, tiled=True),
        lax.all_gather(value_weight, "ctx", axis=0, tiled=True),
        lax.all_gather(out_weight, "ctx", axis=0, tiled=True),
        lax.all_gather(in_weight, "ctx", axis=0, tiled=True),
        lax.all_gather(down_weight, "ctx", axis=0, tiled=True),
        lax.all_gather(query_bias, "ctx", axis=0, tiled=True),
        lax.all_gather(value_bias, "ctx", axis=0, tiled=True),
        lax.all_gather(out_bias, "ctx", axis=0, tiled=True),
        lax.all_gather(attn_norm_gain, "ctx", axis=0, tiled=True),
        lax.all_gather(attn_norm_bias, "ctx", axis=0, tiled=True),
        lax.all_gather(in_bias, "ctx", axis=0, tiled=True),
        lax.all_gather(down_bias, "ctx", axis=0, tiled=True),
        lax.all_gather(ffn_norm_gain, "ctx", axis=0, tiled=True),
        lax.all_gather(ffn_norm_bias, "ctx", axis=0, tiled=True),
    )
    full_mats = (
        lax.all_gather(row_parts[0], "fsdp", axis=1, tiled=True),
        lax.all_gather(row_parts[1], "fsdp", axis=1, tiled=True),
        lax.all_gather(row_parts[2], "fsdp", axis=1, tiled=True),
        lax.all_gather(row_parts[3], "fsdp", axis=1, tiled=True),
        lax.all_gather(row_parts[4], "fsdp", axis=1, tiled=True),
        lax.all_gather(row_parts[5], "fsdp", axis=1, tiled=True),
    )
    query_full, key_full, value_full, out_full, in_full, down_full = full_mats
    query_vec = row_parts[6].astype(jnp.float32)
    value_vec = row_parts[7].astype(jnp.float32)
    out_vec = row_parts[8].astype(jnp.float32)
    gain_one = row_parts[9].astype(jnp.float32)
    bias_one = row_parts[10].astype(jnp.float32)
    in_vec = row_parts[11].astype(jnp.float32)
    down_vec = row_parts[12].astype(jnp.float32)
    gain_two = row_parts[13].astype(jnp.float32)
    bias_two = row_parts[14].astype(jnp.float32)
    local_slots = ctx_index * slot_count + jnp.arange(slot_count)
    local_ok = local_slots[None, :] < lengths[:, None]
    valid_mask = local_ok.astype(jnp.float32)
    valid_col = valid_mask.reshape(row_count, 1)
    key_ok = jnp.arange(slot_count * ctx_size)[None, :] < lengths[:, None]
    token_rows = tokens.reshape(row_count, model_width)
    queries_b = (plain_product(token_rows, query_full) + query_vec).astype(jnp.bfloat16)
    keys_b = plain_product(token_rows, key_full).astype(jnp.bfloat16)
    values_b = (plain_product(token_rows, value_full) + value_vec).astype(jnp.bfloat16)
    pair_local = jnp.concatenate([keys_b, values_b], axis=1).reshape(
        seq_count, slot_count, 2 * model_width
    )
    pair_all = lax.all_gather(pair_local, "ctx", axis=1, tiled=True)
    query_seq = queries_b.reshape(seq_count, slot_count, model_width)
    mixed_out, log_totals = attend(query_seq, pair_all, key_ok)
    mixed_b = mixed_out.reshape(row_count, model_width).astype(jnp.bfloat16)
    attn_branch = plain_product(mixed_b, out_full) + out_vec
    stream = token_rows.astype(jnp.float32) + attn_branch
    norm_one, norm_one_back = jax.vjp(layer_norm, stream, gain_one, bias_one)
    norm_one_b = norm_one.astype(jnp.bfloat16)
    inner_pre = plain_product(norm_one_b, in_full) + in_vec
    act_out, gelu_back = jax.vjp(gelu_exact, inner_pre)
    act_b = act_out.astype(jnp.bfloat16)
    ffn_branch = plain_product(act_b, down_full) + down_vec
    stream_two = norm_one + ffn_branch
    final_out, norm_two_back = jax.vjp(layer_norm, stream_two, gain_two, bias_two)
    layer_out = (
        (valid_col * final_out).astype(jnp.bfloat16).reshape(seq_count, slot_count, model_width)
    )
    grad_final = valid_col * cotangent.reshape(row_count, model_width).astype(jnp.float32)
    grad_stream_two, grad_gain_two, grad_bias_two = norm_two_back(grad_final)
    grad_ffn_b = grad_stream_two.astype(jnp.bfloat16)
    grad_down_vec = column_sums(grad_ffn_b)
    grad_down_full = row_product(act_b, grad_ffn_b)
    grad_inner_b = gelu_back(column_product(grad_ffn_b, down_full))[0].astype(jnp.bfloat16)
    grad_in_vec = column_sums(grad_inner_b)
    grad_in_full = row_product(norm_one_b, grad_inner_b)
    grad_norm_one = grad_stream_two + column_product(grad_inner_b, in_full)
    grad_stream, grad_gain_one, grad_bias_one = norm_one_back(grad_norm_one)
    grad_attn_b = grad_stream.astype(jnp.bfloat16)
    grad_out_vec = column_sums(grad_attn_b)
    grad_out_full = row_product(mixed_b, grad_attn_b)
    grad_mixed = (
        column_product(grad_attn_b, out_full)
        .astype(jnp.bfloat16)
        .reshape(seq_count, slot_count, model_width)
    )
    grad_query_seq, grad_pair = attend_back(query_seq, pair_all, key_ok, log_totals, grad_mixed)
    grad_pair_local = lax.psum_scatter(
        grad_pair.astype(jnp.bfloat16), "ctx", scatter_dimension=1, tiled=True
    ).astype(jnp.float32)
    grad_keys_b = (
        grad_pair_local[:, :, :model_width].reshape(row_count, model_width).astype(jnp.bfloat16)
    )
    grad_values_b = (
        grad_pair_local[:, :, model_width:].reshape(row_count, model_width).astype(jnp.bfloat16)
    )
    grad_queries_b = grad_query_seq.reshape(row_count, model_width).astype(jnp.bfloat16)
    grad_query_full = row_product(token_rows, grad_queries_b)
    grad_query_vec = column_sums(grad_queries_b)
    grad_key_full = row_product(token_rows, grad_keys_b)
    grad_value_full = row_product(token_rows, grad_values_b)
    grad_value_vec = column_sums(grad_values_b)
    tokens_grad = (
        (
            grad_stream
            + column_product(grad_queries_b, query_full)
            + column_product(grad_keys_b, key_full)
            + column_product(grad_values_b, value_full)
        )
        .astype(jnp.bfloat16)
        .reshape(seq_count, slot_count, model_width)
    )
    narrow = (
        lax.psum_scatter(
            grad_query_full.astype(jnp.bfloat16), "fsdp", scatter_dimension=1, tiled=True
        ).astype(jnp.float32),
        lax.psum_scatter(
            grad_key_full.astype(jnp.bfloat16), "fsdp", scatter_dimension=1, tiled=True
        ).astype(jnp.float32),
        lax.psum_scatter(
            grad_value_full.astype(jnp.bfloat16), "fsdp", scatter_dimension=1, tiled=True
        ).astype(jnp.float32),
        lax.psum_scatter(
            grad_out_full.astype(jnp.bfloat16), "fsdp", scatter_dimension=1, tiled=True
        ).astype(jnp.float32),
        lax.psum_scatter(
            grad_in_full.astype(jnp.bfloat16), "fsdp", scatter_dimension=1, tiled=True
        ).astype(jnp.float32),
        lax.psum_scatter(
            grad_down_full.astype(jnp.bfloat16), "fsdp", scatter_dimension=1, tiled=True
        ).astype(jnp.float32),
    )
    owned_grads = (
        lax.psum_scatter(
            narrow[0].astype(jnp.bfloat16), "ctx", scatter_dimension=0, tiled=True
        ).astype(jnp.float32),
        lax.psum_scatter(
            narrow[1].astype(jnp.bfloat16), "ctx", scatter_dimension=0, tiled=True
        ).astype(jnp.float32),
        lax.psum_scatter(
            narrow[2].astype(jnp.bfloat16), "ctx", scatter_dimension=0, tiled=True
        ).astype(jnp.float32),
        lax.psum_scatter(
            narrow[3].astype(jnp.bfloat16), "ctx", scatter_dimension=0, tiled=True
        ).astype(jnp.float32),
        lax.psum_scatter(
            narrow[4].astype(jnp.bfloat16), "ctx", scatter_dimension=0, tiled=True
        ).astype(jnp.float32),
        lax.psum_scatter(
            narrow[5].astype(jnp.bfloat16), "ctx", scatter_dimension=0, tiled=True
        ).astype(jnp.float32),
    )
    moments = jnp.stack(
        [
            jnp.sum(valid_col * stream * stream),
            jnp.sum(valid_col * attn_branch * attn_branch),
            jnp.sum(valid_col * ffn_branch * ffn_branch),
            jnp.sum(valid_col),
        ]
    )
    summed = lax.psum(
        (
            moments,
            grad_query_vec,
            grad_value_vec,
            grad_out_vec,
            grad_gain_one,
            grad_bias_one,
            grad_in_vec,
            grad_down_vec,
            grad_gain_two,
            grad_bias_two,
        ),
        ("ctx", "fsdp"),
    )
    width_shard = query_bias.shape[0]
    hidden_shard = in_bias.shape[0]

    def own_piece(vector_full, shard_len):
        return lax.dynamic_slice_in_dim(vector_full, ctx_index * shard_len, shard_len, 0)

    rms_values = jnp.sqrt(summed[0][:3] / (summed[0][3] * model_width))
    return (
        layer_out,
        tokens_grad,
        owned_grads[0],
        owned_grads[1],
        owned_grads[2],
        owned_grads[3],
        owned_grads[4],
        owned_grads[5],
        own_piece(summed[1], width_shard),
        own_piece(summed[2], width_shard),
        own_piece(summed[3], width_shard),
        own_piece(summed[4], width_shard),
        own_piece(summed[5], width_shard),
        own_piece(summed[6], hidden_shard),
        own_piece(summed[7], width_shard),
        own_piece(summed[8], width_shard),
        own_piece(summed[9], width_shard),
        rms_values,
    )


HEADS_HERE = 3
HEAD_COLS = HEADS_HERE * HEAD_DIM
rows_first = (((0,), (0,)), ((), ()))
lanes_both = (((1,), (1,)), ((), ()))
plain_contract = (((1,), (0,)), ((), ()))
kernel_params = pltpu.CompilerParams(vmem_limit_bytes=40 * 1024 * 1024)


def product32(left_side, right_side, contract):
    return lax.dot_general(left_side, right_side, contract, preferred_element_type=jnp.float32)


def ctx_move(value, mask, levels=None):
    pairs = [(i, i ^ mask) for i in range(16) if levels is None or (i >> 2) in levels]
    return lax.ppermute(value, "ctx", pairs)


def core_swap(value):
    return ctx_move(value, 1)


def y_swap(value):
    return ctx_move(value, 2)


def x_swap(value):
    return lax.ppermute(value, "fsdp", [(0, 1), (1, 0)])


def add_b(left_side, right_side):
    return (left_side.astype(jnp.float32) + right_side.astype(jnp.float32)).astype(jnp.bfloat16)


MIDDLE, ENDS = (1, 2), (0, 3)


def z_gather(block, at_end):
    one = ctx_move(block, 4)
    across = ctx_move(block, 12, MIDDLE)
    two_end = ctx_move(across, 4, MIDDLE)
    two_mid = ctx_move(one, 12, MIDDLE)
    three_end = ctx_move(two_mid, 4, MIDDLE)
    return one, jnp.where(at_end, two_end, two_mid), jnp.where(at_end, three_end, across)


def z_reduce(own, one, two, three):
    two_sum = add_b(two, ctx_move(three, 4, ENDS))
    three_sum = add_b(three, ctx_move(two, 4, ENDS))
    one_sum = add_b(one, ctx_move(two_sum, 12, MIDDLE))
    own_sum = add_b(own, ctx_move(three_sum, 12, MIDDLE))
    return add_b(own_sum, ctx_move(one_sum, 4))


def when_flag(flag_ref, run, idle):
    if flag_ref is None:
        run()
    else:
        pl.when(flag_ref[0] > 0)(run)
        pl.when(flag_ref[0] <= 0)(idle)


def attend_kernel(count, first, last, flagged, *refs):
    flag_ref = refs[0] if flagged else None
    refs = refs[flagged:]
    query_ref, pairs = refs[0], refs[1 : 1 + count]
    refs = refs[1 + count :]
    if not first:
        peak_in, total_in, mixed_in = refs[:3]
        refs = refs[3:]

    def one_head(head, carry):
        key_rows = pl.ds(pl.multiple_of(head * HEAD_DIM, HEAD_DIM), HEAD_DIM)
        value_rows = pl.ds(pl.multiple_of(HEAD_COLS + head * HEAD_DIM, HEAD_DIM), HEAD_DIM)
        query = query_ref[key_rows, :]
        width = query.shape[1]
        if first:
            peak = jnp.full((1, width), -1e30, jnp.float32)
            total = jnp.zeros((1, width), jnp.float32)
            mixed = jnp.zeros((HEAD_DIM, width), jnp.float32)
        else:
            peak, total, mixed = peak_in[head][0:1], total_in[head][0:1], mixed_in[key_rows, :]
        for pair in pairs:
            scores = product32(pair[key_rows, :], query, rows_first)
            new_peak = jnp.maximum(peak, jnp.max(scores, axis=0, keepdims=True))
            expo = jnp.exp(scores - new_peak)
            shrink = jnp.exp(peak - new_peak)
            total = total * shrink + jnp.sum(expo, axis=0, keepdims=True)
            mixed = mixed * shrink + product32(
                pair[value_rows, :], expo.astype(jnp.bfloat16), plain_contract
            )
            peak = new_peak
        if last:
            mixed_out, log_out = refs
            mixed_out[key_rows, :] = (mixed / total).astype(jnp.bfloat16)
            log_out[head] = jnp.broadcast_to(peak + jnp.log(total), (8, width))
        else:
            peak_out, total_out, sum_out = refs
            peak_out[head] = jnp.broadcast_to(peak, (8, width))
            total_out[head] = jnp.broadcast_to(total, (8, width))
            sum_out[key_rows, :] = mixed
        return carry

    def run():
        lax.fori_loop(0, HEADS_HERE, one_head, 0)

    def idle():
        for ref in refs:
            ref[...] = jnp.zeros_like(ref)

    when_flag(flag_ref, run, idle)


def attend_call(query, pairs, state=None, last=False, flag=None):
    width = query.shape[1]
    stat = jax.ShapeDtypeStruct((HEADS_HERE, 8, width), jnp.float32)
    if last:
        outs = [jax.ShapeDtypeStruct((HEAD_COLS, width), jnp.bfloat16), stat]
    else:
        outs = [stat, stat, jax.ShapeDtypeStruct((HEAD_COLS, width), jnp.float32)]
    ins = [query, *pairs, *(() if state is None else state)]
    specs = [pl.BlockSpec(memory_space=pltpu.VMEM)] * len(ins)
    if flag is not None:
        ins, specs = [flag, *ins], [pl.BlockSpec(memory_space=pltpu.SMEM), *specs]
    return pl.pallas_call(
        functools.partial(attend_kernel, len(pairs), state is None, last, int(flag is not None)),
        out_shape=outs,
        in_specs=specs,
        compiler_params=kernel_params,
    )(*ins)


def attend_back_kernel(count, first, flagged, *refs):
    flag_ref = refs[0] if flagged else None
    refs = refs[flagged:]
    query_ref, grad_ref, log_ref, inner_ref = refs[:4]
    pairs = refs[4 : 4 + count]
    refs = refs[4 + count :]
    if not first:
        grad_query_in, refs = refs[0], refs[1:]
    grad_query_out, grad_pairs = refs[0], refs[1:]

    def one_head(head, carry):
        key_rows = pl.ds(pl.multiple_of(head * HEAD_DIM, HEAD_DIM), HEAD_DIM)
        value_rows = pl.ds(pl.multiple_of(HEAD_COLS + head * HEAD_DIM, HEAD_DIM), HEAD_DIM)
        query, grad = query_ref[key_rows, :], grad_ref[key_rows, :]
        log_row, inner = log_ref[head][0:1], inner_ref[head][0:1]
        if first:
            grad_query = jnp.zeros((HEAD_DIM, query.shape[1]), jnp.float32)
        else:
            grad_query = grad_query_in[key_rows, :]
        for pair, grad_pair in zip(pairs, grad_pairs):
            keys = pair[key_rows, :]
            probs = jnp.exp(product32(keys, query, rows_first) - log_row)
            grad_probs = product32(pair[value_rows, :], grad, rows_first)
            grad_scores = (probs * (grad_probs - inner)).astype(jnp.bfloat16)
            grad_query = grad_query + product32(keys, grad_scores, plain_contract)
            grad_pair[key_rows, :] = product32(query, grad_scores, lanes_both).astype(jnp.bfloat16)
            grad_pair[value_rows, :] = product32(
                grad, probs.astype(jnp.bfloat16), lanes_both
            ).astype(jnp.bfloat16)
        grad_query_out[key_rows, :] = grad_query
        return carry

    def run():
        lax.fori_loop(0, HEADS_HERE, one_head, 0)

    def idle():
        for ref in refs:
            ref[...] = jnp.zeros_like(ref)

    when_flag(flag_ref, run, idle)


def attend_back_call(query, grad, log_rows, inner, pairs, grad_query=None, flag=None):
    outs = [jax.ShapeDtypeStruct(query.shape, jnp.float32)]
    outs += [jax.ShapeDtypeStruct(pair.shape, jnp.bfloat16) for pair in pairs]
    ins = [query, grad, log_rows, inner, *pairs, *(() if grad_query is None else (grad_query,))]
    specs = [pl.BlockSpec(memory_space=pltpu.VMEM)] * len(ins)
    if flag is not None:
        ins, specs = [flag, *ins], [pl.BlockSpec(memory_space=pltpu.SMEM), *specs]
    return pl.pallas_call(
        functools.partial(
            attend_back_kernel, len(pairs), grad_query is None, int(flag is not None)
        ),
        out_shape=outs,
        in_specs=specs,
        compiler_params=kernel_params,
    )(*ins)


def place_kernel(count, me_ref, *refs):
    blocks, (mats_ref, vecs_ref, sem) = refs[:count], refs[count:]
    me = me_ref[0]
    copies = []
    for slot, block in enumerate(blocks):
        core, z = slot // 4, slot % 4
        for y in range(2):
            owner = jnp.bitwise_xor(me, z * 4 + y * 2 + core)
            n = (slot * 2 + y) * 2
            copies.append(
                pltpu.make_async_copy(block.at[y, pl.ds(0, 48)], mats_ref.at[owner], sem.at[n])
            )
            copies.append(
                pltpu.make_async_copy(block.at[y, pl.ds(48, 8)], vecs_ref.at[owner], sem.at[n + 1])
            )
    for copy in copies:
        copy.start()
    for copy in copies:
        copy.wait()


def place_blocks(me, blocks):
    width = blocks[0].shape[-1]
    return pl.pallas_call(
        functools.partial(place_kernel, len(blocks)),
        out_shape=[
            jax.ShapeDtypeStruct((16, 48, width), jnp.bfloat16),
            jax.ShapeDtypeStruct((16, 8, width), jnp.bfloat16),
        ],
        in_specs=[pl.BlockSpec(memory_space=pltpu.SMEM)]
        + [pl.BlockSpec(memory_space=pl.ANY)] * len(blocks),
        out_specs=[pl.BlockSpec(memory_space=pl.ANY)] * 2,
        scratch_shapes=[pltpu.SemaphoreType.DMA((len(blocks) * 4,))],
    )(me, *blocks)


def all_sum(packed):
    for mask in (1, 2, 4, 8):
        packed = packed + ctx_move(packed, mask)
    return packed + x_swap(packed)


def fast_body(
    tokens,
    lengths,
    cotangent,
    query_weight,
    key_weight,
    value_weight,
    out_weight,
    in_weight,
    down_weight,
    query_bias,
    value_bias,
    out_bias,
    attn_norm_gain,
    attn_norm_bias,
    in_bias,
    down_bias,
    ffn_norm_gain,
    ffn_norm_bias,
):
    slot_count, width = tokens.shape[1:]
    me = lax.axis_index("ctx")
    x_at = lax.axis_index("fsdp")
    z_at, y_at, core_at = me >> 2, (me >> 1) & 1, me & 1
    at_end = (z_at == 0) | (z_at == 3)
    y_low, x_low, core_low = y_at == 0, x_at == 0, core_at == 0
    own_long = lengths[0] == slot_count * lax.axis_size("ctx")
    short_flag = (z_at == 0).astype(jnp.int32).reshape(1)

    out_all = lax.all_gather(out_weight, ("fsdp", "ctx"), axis=0, tiled=True).reshape(2, 768, 384)
    in_all = lax.all_gather(in_weight, ("fsdp", "ctx"), axis=0, tiled=True).reshape(2, 768, 1536)
    down_all = lax.all_gather(down_weight, ("fsdp", "ctx"), axis=0, tiled=True).reshape(
        2, 3072, 384
    )

    half = HEAD_COLS
    low_cols = jnp.concatenate(
        [query_weight[:, :half], key_weight[:, :half], value_weight[:, :half]], axis=1
    )
    high_cols = jnp.concatenate(
        [query_weight[:, half:], key_weight[:, half:], value_weight[:, half:]], axis=1
    )
    vectors = jnp.concatenate(
        [
            query_bias,
            value_bias,
            out_bias,
            attn_norm_gain,
            attn_norm_bias,
            in_bias,
            down_bias,
            ffn_norm_gain,
            ffn_norm_bias,
        ]
    )
    vector_rows = jnp.broadcast_to(vectors[None, :], (8, 576))
    keep_cols = jnp.concatenate([jnp.where(y_low, low_cols, high_cols), vector_rows], axis=0)
    send_cols = jnp.concatenate([jnp.where(y_low, high_cols, low_cols), vector_rows], axis=0)
    own_block = jnp.stack([keep_cols, y_swap(send_cols)])
    z_blocks = [own_block] + [ctx_move(own_block, mask) for mask in (4, 8, 12)]
    blocks = z_blocks + [core_swap(block) for block in z_blocks]
    qkv_weight, vecs = place_blocks(me.reshape(1), blocks)
    qkv_weight = qkv_weight.reshape(768, 576)
    vecs = vecs[:, 0, :].astype(jnp.float32)

    def vector(start, count):
        return vecs[:, start : start + count].reshape(16 * count)

    query_vec, value_vec, out_vec = vector(0, 48), vector(48, 48), vector(96, 48)
    gain_one, bias_one = vector(144, 48), vector(192, 48)
    in_vec = vector(240, 192)
    down_vec, gain_two, bias_two = vector(432, 48), vector(480, 48), vector(528, 48)
    head_start = 384 * x_at + half * y_at
    query_add = lax.dynamic_slice_in_dim(query_vec, head_start, half, 0)[:, None]
    value_add = lax.dynamic_slice_in_dim(value_vec, head_start, half, 0)[:, None]
    pair_add = jnp.concatenate([jnp.zeros_like(value_add), value_add], axis=0)

    token_rows = tokens[0]
    other_rows = x_swap(token_rows)
    long_own = jnp.where(own_long, token_rows, other_rows)
    short_own = jnp.where(own_long, other_rows, token_rows)
    long_rows = jnp.concatenate([long_own, y_swap(long_own)], axis=0)
    short_rows = jnp.concatenate([short_own, y_swap(short_own)], axis=0)

    def project(rows):
        query = product32(qkv_weight[:, :half], rows, (((0,), (1,)), ((), ()))) + query_add
        pair = product32(qkv_weight[:, half:], rows, (((0,), (1,)), ((), ()))) + pair_add
        scale = jnp.asarray(score_scale, jnp.bfloat16)
        return query.astype(jnp.bfloat16) * scale, pair.astype(jnp.bfloat16)

    long_query, long_pair = project(long_rows)
    short_query, short_pair = project(short_rows)
    z_pairs = (long_pair, *z_gather(long_pair, at_end))
    pairs = [(pair, core_swap(pair)) for pair in z_pairs]
    short_pairs = (short_pair, core_swap(short_pair))
    short_mixed, short_log = attend_call(short_query, short_pairs, last=True, flag=short_flag)
    state = None
    for step, both in enumerate(pairs):
        state = attend_call(long_query, both, state, last=step == 3)
    long_mixed, long_log = state

    rows_here = slot_count
    sent = jnp.concatenate([long_mixed[:, rows_here:], short_mixed[:, rows_here:]], axis=0)
    got = y_swap(sent)

    def by_y(mine, theirs):
        return jnp.concatenate(
            [jnp.where(y_low, mine, theirs), jnp.where(y_low, theirs, mine)], axis=0
        )

    long_heads = by_y(long_mixed[:, :rows_here], got[:half])
    short_heads = by_y(short_mixed[:, :rows_here], got[half:])
    own_heads = jnp.where(own_long, long_heads, short_heads)
    far_heads = x_swap(jnp.where(own_long, short_heads, long_heads))
    mixed_t = jnp.concatenate(
        [jnp.where(x_low, own_heads, far_heads), jnp.where(x_low, far_heads, own_heads)], axis=0
    )

    local_slots = me * slot_count + jnp.arange(slot_count)
    valid_col = (local_slots < lengths[0]).astype(jnp.float32)[:, None]
    attn_branch = (
        jnp.concatenate([product32(mixed_t, out_all[i], rows_first) for i in range(2)], axis=1)
        + out_vec
    )
    stream = token_rows.astype(jnp.float32) + attn_branch
    norm_one, norm_one_back = jax.vjp(layer_norm, stream, gain_one, bias_one)
    norm_one_b = norm_one.astype(jnp.bfloat16)
    inner_pre = [
        plain_product(norm_one_b, in_all[i]) + in_vec[1536 * i : 1536 * (i + 1)] for i in range(2)
    ]
    act_b, gelu_backs = [], []
    for part in inner_pre:
        act_out, gelu_back = jax.vjp(gelu_exact, part)
        act_b.append(act_out.astype(jnp.bfloat16))
        gelu_backs.append(gelu_back)
    act_all = jnp.concatenate(act_b, axis=1)
    ffn_branch = (
        jnp.concatenate([plain_product(act_all, down_all[i]) for i in range(2)], axis=1) + down_vec
    )
    stream_two = norm_one + ffn_branch
    final_out, norm_two_back = jax.vjp(layer_norm, stream_two, gain_two, bias_two)
    layer_out = (valid_col * final_out).astype(jnp.bfloat16)[None]
    grad_final = valid_col * cotangent[0].astype(jnp.float32)
    grad_stream_two, grad_gain_two, grad_bias_two = norm_two_back(grad_final)
    grad_ffn_b = grad_stream_two.astype(jnp.bfloat16)
    grad_down_vec = column_sums(grad_ffn_b)
    grad_down = jnp.concatenate(
        [row_product(act_all, grad_ffn_b[:, 384 * i : 384 * (i + 1)]) for i in range(2)], axis=0
    ).astype(jnp.bfloat16)
    grad_act = sum(
        column_product(grad_ffn_b[:, 384 * i : 384 * (i + 1)], down_all[i]) for i in range(2)
    )
    grad_inner_b = [
        gelu_backs[i](grad_act[:, 1536 * i : 1536 * (i + 1)])[0].astype(jnp.bfloat16)
        for i in range(2)
    ]
    grad_in_vec = jnp.concatenate([column_sums(part) for part in grad_inner_b])
    grad_in = jnp.concatenate([row_product(norm_one_b, part) for part in grad_inner_b], axis=0)
    grad_in = grad_in.astype(jnp.bfloat16)
    grad_norm_one = grad_stream_two + sum(
        column_product(grad_inner_b[i], in_all[i]) for i in range(2)
    )
    grad_stream, grad_gain_one, grad_bias_one = norm_one_back(grad_norm_one)
    grad_attn_b = grad_stream.astype(jnp.bfloat16)
    grad_out_vec = column_sums(grad_attn_b)
    grad_out = jnp.concatenate(
        [plain_product(mixed_t, grad_attn_b[:, 384 * i : 384 * (i + 1)]) for i in range(2)], axis=0
    ).astype(jnp.bfloat16)
    grad_mixed_t = sum(
        product32(out_all[i], grad_attn_b[:, 384 * i : 384 * (i + 1)], lanes_both)
        for i in range(2)
    ).astype(jnp.bfloat16)

    owned_out = lax.psum_scatter(grad_out, ("fsdp", "ctx"), scatter_dimension=0, tiled=True)
    owned_in = lax.psum_scatter(grad_in, ("fsdp", "ctx"), scatter_dimension=0, tiled=True)
    owned_down = lax.psum_scatter(grad_down, ("fsdp", "ctx"), scatter_dimension=0, tiled=True)

    keep_x = jnp.where(x_low, grad_mixed_t[:384], grad_mixed_t[384:])
    got_x = x_swap(jnp.where(x_low, grad_mixed_t[384:], grad_mixed_t[:384]))
    long_x = jnp.where(own_long, keep_x, got_x)
    short_x = jnp.where(own_long, got_x, keep_x)
    both_keep = jnp.where(y_low, long_x[:half], long_x[half:])
    short_keep = jnp.where(y_low, short_x[:half], short_x[half:])
    sent = jnp.concatenate(
        [
            jnp.where(y_low, long_x[half:], long_x[:half]),
            jnp.where(y_low, short_x[half:], short_x[:half]),
        ],
        axis=0,
    )
    got = y_swap(sent)
    long_grad = jnp.concatenate([both_keep, got[:half]], axis=1)
    short_grad = jnp.concatenate([short_keep, got[half:]], axis=1)

    def inner_rows(mixed, grad):
        product = mixed.astype(jnp.float32) * grad.astype(jnp.float32)
        sums = jnp.sum(product.reshape(HEADS_HERE, HEAD_DIM, -1), axis=1, keepdims=True)
        return jnp.broadcast_to(sums, (HEADS_HERE, 8, sums.shape[-1]))

    short_back = attend_back_call(
        short_query,
        short_grad,
        short_log,
        inner_rows(short_mixed, short_grad),
        short_pairs,
        flag=short_flag,
    )
    long_inner = inner_rows(long_mixed, long_grad)
    grad_query, reduced = None, [None] * 4
    for step in (3, 2, 1, 0):
        grad_query, near, far = attend_back_call(
            long_query, long_grad, long_log, long_inner, pairs[step], grad_query
        )
        reduced[step] = add_b(near, core_swap(far))
    long_pair_grad = z_reduce(*reduced)
    short_pair_grad = add_b(short_back[1], core_swap(short_back[2]))
    long_all = jnp.concatenate(
        [(grad_query * score_scale).astype(jnp.bfloat16), long_pair_grad], axis=0
    )
    short_all = jnp.concatenate(
        [(short_back[0] * score_scale).astype(jnp.bfloat16), short_pair_grad], axis=0
    )

    grad_qkv = product32(long_rows, long_all, (((0,), (1,)), ((), ()))) + product32(
        short_rows, short_all, (((0,), (1,)), ((), ()))
    )
    grad_qkv = grad_qkv.astype(jnp.bfloat16).reshape(4, 2, 2, 48, 576)
    core_keep = jnp.where(core_low, grad_qkv[:, :, 0], grad_qkv[:, :, 1])
    core_send = jnp.where(core_low, grad_qkv[:, :, 1], grad_qkv[:, :, 0])
    core_sum = add_b(core_keep, core_swap(core_send))
    own_sum = lax.dynamic_index_in_dim(core_sum, z_at, 0, keepdims=False).astype(jnp.float32)
    for mask in (1, 2, 3):
        piece = lax.dynamic_index_in_dim(core_sum, z_at ^ mask, 0, keepdims=False)
        own_sum = own_sum + ctx_move(piece, 4 * mask).astype(jnp.float32)
    y_keep = jnp.where(y_low, own_sum[0], own_sum[1])
    y_got = y_swap(jnp.where(y_low, own_sum[1], own_sum[0]).astype(jnp.bfloat16))
    y_got = y_got.astype(jnp.float32)
    low_part, high_part = jnp.where(y_low, y_keep, y_got), jnp.where(y_low, y_got, y_keep)
    owned_qkv = [
        jnp.concatenate(
            [low_part[:, half * i : half * (i + 1)], high_part[:, half * i : half * (i + 1)]],
            axis=1,
        )
        for i in range(3)
    ]

    def back_rows(grads):
        return product32(grads, qkv_weight, (((0,), (1,)), ((), ())))

    long_back, short_rows_back = back_rows(long_all), back_rows(short_all)
    sent = jnp.concatenate([long_back[rows_here:], short_rows_back[rows_here:]], axis=0)
    got = y_swap(sent.astype(jnp.bfloat16)).astype(jnp.float32)
    long_part = long_back[:rows_here] + got[:rows_here]
    short_part = short_rows_back[:rows_here] + got[rows_here:]
    own_part = jnp.where(own_long, long_part, short_part)
    far_part = x_swap(jnp.where(own_long, short_part, long_part).astype(jnp.bfloat16))
    tokens_grad = (grad_stream + own_part + far_part.astype(jnp.float32)).astype(jnp.bfloat16)

    moments = jnp.stack(
        [
            jnp.sum(valid_col * stream * stream),
            jnp.sum(valid_col * attn_branch * attn_branch),
            jnp.sum(valid_col * ffn_branch * ffn_branch),
            jnp.sum(valid_col),
        ]
    )
    packed = jnp.concatenate(
        [
            grad_out_vec,
            grad_gain_one,
            grad_bias_one,
            grad_in_vec,
            grad_down_vec,
            grad_gain_two,
            grad_bias_two,
            moments,
            jnp.zeros((508,), jnp.float32),
        ]
    )
    summed = all_sum(packed.reshape(64, 128)).reshape(8192)

    def lane_sums(first_part, second_part):
        return jnp.sum(first_part.astype(jnp.float32), axis=1) + jnp.sum(
            second_part.astype(jnp.float32), axis=1
        )

    query_sums = lane_sums(long_all[:half], short_all[:half])
    value_sums = lane_sums(long_all[2 * half :], short_all[2 * half :])
    at_heads = (jnp.arange(4) == 2 * x_at + y_at).astype(jnp.float32)[:, None]
    head_sums = jnp.concatenate(
        [
            (at_heads * query_sums[None, :]).reshape(6, 128),
            (at_heads * value_sums[None, :]).reshape(6, 128),
            jnp.zeros((4, 128), jnp.float32),
        ],
        axis=0,
    )
    head_sums = all_sum(head_sums).reshape(2048)

    def own_piece(vector_all, start, shard):
        return lax.dynamic_slice_in_dim(vector_all, start + me * shard, shard, 0)

    rms_values = jnp.sqrt(summed[7680:7683] / (summed[7683] * width))
    return (
        layer_out,
        tokens_grad[None],
        owned_qkv[0],
        owned_qkv[1],
        owned_qkv[2],
        owned_out.astype(jnp.float32),
        owned_in.astype(jnp.float32),
        owned_down.astype(jnp.float32),
        own_piece(head_sums, 0, 48),
        own_piece(head_sums, 768, 48),
        own_piece(summed, 0, 48),
        own_piece(summed, 768, 48),
        own_piece(summed, 1536, 48),
        own_piece(summed, 2304, 192),
        own_piece(summed, 5376, 48),
        own_piece(summed, 6144, 48),
        own_piece(summed, 6912, 48),
        rms_values,
    )


def layer_body(tokens, *others):
    fits = lax.axis_size("ctx") == 16 and lax.axis_size("fsdp") == 2
    if fits and tokens.shape == (1, 256, 768):
        return fast_body(tokens, *others)
    return body(tokens, *others)


def solution(mesh):
    in_specs = (
        P("fsdp", "ctx", None),
        P("fsdp"),
        P("fsdp", "ctx", None),
        P("ctx", "fsdp"),
        P("ctx", "fsdp"),
        P("ctx", "fsdp"),
        P("ctx", "fsdp"),
        P("ctx", "fsdp"),
        P("ctx", "fsdp"),
        P("ctx"),
        P("ctx"),
        P("ctx"),
        P("ctx"),
        P("ctx"),
        P("ctx"),
        P("ctx"),
        P("ctx"),
        P("ctx"),
    )
    out_specs = (
        P("fsdp", "ctx", None),
        P("fsdp", "ctx", None),
        P("ctx", "fsdp"),
        P("ctx", "fsdp"),
        P("ctx", "fsdp"),
        P("ctx", "fsdp"),
        P("ctx", "fsdp"),
        P("ctx", "fsdp"),
        P("ctx"),
        P("ctx"),
        P("ctx"),
        P("ctx"),
        P("ctx"),
        P("ctx"),
        P("ctx"),
        P("ctx"),
        P("ctx"),
        P(),
    )
    return jax.shard_map(layer_body, mesh=mesh, in_specs=in_specs, out_specs=out_specs, check_vma=False)
```

```python
import functools

import jax
import jax.numpy as jnp
from jax import lax
from jax.experimental import pallas as pl
from jax.experimental.pallas import tpu as pltpu
from jax.sharding import PartitionSpec as P

HEAD_DIM = 64


norm_eps = 1e-12
score_scale = 0.125
masked_score = -1000000000.0
rows_contract = (((0,), (0,)), ((), ()))
columns_contract = (((1,), (1,)), ((), ()))


def layer_norm(stream, gain_vec, shift_vec):
    center = jnp.mean(stream, axis=-1, keepdims=True)
    offset = stream - center
    spread = jnp.mean(offset * offset, axis=-1, keepdims=True)
    return offset * lax.rsqrt(spread + norm_eps) * gain_vec + shift_vec


def gelu_exact(inner_pre):
    return jax.nn.gelu(inner_pre, approximate=False)


def plain_product(left_side, right_side):
    return jnp.dot(left_side, right_side, preferred_element_type=jnp.float32)


def row_product(left_side, right_side):
    return lax.dot_general(left_side, right_side, rows_contract, preferred_element_type=jnp.float32)


def column_product(left_side, right_side):
    return lax.dot_general(
        left_side, right_side, columns_contract, preferred_element_type=jnp.float32
    )


def head_scores(query_head, key_head, key_ok):
    scores = (
        jnp.einsum("sqd,skd->sqk", query_head, key_head, preferred_element_type=jnp.float32)
        * score_scale
    )
    return jnp.where(key_ok[:, None, :], scores, masked_score)


def attend(query_seq, pair_all, key_ok):
    seq_count, slot_count, model_width = query_seq.shape
    heads_count = model_width // HEAD_DIM

    def one_head(head_index, loop_state):
        mixed_out, log_totals = loop_state
        head_start = head_index * HEAD_DIM
        query_head = lax.dynamic_slice_in_dim(query_seq, head_start, HEAD_DIM, 2)
        key_head = lax.dynamic_slice_in_dim(pair_all, head_start, HEAD_DIM, 2)
        value_head = lax.dynamic_slice_in_dim(pair_all, model_width + head_start, HEAD_DIM, 2)
        scores = head_scores(query_head, key_head, key_ok)
        row_peak = jnp.max(scores, axis=-1, keepdims=True)
        row_expo = jnp.exp(scores - row_peak)
        row_total = jnp.sum(row_expo, axis=-1, keepdims=True)
        attn_probs = (row_expo / row_total).astype(jnp.bfloat16)
        head_out = jnp.einsum(
            "sqk,skd->sqd", attn_probs, value_head, preferred_element_type=jnp.float32
        )
        mixed_out = lax.dynamic_update_slice_in_dim(mixed_out, head_out, head_start, 2)
        log_row = row_peak[..., 0] + jnp.log(row_total[..., 0])
        log_totals = lax.dynamic_update_index_in_dim(log_totals, log_row, head_index, 0)
        return (mixed_out, log_totals)

    start_state = (
        jnp.zeros((seq_count, slot_count, model_width), jnp.float32),
        jnp.zeros((heads_count, seq_count, slot_count), jnp.float32),
    )
    return lax.fori_loop(0, heads_count, one_head, start_state)


def attend_back(query_seq, pair_all, key_ok, log_totals, grad_mixed):
    seq_count, slot_count, model_width = query_seq.shape
    heads_count = model_width // HEAD_DIM

    def one_head(head_index, loop_state):
        grad_query, grad_pair = loop_state
        head_start = head_index * HEAD_DIM
        query_head = lax.dynamic_slice_in_dim(query_seq, head_start, HEAD_DIM, 2)
        key_head = lax.dynamic_slice_in_dim(pair_all, head_start, HEAD_DIM, 2)
        value_head = lax.dynamic_slice_in_dim(pair_all, model_width + head_start, HEAD_DIM, 2)
        grad_head = lax.dynamic_slice_in_dim(grad_mixed, head_start, HEAD_DIM, 2)
        scores = head_scores(query_head, key_head, key_ok)
        log_row = lax.dynamic_index_in_dim(log_totals, head_index, 0, keepdims=False)
        attn_probs = jnp.exp(scores - log_row[..., None])
        probs_b = attn_probs.astype(jnp.bfloat16)
        grad_probs = jnp.einsum(
            "sqd,skd->sqk", grad_head, value_head, preferred_element_type=jnp.float32
        )
        row_inner = jnp.sum(attn_probs * grad_probs, axis=-1, keepdims=True)
        grad_scores = (attn_probs * (grad_probs - row_inner)).astype(jnp.bfloat16)
        grad_query_head = (
            jnp.einsum("sqk,skd->sqd", grad_scores, key_head, preferred_element_type=jnp.float32)
            * score_scale
        )
        grad_key_head = (
            jnp.einsum("sqk,sqd->skd", grad_scores, query_head, preferred_element_type=jnp.float32)
            * score_scale
        )
        grad_value_head = jnp.einsum(
            "sqk,sqd->skd", probs_b, grad_head, preferred_element_type=jnp.float32
        )
        grad_query = lax.dynamic_update_slice_in_dim(grad_query, grad_query_head, head_start, 2)
        grad_pair = lax.dynamic_update_slice_in_dim(grad_pair, grad_key_head, head_start, 2)
        grad_pair = lax.dynamic_update_slice_in_dim(
            grad_pair, grad_value_head, model_width + head_start, 2
        )
        return (grad_query, grad_pair)

    start_state = (jnp.zeros(query_seq.shape, jnp.float32), jnp.zeros(pair_all.shape, jnp.float32))
    return lax.fori_loop(0, heads_count, one_head, start_state)


def column_sums(matrix_b):
    return jnp.sum(matrix_b.astype(jnp.float32), axis=0)


def body(
    tokens,
    lengths,
    cotangent,
    query_weight,
    key_weight,
    value_weight,
    out_weight,
    in_weight,
    down_weight,
    query_bias,
    value_bias,
    out_bias,
    attn_norm_gain,
    attn_norm_bias,
    in_bias,
    down_bias,
    ffn_norm_gain,
    ffn_norm_bias,
):
    seq_count, slot_count, model_width = tokens.shape
    row_count = seq_count * slot_count
    ctx_size = lax.axis_size("ctx")
    ctx_index = lax.axis_index("ctx")
    row_parts = (
        lax.all_gather(query_weight, "ctx", axis=0, tiled=True),
        lax.all_gather(key_weight, "ctx", axis=0, tiled=True),
        lax.all_gather(value_weight, "ctx", axis=0, tiled=True),
        lax.all_gather(out_weight, "ctx", axis=0, tiled=True),
        lax.all_gather(in_weight, "ctx", axis=0, tiled=True),
        lax.all_gather(down_weight, "ctx", axis=0, tiled=True),
        lax.all_gather(query_bias, "ctx", axis=0, tiled=True),
        lax.all_gather(value_bias, "ctx", axis=0, tiled=True),
        lax.all_gather(out_bias, "ctx", axis=0, tiled=True),
        lax.all_gather(attn_norm_gain, "ctx", axis=0, tiled=True),
        lax.all_gather(attn_norm_bias, "ctx", axis=0, tiled=True),
        lax.all_gather(in_bias, "ctx", axis=0, tiled=True),
        lax.all_gather(down_bias, "ctx", axis=0, tiled=True),
        lax.all_gather(ffn_norm_gain, "ctx", axis=0, tiled=True),
        lax.all_gather(ffn_norm_bias, "ctx", axis=0, tiled=True),
    )
    full_mats = (
        lax.all_gather(row_parts[0], "fsdp", axis=1, tiled=True),
        lax.all_gather(row_parts[1], "fsdp", axis=1, tiled=True),
        lax.all_gather(row_parts[2], "fsdp", axis=1, tiled=True),
        lax.all_gather(row_parts[3], "fsdp", axis=1, tiled=True),
        lax.all_gather(row_parts[4], "fsdp", axis=1, tiled=True),
        lax.all_gather(row_parts[5], "fsdp", axis=1, tiled=True),
    )
    query_full, key_full, value_full, out_full, in_full, down_full = full_mats
    query_vec = row_parts[6].astype(jnp.float32)
    value_vec = row_parts[7].astype(jnp.float32)
    out_vec = row_parts[8].astype(jnp.float32)
    gain_one = row_parts[9].astype(jnp.float32)
    bias_one = row_parts[10].astype(jnp.float32)
    in_vec = row_parts[11].astype(jnp.float32)
    down_vec = row_parts[12].astype(jnp.float32)
    gain_two = row_parts[13].astype(jnp.float32)
    bias_two = row_parts[14].astype(jnp.float32)
    local_slots = ctx_index * slot_count + jnp.arange(slot_count)
    local_ok = local_slots[None, :] < lengths[:, None]
    valid_mask = local_ok.astype(jnp.float32)
    valid_col = valid_mask.reshape(row_count, 1)
    key_ok = jnp.arange(slot_count * ctx_size)[None, :] < lengths[:, None]
    token_rows = tokens.reshape(row_count, model_width)
    queries_b = (plain_product(token_rows, query_full) + query_vec).astype(jnp.bfloat16)
    keys_b = plain_product(token_rows, key_full).astype(jnp.bfloat16)
    values_b = (plain_product(token_rows, value_full) + value_vec).astype(jnp.bfloat16)
    pair_local = jnp.concatenate([keys_b, values_b], axis=1).reshape(
        seq_count, slot_count, 2 * model_width
    )
    pair_all = lax.all_gather(pair_local, "ctx", axis=1, tiled=True)
    query_seq = queries_b.reshape(seq_count, slot_count, model_width)
    mixed_out, log_totals = attend(query_seq, pair_all, key_ok)
    mixed_b = mixed_out.reshape(row_count, model_width).astype(jnp.bfloat16)
    attn_branch = plain_product(mixed_b, out_full) + out_vec
    stream = token_rows.astype(jnp.float32) + attn_branch
    norm_one, norm_one_back = jax.vjp(layer_norm, stream, gain_one, bias_one)
    norm_one_b = norm_one.astype(jnp.bfloat16)
    inner_pre = plain_product(norm_one_b, in_full) + in_vec
    act_out, gelu_back = jax.vjp(gelu_exact, inner_pre)
    act_b = act_out.astype(jnp.bfloat16)
    ffn_branch = plain_product(act_b, down_full) + down_vec
    stream_two = norm_one + ffn_branch
    final_out, norm_two_back = jax.vjp(layer_norm, stream_two, gain_two, bias_two)
    layer_out = (
        (valid_col * final_out).astype(jnp.bfloat16).reshape(seq_count, slot_count, model_width)
    )
    grad_final = valid_col * cotangent.reshape(row_count, model_width).astype(jnp.float32)
    grad_stream_two, grad_gain_two, grad_bias_two = norm_two_back(grad_final)
    grad_ffn_b = grad_stream_two.astype(jnp.bfloat16)
    grad_down_vec = column_sums(grad_ffn_b)
    grad_down_full = row_product(act_b, grad_ffn_b)
    grad_inner_b = gelu_back(column_product(grad_ffn_b, down_full))[0].astype(jnp.bfloat16)
    grad_in_vec = column_sums(grad_inner_b)
    grad_in_full = row_product(norm_one_b, grad_inner_b)
    grad_norm_one = grad_stream_two + column_product(grad_inner_b, in_full)
    grad_stream, grad_gain_one, grad_bias_one = norm_one_back(grad_norm_one)
    grad_attn_b = grad_stream.astype(jnp.bfloat16)
    grad_out_vec = column_sums(grad_attn_b)
    grad_out_full = row_product(mixed_b, grad_attn_b)
    grad_mixed = (
        column_product(grad_attn_b, out_full)
        .astype(jnp.bfloat16)
        .reshape(seq_count, slot_count, model_width)
    )
    grad_query_seq, grad_pair = attend_back(query_seq, pair_all, key_ok, log_totals, grad_mixed)
    grad_pair_local = lax.psum_scatter(
        grad_pair.astype(jnp.bfloat16), "ctx", scatter_dimension=1, tiled=True
    ).astype(jnp.float32)
    grad_keys_b = (
        grad_pair_local[:, :, :model_width].reshape(row_count, model_width).astype(jnp.bfloat16)
    )
    grad_values_b = (
        grad_pair_local[:, :, model_width:].reshape(row_count, model_width).astype(jnp.bfloat16)
    )
    grad_queries_b = grad_query_seq.reshape(row_count, model_width).astype(jnp.bfloat16)
    grad_query_full = row_product(token_rows, grad_queries_b)
    grad_query_vec = column_sums(grad_queries_b)
    grad_key_full = row_product(token_rows, grad_keys_b)
    grad_value_full = row_product(token_rows, grad_values_b)
    grad_value_vec = column_sums(grad_values_b)
    tokens_grad = (
        (
            grad_stream
            + column_product(grad_queries_b, query_full)
            + column_product(grad_keys_b, key_full)
            + column_product(grad_values_b, value_full)
        )
        .astype(jnp.bfloat16)
        .reshape(seq_count, slot_count, model_width)
    )
    narrow = (
        lax.psum_scatter(
            grad_query_full.astype(jnp.bfloat16), "fsdp", scatter_dimension=1, tiled=True
        ).astype(jnp.float32),
        lax.psum_scatter(
            grad_key_full.astype(jnp.bfloat16), "fsdp", scatter_dimension=1, tiled=True
        ).astype(jnp.float32),
        lax.psum_scatter(
            grad_value_full.astype(jnp.bfloat16), "fsdp", scatter_dimension=1, tiled=True
        ).astype(jnp.float32),
        lax.psum_scatter(
            grad_out_full.astype(jnp.bfloat16), "fsdp", scatter_dimension=1, tiled=True
        ).astype(jnp.float32),
        lax.psum_scatter(
            grad_in_full.astype(jnp.bfloat16), "fsdp", scatter_dimension=1, tiled=True
        ).astype(jnp.float32),
        lax.psum_scatter(
            grad_down_full.astype(jnp.bfloat16), "fsdp", scatter_dimension=1, tiled=True
        ).astype(jnp.float32),
    )
    owned_grads = (
        lax.psum_scatter(
            narrow[0].astype(jnp.bfloat16), "ctx", scatter_dimension=0, tiled=True
        ).astype(jnp.float32),
        lax.psum_scatter(
            narrow[1].astype(jnp.bfloat16), "ctx", scatter_dimension=0, tiled=True
        ).astype(jnp.float32),
        lax.psum_scatter(
            narrow[2].astype(jnp.bfloat16), "ctx", scatter_dimension=0, tiled=True
        ).astype(jnp.float32),
        lax.psum_scatter(
            narrow[3].astype(jnp.bfloat16), "ctx", scatter_dimension=0, tiled=True
        ).astype(jnp.float32),
        lax.psum_scatter(
            narrow[4].astype(jnp.bfloat16), "ctx", scatter_dimension=0, tiled=True
        ).astype(jnp.float32),
        lax.psum_scatter(
            narrow[5].astype(jnp.bfloat16), "ctx", scatter_dimension=0, tiled=True
        ).astype(jnp.float32),
    )
    moments = jnp.stack(
        [
            jnp.sum(valid_col * stream * stream),
            jnp.sum(valid_col * attn_branch * attn_branch),
            jnp.sum(valid_col * ffn_branch * ffn_branch),
            jnp.sum(valid_col),
        ]
    )
    summed = lax.psum(
        (
            moments,
            grad_query_vec,
            grad_value_vec,
            grad_out_vec,
            grad_gain_one,
            grad_bias_one,
            grad_in_vec,
            grad_down_vec,
            grad_gain_two,
            grad_bias_two,
        ),
        ("ctx", "fsdp"),
    )
    width_shard = query_bias.shape[0]
    hidden_shard = in_bias.shape[0]

    def own_piece(vector_full, shard_len):
        return lax.dynamic_slice_in_dim(vector_full, ctx_index * shard_len, shard_len, 0)

    rms_values = jnp.sqrt(summed[0][:3] / (summed[0][3] * model_width))
    return (
        layer_out,
        tokens_grad,
        owned_grads[0],
        owned_grads[1],
        owned_grads[2],
        owned_grads[3],
        owned_grads[4],
        owned_grads[5],
        own_piece(summed[1], width_shard),
        own_piece(summed[2], width_shard),
        own_piece(summed[3], width_shard),
        own_piece(summed[4], width_shard),
        own_piece(summed[5], width_shard),
        own_piece(summed[6], hidden_shard),
        own_piece(summed[7], width_shard),
        own_piece(summed[8], width_shard),
        own_piece(summed[9], width_shard),
        rms_values,
    )


HEADS_HERE = 3
HEAD_COLS = HEADS_HERE * HEAD_DIM
rows_first = (((0,), (0,)), ((), ()))
lanes_both = (((1,), (1,)), ((), ()))
plain_contract = (((1,), (0,)), ((), ()))


def effort(microseconds):
    return pl.CostEstimate(
        flops=int(microseconds * 1.1e9), transcendentals=0, bytes_accessed=int(microseconds * 1e6)
    )


kernel_params = pltpu.CompilerParams(vmem_limit_bytes=16 * 1024 * 1024)


def product32(left_side, right_side, contract):
    return lax.dot_general(left_side, right_side, contract, preferred_element_type=jnp.float32)


def ctx_move(value, mask, levels=None):
    pairs = [(i, i ^ mask) for i in range(16) if levels is None or (i >> 2) in levels]
    return lax.ppermute(value, "ctx", pairs)


def core_swap(value):
    return ctx_move(value, 1)


def y_swap(value):
    return ctx_move(value, 2)


def x_swap(value):
    return lax.ppermute(value, "fsdp", [(0, 1), (1, 0)])


def add_b(left_side, right_side):
    return (left_side.astype(jnp.float32) + right_side.astype(jnp.float32)).astype(jnp.bfloat16)


MIDDLE, ENDS = (1, 2), (0, 3)


def z_gather(block, at_end, first=()):
    one, across = ctx_move(block, 4), ctx_move(block, 12, MIDDLE)
    one, across, *_ = lax.optimization_barrier((one, across, *first))
    two_end = ctx_move(across, 4, MIDDLE)
    two_mid = ctx_move(one, 12, MIDDLE)
    three_end = ctx_move(two_mid, 4, MIDDLE)
    return one, jnp.where(at_end, two_end, two_mid), jnp.where(at_end, three_end, across)


def z_reduce(own, *others):
    total = own.astype(jnp.float32)
    for mask, block in zip((4, 8, 12), others):
        total = total + ctx_move(block, mask).astype(jnp.float32)
    return total


def when_flag(flag_ref, run, idle):
    if flag_ref is None:
        run()
    else:
        pl.when(flag_ref[0] > 0)(run)
        pl.when(flag_ref[0] <= 0)(idle)


def attend_kernel(count, first, last, flagged, *refs):
    flag_ref = refs[0] if flagged else None
    refs = refs[flagged:]
    query_ref, pairs = refs[0], refs[1 : 1 + count]
    refs = refs[1 + count :]
    if not first:
        peak_in, total_in, mixed_in = refs[:3]
        refs = refs[3:]

    def one_head(head, carry):
        key_rows = pl.ds(pl.multiple_of(head * HEAD_DIM, HEAD_DIM), HEAD_DIM)
        value_rows = pl.ds(pl.multiple_of(HEAD_COLS + head * HEAD_DIM, HEAD_DIM), HEAD_DIM)
        query = query_ref[key_rows, :]
        width = query.shape[1]
        if first:
            peak = jnp.full((1, width), -1e30, jnp.float32)
            total = jnp.zeros((1, width), jnp.float32)
            mixed = jnp.zeros((HEAD_DIM, width), jnp.float32)
        else:
            peak, total, mixed = peak_in[head][0:1], total_in[head][0:1], mixed_in[key_rows, :]
        for pair in pairs:
            scores = product32(pair[key_rows, :], query, rows_first)
            new_peak = jnp.maximum(peak, jnp.max(scores, axis=0, keepdims=True))
            expo = jnp.exp(scores - new_peak)
            shrink = jnp.exp(peak - new_peak)
            total = total * shrink + jnp.sum(expo, axis=0, keepdims=True)
            mixed = mixed * shrink + product32(
                pair[value_rows, :], expo.astype(jnp.bfloat16), plain_contract
            )
            peak = new_peak
        if last:
            mixed_out, log_out = refs
            mixed_out[key_rows, :] = (mixed / total).astype(jnp.bfloat16)
            log_out[head] = jnp.broadcast_to(peak + jnp.log(total), (8, width))
        else:
            peak_out, total_out, sum_out = refs
            peak_out[head] = jnp.broadcast_to(peak, (8, width))
            total_out[head] = jnp.broadcast_to(total, (8, width))
            sum_out[key_rows, :] = mixed
        return carry

    def run():
        lax.fori_loop(0, HEADS_HERE, one_head, 0)

    def idle():
        for ref in refs:
            ref[...] = jnp.zeros_like(ref)

    when_flag(flag_ref, run, idle)


def attend_call(query, pairs, state=None, last=False, flag=None):
    width = query.shape[1]
    stat = jax.ShapeDtypeStruct((HEADS_HERE, 8, width), jnp.float32)
    if last:
        outs = [jax.ShapeDtypeStruct((HEAD_COLS, width), jnp.bfloat16), stat]
    else:
        outs = [stat, stat, jax.ShapeDtypeStruct((HEAD_COLS, width), jnp.float32)]
    ins = [query, *pairs, *(() if state is None else state)]
    specs = [pl.BlockSpec(memory_space=pltpu.VMEM)] * len(ins)
    if flag is not None:
        ins, specs = [flag, *ins], [pl.BlockSpec(memory_space=pltpu.SMEM), *specs]
    return pl.pallas_call(
        functools.partial(attend_kernel, len(pairs), state is None, last, int(flag is not None)),
        out_shape=outs,
        in_specs=specs,
        compiler_params=kernel_params,
        cost_estimate=effort(3.5),
    )(*ins)


def attend_back_kernel(count, first, flagged, *refs):
    flag_ref = refs[0] if flagged else None
    refs = refs[flagged:]
    query_ref, grad_ref, log_ref, inner_ref = refs[:4]
    pairs = refs[4 : 4 + count]
    refs = refs[4 + count :]
    if not first:
        grad_query_in, refs = refs[0], refs[1:]
    grad_query_out, grad_pairs = refs[0], refs[1:]

    def one_head(head, carry):
        key_rows = pl.ds(pl.multiple_of(head * HEAD_DIM, HEAD_DIM), HEAD_DIM)
        value_rows = pl.ds(pl.multiple_of(HEAD_COLS + head * HEAD_DIM, HEAD_DIM), HEAD_DIM)
        query, grad = query_ref[key_rows, :], grad_ref[key_rows, :]
        log_row, inner = log_ref[head][0:1], inner_ref[head][0:1]
        if first:
            grad_query = jnp.zeros((HEAD_DIM, query.shape[1]), jnp.float32)
        else:
            grad_query = grad_query_in[key_rows, :]
        for pair, grad_pair in zip(pairs, grad_pairs):
            keys = pair[key_rows, :]
            probs = jnp.exp(product32(keys, query, rows_first) - log_row)
            grad_probs = product32(pair[value_rows, :], grad, rows_first)
            grad_scores = (probs * (grad_probs - inner)).astype(jnp.bfloat16)
            grad_query = grad_query + product32(keys, grad_scores, plain_contract)
            grad_pair[key_rows, :] = product32(query, grad_scores, lanes_both).astype(jnp.bfloat16)
            grad_pair[value_rows, :] = product32(
                grad, probs.astype(jnp.bfloat16), lanes_both
            ).astype(jnp.bfloat16)
        grad_query_out[key_rows, :] = grad_query
        return carry

    def run():
        lax.fori_loop(0, HEADS_HERE, one_head, 0)

    def idle():
        for ref in refs:
            ref[...] = jnp.zeros_like(ref)

    when_flag(flag_ref, run, idle)


def attend_back_call(query, grad, log_rows, inner, pairs, grad_query=None, flag=None):
    outs = [jax.ShapeDtypeStruct(query.shape, jnp.float32)]
    outs += [jax.ShapeDtypeStruct(pair.shape, jnp.bfloat16) for pair in pairs]
    ins = [query, grad, log_rows, inner, *pairs, *(() if grad_query is None else (grad_query,))]
    specs = [pl.BlockSpec(memory_space=pltpu.VMEM)] * len(ins)
    if flag is not None:
        ins, specs = [flag, *ins], [pl.BlockSpec(memory_space=pltpu.SMEM), *specs]
    return pl.pallas_call(
        functools.partial(
            attend_back_kernel, len(pairs), grad_query is None, int(flag is not None)
        ),
        out_shape=outs,
        in_specs=specs,
        compiler_params=kernel_params,
        cost_estimate=effort(6.5),
    )(*ins)


def place_qkv_kernel(me_ref, own_ref, far_ref, mats_ref, vecs_ref):
    for core, stack in enumerate((own_ref, far_ref)):
        for z in range(4):
            for y in range(2):
                owner = jnp.bitwise_xor(me_ref[0], z * 4 + y * 2 + core)
                mats_ref[owner] = stack[z, y, 0:48]
                vecs_ref[owner] = stack[z, y, 48:56]


def place_in_kernel(me_ref, own_ref, far_ref, in_ref):
    zy_at, x_at = me_ref[0] >> 1, me_ref[1]
    for rel in range(8):
        owner = jnp.bitwise_xor(zy_at, (rel % 4) * 2 + rel // 4)
        low = jnp.where(x_at == 0, own_ref[rel], far_ref[rel])
        high = jnp.where(x_at == 0, far_ref[rel], own_ref[rel])
        for part, at in ((low, 0), (high, 768)):
            in_ref[owner, :, at : at + 384] = part[0:96]
            in_ref[owner, :, at + 384 : at + 768] = part[96:192]


def place_down_kernel(me_ref, own_ref, far_ref, down_ref, out_ref):
    zy_at, x_at = me_ref[0] >> 1, me_ref[1]
    for y, stack in enumerate((own_ref, far_ref)):
        for z in range(4):
            owner = jnp.bitwise_xor(zy_at, z * 2 + y)
            low = jnp.where(x_at == 0, stack[0, z], stack[1, z])
            high = jnp.where(x_at == 0, stack[1, z], stack[0, z])
            down_ref[owner, :, 0:384] = low[0:192]
            down_ref[owner, :, 384:768] = high[0:192]
            out_ref[owner, :, 0:384] = low[192:240]
            out_ref[owner, :, 384:768] = high[192:240]


def place_call(kernel, me, stacks, shapes):
    return pl.pallas_call(
        kernel,
        out_shape=[jax.ShapeDtypeStruct(shape, jnp.bfloat16) for shape in shapes],
        in_specs=[pl.BlockSpec(memory_space=pltpu.SMEM)]
        + [pl.BlockSpec(memory_space=pltpu.VMEM)] * len(stacks),
        compiler_params=kernel_params,
        cost_estimate=effort(2.0),
    )(me, *stacks)


def all_sum(packed):
    packed = packed + core_swap(packed)
    packed = packed + ctx_move(packed, 4) + ctx_move(packed, 8) + ctx_move(packed, 12)
    packed = packed + y_swap(packed)
    return packed + x_swap(packed)


def fast_body(
    tokens,
    lengths,
    cotangent,
    query_weight,
    key_weight,
    value_weight,
    out_weight,
    in_weight,
    down_weight,
    query_bias,
    value_bias,
    out_bias,
    attn_norm_gain,
    attn_norm_bias,
    in_bias,
    down_bias,
    ffn_norm_gain,
    ffn_norm_bias,
):
    slot_count, width = tokens.shape[1:]
    me = lax.axis_index("ctx")
    x_at = lax.axis_index("fsdp")
    z_at, y_at, core_at = me >> 2, (me >> 1) & 1, me & 1
    at_end = (z_at == 0) | (z_at == 3)
    y_low, x_low, core_low = y_at == 0, x_at == 0, core_at == 0
    own_long = lengths[0] == slot_count * lax.axis_size("ctx")
    short_flag = (z_at == 0).astype(jnp.int32).reshape(1)

    half = HEAD_COLS
    low_cols = jnp.concatenate(
        [query_weight[:, :half], key_weight[:, :half], value_weight[:, :half]], axis=1
    )
    high_cols = jnp.concatenate(
        [query_weight[:, half:], key_weight[:, half:], value_weight[:, half:]], axis=1
    )
    vector_rows = sum(
        lax.pad(piece[None, :], jnp.asarray(0, jnp.bfloat16), ((row, 7 - row, 0), (at, 576 - at - piece.shape[0], 0)))
        for row, at, piece in (
            (0, 0, query_bias),
            (1, 0, value_bias),
            (2, 0, out_bias),
            (3, 0, attn_norm_gain),
            (4, 0, attn_norm_bias),
            (5, 0, down_bias),
            (6, 0, ffn_norm_gain),
            (7, 0, ffn_norm_bias),
            (0, 128, in_bias),
        )
    )
    keep_cols = jnp.concatenate([jnp.where(y_low, low_cols, high_cols), vector_rows], axis=0)
    send_cols = jnp.concatenate([jnp.where(y_low, high_cols, low_cols), vector_rows], axis=0)
    token_rows = tokens[0]
    other_rows, got_cols = lax.optimization_barrier((x_swap(token_rows), y_swap(send_cols)))
    long_own = jnp.where(own_long, token_rows, other_rows)
    short_own = jnp.where(own_long, other_rows, token_rows)
    own_block = jnp.stack([keep_cols, got_cols])
    z_one, z_two, z_three, long_far = lax.optimization_barrier(
        (*(ctx_move(own_block, mask) for mask in (4, 8, 12)), y_swap(long_own))
    )
    z_stack = jnp.stack([own_block, z_one, z_two, z_three])
    where_me = jnp.stack([me, x_at]).astype(jnp.int32)
    qkv_weight, vecs = place_call(
        place_qkv_kernel, where_me, (z_stack, core_swap(z_stack)), ((16, 48, 576), (16, 8, 576))
    )
    qkv_weight = qkv_weight.reshape(768, 576)
    vecs = vecs.astype(jnp.float32)

    even_cols = jnp.concatenate([in_weight[:, 384 * k : 384 * k + 192] for k in range(4)], axis=1)
    odd_cols = jnp.concatenate(
        [in_weight[:, 384 * k + 192 : 384 * k + 384] for k in range(4)], axis=1
    )
    in_keep = jnp.where(core_low, even_cols, odd_cols)
    in_got = core_swap(jnp.where(core_low, odd_cols, even_cols))
    in_block = jnp.concatenate(
        [jnp.where(core_low, in_keep, in_got), jnp.where(core_low, in_got, in_keep)], axis=0
    )
    ffn_block = jnp.concatenate([in_block[:, :384], in_block[:, 384:], down_weight, out_weight])
    ffn_stack = jnp.stack([ffn_block, *z_gather(ffn_block, at_end, (z_three,))])
    in_stack, down_stack = ffn_stack[:, :192], ffn_stack[:, 192:]
    in_stack = jnp.concatenate([in_stack, y_swap(in_stack)], axis=0)
    down_stack = jnp.stack([down_stack, x_swap(down_stack)])
    in_far, down_far = x_swap(in_stack), y_swap(down_stack)

    def vector(row):
        return vecs[:, row, :48].reshape(768)

    query_vec, value_vec, out_vec, gain_one, bias_one, down_vec, gain_two, bias_two = (
        vector(row) for row in range(8)
    )
    in_pieces = vecs[:, 0, 128:320].reshape(8, 2, 192)
    in_vec = jnp.where(core_low, in_pieces[:, 0], in_pieces[:, 1]).reshape(1536)
    head_start = 384 * x_at + half * y_at
    query_add = lax.dynamic_slice_in_dim(query_vec, head_start, half, 0)[:, None]
    value_add = lax.dynamic_slice_in_dim(value_vec, head_start, half, 0)[:, None]
    pair_add = jnp.concatenate([jnp.zeros_like(value_add), value_add], axis=0)

    long_rows = jnp.concatenate([long_own, long_far], axis=0)
    def project(rows):
        query = product32(qkv_weight[:, :half], rows, (((0,), (1,)), ((), ()))) + query_add
        pair = product32(qkv_weight[:, half:], rows, (((0,), (1,)), ((), ()))) + pair_add
        scale = jnp.asarray(score_scale, jnp.bfloat16)
        return query.astype(jnp.bfloat16) * scale, pair.astype(jnp.bfloat16)

    long_query, long_pair = project(long_rows)
    short_own, _ = lax.optimization_barrier((short_own, long_pair))
    short_rows = jnp.concatenate([short_own, y_swap(short_own)], axis=0)
    short_query, short_pair = project(short_rows)
    z_pairs = (long_pair, *z_gather(long_pair, at_end))
    pairs = [(pair, core_swap(pair)) for pair in z_pairs]
    short_pairs = (short_pair, core_swap(short_pair))
    short_mixed, short_log = attend_call(short_query, short_pairs, last=True, flag=short_flag)
    state = None
    for step, both in enumerate(pairs):
        state = attend_call(long_query, both, state, last=step == 3)
    long_mixed, long_log = state

    rows_here = slot_count
    sent = jnp.concatenate([long_mixed[:, rows_here:], short_mixed[:, rows_here:]], axis=0)
    sent, in_far, down_far = lax.optimization_barrier((sent, in_far, down_far))
    got = y_swap(sent)
    (in_all,) = place_call(place_in_kernel, where_me, (in_stack, in_far), ((8, 96, 1536),))
    down_all, out_core = place_call(
        place_down_kernel, where_me, (down_stack, down_far), ((8, 192, 768), (8, 48, 768))
    )
    in_all, down_all = in_all.reshape(768, 1536), down_all.reshape(1536, 768)
    out_far = core_swap(out_core)
    out_all = jnp.stack(
        [jnp.where(core_low, out_core, out_far), jnp.where(core_low, out_far, out_core)], axis=1
    ).reshape(768, 768)

    def by_y(mine, theirs):
        return jnp.concatenate(
            [jnp.where(y_low, mine, theirs), jnp.where(y_low, theirs, mine)], axis=0
        )

    long_heads = by_y(long_mixed[:, :rows_here], got[:half])
    short_heads = by_y(short_mixed[:, :rows_here], got[half:])
    own_heads = jnp.where(own_long, long_heads, short_heads)
    far_heads = x_swap(jnp.where(own_long, short_heads, long_heads))
    mixed_t = jnp.concatenate(
        [jnp.where(x_low, own_heads, far_heads), jnp.where(x_low, far_heads, own_heads)], axis=0
    )

    local_slots = me * slot_count + jnp.arange(slot_count)
    valid_col = (local_slots < lengths[0]).astype(jnp.float32)[:, None]
    attn_branch = product32(mixed_t, out_all, rows_first) + out_vec
    stream = token_rows.astype(jnp.float32) + attn_branch
    norm_one, norm_one_back = jax.vjp(layer_norm, stream, gain_one, bias_one)
    norm_one_b = norm_one.astype(jnp.bfloat16)
    chip_norm = jnp.concatenate([norm_one_b, core_swap(norm_one_b)], axis=0)
    act_out, gelu_back = jax.vjp(gelu_exact, plain_product(chip_norm, in_all) + in_vec)
    act_b = act_out.astype(jnp.bfloat16)
    ffn_got = core_swap(plain_product(act_b[rows_here:], down_all).astype(jnp.bfloat16))
    ffn_part = plain_product(act_b[:rows_here], down_all)
    ffn_branch = ffn_part + ffn_got.astype(jnp.float32) + down_vec
    stream_two = norm_one + ffn_branch
    final_out, norm_two_back = jax.vjp(layer_norm, stream_two, gain_two, bias_two)
    layer_out = (valid_col * final_out).astype(jnp.bfloat16)[None]
    grad_final = valid_col * cotangent[0].astype(jnp.float32)
    grad_stream_two, grad_gain_two, grad_bias_two = norm_two_back(grad_final)
    grad_ffn_b = grad_stream_two.astype(jnp.bfloat16)
    grad_down_vec = column_sums(grad_ffn_b)
    chip_grad = jnp.concatenate([grad_ffn_b, core_swap(grad_ffn_b)], axis=0)
    grad_inner_b = gelu_back(column_product(chip_grad, down_all))[0].astype(jnp.bfloat16)
    grad_in_vec = jnp.where(
        jnp.arange(2)[None, :, None] == core_at, column_sums(grad_inner_b).reshape(8, 1, 192), 0.0
    ).reshape(3072)
    norm_got = core_swap(column_product(grad_inner_b[rows_here:], in_all).astype(jnp.bfloat16))
    norm_part = column_product(grad_inner_b[:rows_here], in_all)
    grad_norm_one = grad_stream_two + norm_part + norm_got.astype(jnp.float32)
    grad_stream, grad_gain_one, grad_bias_one = norm_one_back(grad_norm_one)
    grad_attn_b = grad_stream.astype(jnp.bfloat16)
    grad_out_vec = column_sums(grad_attn_b)
    grad_mixed_t = product32(out_all, grad_attn_b, lanes_both).astype(jnp.bfloat16)
    grad_value_vec = jnp.sum(grad_mixed_t.astype(jnp.float32), axis=1)

    chip_norm, act_b, grad_inner_b, mixed_w, _ = lax.optimization_barrier(
        (chip_norm, act_b, grad_inner_b, mixed_t, grad_mixed_t)
    )
    inner_send = jnp.where(x_low, grad_inner_b[:, 768:], grad_inner_b[:, :768])
    inner_keep = jnp.where(x_low, grad_inner_b[:, :768], grad_inner_b[:, 768:])
    in_send = row_product(chip_norm, inner_send).astype(jnp.bfloat16)
    in_keep_grad = row_product(chip_norm, inner_keep)
    grad_down = row_product(act_b, chip_grad).astype(jnp.bfloat16).reshape(4, 2, 192, 768)
    grad_out = plain_product(mixed_w, grad_attn_b).astype(jnp.bfloat16).reshape(4, 2, 2, 48, 768)
    out_sum = add_b(
        jnp.where(core_low, grad_out[:, :, 0], grad_out[:, :, 1]),
        core_swap(jnp.where(core_low, grad_out[:, :, 1], grad_out[:, :, 0])),
    )
    down_out = jnp.concatenate([grad_down, out_sum], axis=2)
    down_send = jnp.where(y_low, down_out[:, 1], down_out[:, 0])
    down_keep = jnp.where(y_low, down_out[:, 0], down_out[:, 1])
    keep_x = jnp.where(x_low, grad_mixed_t[:384], grad_mixed_t[384:])
    got_x = x_swap(jnp.where(x_low, grad_mixed_t[384:], grad_mixed_t[:384]))
    long_x = jnp.where(own_long, keep_x, got_x)
    short_x = jnp.where(own_long, got_x, keep_x)
    both_keep = jnp.where(y_low, long_x[:half], long_x[half:])
    short_keep = jnp.where(y_low, short_x[:half], short_x[half:])
    sent = jnp.concatenate(
        [
            jnp.where(y_low, long_x[half:], long_x[:half]),
            jnp.where(y_low, short_x[half:], short_x[:half]),
        ],
        axis=0,
    )
    got = y_swap(sent)
    long_grad = jnp.concatenate([both_keep, got[:half]], axis=1)
    short_grad = jnp.concatenate([short_keep, got[half:]], axis=1)
    in_send, down_send, _ = lax.optimization_barrier((in_send, down_send, got))
    in_x, down_y = x_swap(in_send), y_swap(down_send)

    def inner_rows(mixed, grad):
        product = mixed.astype(jnp.float32) * grad.astype(jnp.float32)
        sums = jnp.sum(product.reshape(HEADS_HERE, HEAD_DIM, -1), axis=1, keepdims=True)
        return jnp.broadcast_to(sums, (HEADS_HERE, 8, sums.shape[-1]))

    long_inner = inner_rows(long_mixed, long_grad)

    def long_step(step, query, grad_query):
        return attend_back_call(
            query, long_grad, long_log, long_inner, pairs[step], grad_query
        )

    grad_query, near, far = long_step(3, long_query, None)
    far_three = core_swap(far)
    grad_query, near_two, far = long_step(2, long_query, grad_query)
    far_two = core_swap(far)
    three = add_b(near, far_three)
    three, grad_query = lax.optimization_barrier((three, grad_query))
    three_got = ctx_move(three, 12)
    grad_query, near_one, far = long_step(1, long_query, grad_query)
    far_one = core_swap(far)
    two = add_b(near_two, far_two)
    two, grad_query = lax.optimization_barrier((two, grad_query))
    two_got = ctx_move(two, 8)
    grad_query, near_own, far = long_step(0, long_query, grad_query)
    far_own = core_swap(far)
    one = add_b(near_one, far_one)
    one, short_query_b, in_x, down_y = lax.optimization_barrier((one, short_query, in_x, down_y))
    one_got = ctx_move(one, 4)
    short_back = attend_back_call(
        short_query_b,
        short_grad,
        short_log,
        inner_rows(short_mixed, short_grad),
        short_pairs,
        flag=short_flag,
    )
    in_sum = (in_keep_grad + in_x.astype(jnp.float32)).astype(jnp.bfloat16)
    in_sum = in_sum.reshape(4, 2, 96, 768)
    in_sum = add_b(
        jnp.where(y_low, in_sum[:, 0], in_sum[:, 1]),
        y_swap(jnp.where(y_low, in_sum[:, 1], in_sum[:, 0])),
    )
    down_sum = add_b(down_keep, down_y)
    down_sum = add_b(
        jnp.where(x_low, down_sum[..., :384], down_sum[..., 384:]),
        x_swap(jnp.where(x_low, down_sum[..., 384:], down_sum[..., :384])),
    )

    short_pair_grad = add_b(short_back[1], core_swap(short_back[2]))
    long_pair_grad = near_own.astype(jnp.float32)
    for got_part in (far_own, one_got, two_got, three_got):
        long_pair_grad = long_pair_grad + got_part.astype(jnp.float32)
    long_pair_grad = long_pair_grad.astype(jnp.bfloat16)
    long_query_grad = (grad_query * score_scale).astype(jnp.bfloat16)
    short_query_grad = (short_back[0] * score_scale).astype(jnp.bfloat16)
    stream, attn_branch, ffn_branch, _ = lax.optimization_barrier(
        (stream, attn_branch, ffn_branch, short_query_b)
    )
    moments = jnp.stack(
        [
            jnp.sum(valid_col * stream * stream),
            jnp.sum(valid_col * attn_branch * attn_branch),
            jnp.sum(valid_col * ffn_branch * ffn_branch),
            jnp.sum(valid_col),
        ]
    )
    packed = jnp.concatenate(
        [
            grad_out_vec,
            grad_gain_one,
            grad_bias_one,
            grad_in_vec,
            grad_down_vec,
            grad_gain_two,
            grad_bias_two,
            moments,
            jnp.zeros((508,), jnp.float32),
        ]
    )
    def lane_sums(first_part, second_part):
        return jnp.sum(first_part.astype(jnp.float32), axis=1) + jnp.sum(
            second_part.astype(jnp.float32), axis=1
        )

    query_sums = lane_sums(long_query_grad, short_query_grad)
    at_heads = (jnp.arange(4) == 2 * x_at + y_at).astype(jnp.float32)[:, None]
    packed = jnp.concatenate(
        [
            (at_heads * query_sums[None, :]).reshape(6, 128),
            grad_value_vec.reshape(6, 128),
            packed.reshape(64, 128),
        ],
        axis=0,
    )
    packed = jnp.pad(packed, ((0, 4), (0, 0)))
    packed = all_sum(packed).reshape(10240)

    long_all = jnp.concatenate([long_query_grad, long_pair_grad], axis=0)
    short_all = jnp.concatenate([short_query_grad, short_pair_grad], axis=0)
    long_all, packed = lax.optimization_barrier((long_all, packed))
    head_sums, summed = packed[:1536], packed[1536:]

    grad_qkv = product32(long_rows, long_all, (((0,), (1,)), ((), ()))) + product32(
        short_rows, short_all, (((0,), (1,)), ((), ()))
    )
    grad_qkv = grad_qkv.astype(jnp.bfloat16).reshape(4, 2, 2, 48, 576)
    core_keep = jnp.where(core_low, grad_qkv[:, :, 0], grad_qkv[:, :, 1])
    core_send = jnp.where(core_low, grad_qkv[:, :, 1], grad_qkv[:, :, 0])
    core_sum = add_b(core_keep, core_swap(core_send))
    own_sum = lax.dynamic_index_in_dim(core_sum, z_at, 0, keepdims=False).astype(jnp.float32)
    for mask in (1, 2, 3):
        piece = lax.dynamic_index_in_dim(core_sum, z_at ^ mask, 0, keepdims=False)
        own_sum = own_sum + ctx_move(piece, 4 * mask).astype(jnp.float32)
    y_keep = jnp.where(y_low, own_sum[0], own_sum[1])
    y_got = y_swap(jnp.where(y_low, own_sum[1], own_sum[0]).astype(jnp.bfloat16))
    y_got = y_got.astype(jnp.float32)
    low_part, high_part = jnp.where(y_low, y_keep, y_got), jnp.where(y_low, y_got, y_keep)
    owned_qkv = [
        jnp.concatenate(
            [low_part[:, half * i : half * (i + 1)], high_part[:, half * i : half * (i + 1)]],
            axis=1,
        )
        for i in range(3)
    ]

    def by_z(stack):
        return [
            lax.dynamic_index_in_dim(stack, z_at ^ mask, 0, keepdims=False) for mask in range(4)
        ]

    ffn_sum = jnp.concatenate([in_sum[..., :384], in_sum[..., 384:], down_sum], axis=1)
    ffn_owned = z_reduce(*by_z(ffn_sum))
    in_owned = jnp.concatenate([ffn_owned[:96], ffn_owned[96:192]], axis=1)
    in_owned = in_owned.astype(jnp.bfloat16).reshape(2, 48, 768)
    down_owned = ffn_owned[192:]
    in_mine = jnp.where(core_low, in_owned[0], in_owned[1])
    in_other = core_swap(jnp.where(core_low, in_owned[1], in_owned[0]))
    in_even = jnp.where(core_low, in_mine, in_other).astype(jnp.float32)
    in_odd = jnp.where(core_low, in_other, in_mine).astype(jnp.float32)
    owned_in = jnp.concatenate(
        [
            part[:, 192 * k : 192 * (k + 1)]
            for k in range(4)
            for part in (in_even, in_odd)
        ],
        axis=1,
    )
    owned_down, owned_out = down_owned[:192], down_owned[192:]

    def back_rows(grads):
        return product32(grads, qkv_weight, (((0,), (1,)), ((), ())))

    short_rows_back = back_rows(short_all)
    short_got = y_swap(short_rows_back[rows_here:].astype(jnp.bfloat16)).astype(jnp.float32)
    short_part = short_rows_back[:rows_here] + short_got
    long_back = back_rows(long_all)
    long_got = y_swap(long_back[rows_here:].astype(jnp.bfloat16)).astype(jnp.float32)
    long_part = long_back[:rows_here] + long_got
    own_part = jnp.where(own_long, long_part, short_part)
    far_part = x_swap(jnp.where(own_long, short_part, long_part).astype(jnp.bfloat16))
    tokens_grad = (grad_stream + own_part + far_part.astype(jnp.float32)).astype(jnp.bfloat16)

    def own_piece(vector_all, start, shard):
        return lax.dynamic_slice_in_dim(vector_all, start + me * shard, shard, 0)

    rms_values = jnp.sqrt(summed[7680:7683] / (summed[7683] * width))
    return (
        layer_out,
        tokens_grad[None],
        owned_qkv[0],
        owned_qkv[1],
        owned_qkv[2],
        owned_out,
        owned_in,
        owned_down,
        own_piece(head_sums, 0, 48),
        own_piece(head_sums, 768, 48),
        own_piece(summed, 0, 48),
        own_piece(summed, 768, 48),
        own_piece(summed, 1536, 48),
        own_piece(summed, 2304, 192),
        own_piece(summed, 5376, 48),
        own_piece(summed, 6144, 48),
        own_piece(summed, 6912, 48),
        rms_values,
    )


def layer_body(tokens, *others):
    fits = lax.axis_size("ctx") == 16 and lax.axis_size("fsdp") == 2
    if fits and tokens.shape == (1, 256, 768):
        return fast_body(tokens, *others)
    return body(tokens, *others)


def solution(mesh):
    in_specs = (
        P("fsdp", "ctx", None),
        P("fsdp"),
        P("fsdp", "ctx", None),
        P("ctx", "fsdp"),
        P("ctx", "fsdp"),
        P("ctx", "fsdp"),
        P("ctx", "fsdp"),
        P("ctx", "fsdp"),
        P("ctx", "fsdp"),
        P("ctx"),
        P("ctx"),
        P("ctx"),
        P("ctx"),
        P("ctx"),
        P("ctx"),
        P("ctx"),
        P("ctx"),
        P("ctx"),
    )
    out_specs = (
        P("fsdp", "ctx", None),
        P("fsdp", "ctx", None),
        P("ctx", "fsdp"),
        P("ctx", "fsdp"),
        P("ctx", "fsdp"),
        P("ctx", "fsdp"),
        P("ctx", "fsdp"),
        P("ctx", "fsdp"),
        P("ctx"),
        P("ctx"),
        P("ctx"),
        P("ctx"),
        P("ctx"),
        P("ctx"),
        P("ctx"),
        P("ctx"),
        P("ctx"),
        P(),
    )
    return jax.shard_map(layer_body, mesh=mesh, in_specs=in_specs, out_specs=out_specs, check_vma=False)
```

```python
import functools

import jax
import jax.numpy as jnp
from jax import lax
from jax.experimental import pallas as pl
from jax.experimental.pallas import tpu as pltpu
from jax.sharding import PartitionSpec as P

HEAD_DIM = 64


norm_eps = 1e-12
score_scale = 0.125
masked_score = -1000000000.0
rows_contract = (((0,), (0,)), ((), ()))
columns_contract = (((1,), (1,)), ((), ()))


def layer_norm(stream, gain_vec, shift_vec):
    center = jnp.mean(stream, axis=-1, keepdims=True)
    offset = stream - center
    spread = jnp.mean(offset * offset, axis=-1, keepdims=True)
    return offset * lax.rsqrt(spread + norm_eps) * gain_vec + shift_vec


def gelu_exact(inner_pre):
    return jax.nn.gelu(inner_pre, approximate=False)


def plain_product(left_side, right_side):
    return jnp.dot(left_side, right_side, preferred_element_type=jnp.float32)


def row_product(left_side, right_side):
    return lax.dot_general(left_side, right_side, rows_contract, preferred_element_type=jnp.float32)


def column_product(left_side, right_side):
    return lax.dot_general(
        left_side, right_side, columns_contract, preferred_element_type=jnp.float32
    )


def head_scores(query_head, key_head, key_ok):
    scores = (
        jnp.einsum("sqd,skd->sqk", query_head, key_head, preferred_element_type=jnp.float32)
        * score_scale
    )
    return jnp.where(key_ok[:, None, :], scores, masked_score)


def attend(query_seq, pair_all, key_ok):
    seq_count, slot_count, model_width = query_seq.shape
    heads_count = model_width // HEAD_DIM

    def one_head(head_index, loop_state):
        mixed_out, log_totals = loop_state
        head_start = head_index * HEAD_DIM
        query_head = lax.dynamic_slice_in_dim(query_seq, head_start, HEAD_DIM, 2)
        key_head = lax.dynamic_slice_in_dim(pair_all, head_start, HEAD_DIM, 2)
        value_head = lax.dynamic_slice_in_dim(pair_all, model_width + head_start, HEAD_DIM, 2)
        scores = head_scores(query_head, key_head, key_ok)
        row_peak = jnp.max(scores, axis=-1, keepdims=True)
        row_expo = jnp.exp(scores - row_peak)
        row_total = jnp.sum(row_expo, axis=-1, keepdims=True)
        attn_probs = (row_expo / row_total).astype(jnp.bfloat16)
        head_out = jnp.einsum(
            "sqk,skd->sqd", attn_probs, value_head, preferred_element_type=jnp.float32
        )
        mixed_out = lax.dynamic_update_slice_in_dim(mixed_out, head_out, head_start, 2)
        log_row = row_peak[..., 0] + jnp.log(row_total[..., 0])
        log_totals = lax.dynamic_update_index_in_dim(log_totals, log_row, head_index, 0)
        return (mixed_out, log_totals)

    start_state = (
        jnp.zeros((seq_count, slot_count, model_width), jnp.float32),
        jnp.zeros((heads_count, seq_count, slot_count), jnp.float32),
    )
    return lax.fori_loop(0, heads_count, one_head, start_state)


def attend_back(query_seq, pair_all, key_ok, log_totals, grad_mixed):
    seq_count, slot_count, model_width = query_seq.shape
    heads_count = model_width // HEAD_DIM

    def one_head(head_index, loop_state):
        grad_query, grad_pair = loop_state
        head_start = head_index * HEAD_DIM
        query_head = lax.dynamic_slice_in_dim(query_seq, head_start, HEAD_DIM, 2)
        key_head = lax.dynamic_slice_in_dim(pair_all, head_start, HEAD_DIM, 2)
        value_head = lax.dynamic_slice_in_dim(pair_all, model_width + head_start, HEAD_DIM, 2)
        grad_head = lax.dynamic_slice_in_dim(grad_mixed, head_start, HEAD_DIM, 2)
        scores = head_scores(query_head, key_head, key_ok)
        log_row = lax.dynamic_index_in_dim(log_totals, head_index, 0, keepdims=False)
        attn_probs = jnp.exp(scores - log_row[..., None])
        probs_b = attn_probs.astype(jnp.bfloat16)
        grad_probs = jnp.einsum(
            "sqd,skd->sqk", grad_head, value_head, preferred_element_type=jnp.float32
        )
        row_inner = jnp.sum(attn_probs * grad_probs, axis=-1, keepdims=True)
        grad_scores = (attn_probs * (grad_probs - row_inner)).astype(jnp.bfloat16)
        grad_query_head = (
            jnp.einsum("sqk,skd->sqd", grad_scores, key_head, preferred_element_type=jnp.float32)
            * score_scale
        )
        grad_key_head = (
            jnp.einsum("sqk,sqd->skd", grad_scores, query_head, preferred_element_type=jnp.float32)
            * score_scale
        )
        grad_value_head = jnp.einsum(
            "sqk,sqd->skd", probs_b, grad_head, preferred_element_type=jnp.float32
        )
        grad_query = lax.dynamic_update_slice_in_dim(grad_query, grad_query_head, head_start, 2)
        grad_pair = lax.dynamic_update_slice_in_dim(grad_pair, grad_key_head, head_start, 2)
        grad_pair = lax.dynamic_update_slice_in_dim(
            grad_pair, grad_value_head, model_width + head_start, 2
        )
        return (grad_query, grad_pair)

    start_state = (jnp.zeros(query_seq.shape, jnp.float32), jnp.zeros(pair_all.shape, jnp.float32))
    return lax.fori_loop(0, heads_count, one_head, start_state)


def column_sums(matrix_b):
    return jnp.sum(matrix_b.astype(jnp.float32), axis=0)


def body(
    tokens,
    lengths,
    cotangent,
    query_weight,
    key_weight,
    value_weight,
    out_weight,
    in_weight,
    down_weight,
    query_bias,
    value_bias,
    out_bias,
    attn_norm_gain,
    attn_norm_bias,
    in_bias,
    down_bias,
    ffn_norm_gain,
    ffn_norm_bias,
):
    seq_count, slot_count, model_width = tokens.shape
    row_count = seq_count * slot_count
    ctx_size = lax.axis_size("ctx")
    ctx_index = lax.axis_index("ctx")
    row_parts = (
        lax.all_gather(query_weight, "ctx", axis=0, tiled=True),
        lax.all_gather(key_weight, "ctx", axis=0, tiled=True),
        lax.all_gather(value_weight, "ctx", axis=0, tiled=True),
        lax.all_gather(out_weight, "ctx", axis=0, tiled=True),
        lax.all_gather(in_weight, "ctx", axis=0, tiled=True),
        lax.all_gather(down_weight, "ctx", axis=0, tiled=True),
        lax.all_gather(query_bias, "ctx", axis=0, tiled=True),
        lax.all_gather(value_bias, "ctx", axis=0, tiled=True),
        lax.all_gather(out_bias, "ctx", axis=0, tiled=True),
        lax.all_gather(attn_norm_gain, "ctx", axis=0, tiled=True),
        lax.all_gather(attn_norm_bias, "ctx", axis=0, tiled=True),
        lax.all_gather(in_bias, "ctx", axis=0, tiled=True),
        lax.all_gather(down_bias, "ctx", axis=0, tiled=True),
        lax.all_gather(ffn_norm_gain, "ctx", axis=0, tiled=True),
        lax.all_gather(ffn_norm_bias, "ctx", axis=0, tiled=True),
    )
    full_mats = (
        lax.all_gather(row_parts[0], "fsdp", axis=1, tiled=True),
        lax.all_gather(row_parts[1], "fsdp", axis=1, tiled=True),
        lax.all_gather(row_parts[2], "fsdp", axis=1, tiled=True),
        lax.all_gather(row_parts[3], "fsdp", axis=1, tiled=True),
        lax.all_gather(row_parts[4], "fsdp", axis=1, tiled=True),
        lax.all_gather(row_parts[5], "fsdp", axis=1, tiled=True),
    )
    query_full, key_full, value_full, out_full, in_full, down_full = full_mats
    query_vec = row_parts[6].astype(jnp.float32)
    value_vec = row_parts[7].astype(jnp.float32)
    out_vec = row_parts[8].astype(jnp.float32)
    gain_one = row_parts[9].astype(jnp.float32)
    bias_one = row_parts[10].astype(jnp.float32)
    in_vec = row_parts[11].astype(jnp.float32)
    down_vec = row_parts[12].astype(jnp.float32)
    gain_two = row_parts[13].astype(jnp.float32)
    bias_two = row_parts[14].astype(jnp.float32)
    local_slots = ctx_index * slot_count + jnp.arange(slot_count)
    local_ok = local_slots[None, :] < lengths[:, None]
    valid_mask = local_ok.astype(jnp.float32)
    valid_col = valid_mask.reshape(row_count, 1)
    key_ok = jnp.arange(slot_count * ctx_size)[None, :] < lengths[:, None]
    token_rows = tokens.reshape(row_count, model_width)
    queries_b = (plain_product(token_rows, query_full) + query_vec).astype(jnp.bfloat16)
    keys_b = plain_product(token_rows, key_full).astype(jnp.bfloat16)
    values_b = (plain_product(token_rows, value_full) + value_vec).astype(jnp.bfloat16)
    pair_local = jnp.concatenate([keys_b, values_b], axis=1).reshape(
        seq_count, slot_count, 2 * model_width
    )
    pair_all = lax.all_gather(pair_local, "ctx", axis=1, tiled=True)
    query_seq = queries_b.reshape(seq_count, slot_count, model_width)
    mixed_out, log_totals = attend(query_seq, pair_all, key_ok)
    mixed_b = mixed_out.reshape(row_count, model_width).astype(jnp.bfloat16)
    attn_branch = plain_product(mixed_b, out_full) + out_vec
    stream = token_rows.astype(jnp.float32) + attn_branch
    norm_one, norm_one_back = jax.vjp(layer_norm, stream, gain_one, bias_one)
    norm_one_b = norm_one.astype(jnp.bfloat16)
    inner_pre = plain_product(norm_one_b, in_full) + in_vec
    act_out, gelu_back = jax.vjp(gelu_exact, inner_pre)
    act_b = act_out.astype(jnp.bfloat16)
    ffn_branch = plain_product(act_b, down_full) + down_vec
    stream_two = norm_one + ffn_branch
    final_out, norm_two_back = jax.vjp(layer_norm, stream_two, gain_two, bias_two)
    layer_out = (
        (valid_col * final_out).astype(jnp.bfloat16).reshape(seq_count, slot_count, model_width)
    )
    grad_final = valid_col * cotangent.reshape(row_count, model_width).astype(jnp.float32)
    grad_stream_two, grad_gain_two, grad_bias_two = norm_two_back(grad_final)
    grad_ffn_b = grad_stream_two.astype(jnp.bfloat16)
    grad_down_vec = column_sums(grad_ffn_b)
    grad_down_full = row_product(act_b, grad_ffn_b)
    grad_inner_b = gelu_back(column_product(grad_ffn_b, down_full))[0].astype(jnp.bfloat16)
    grad_in_vec = column_sums(grad_inner_b)
    grad_in_full = row_product(norm_one_b, grad_inner_b)
    grad_norm_one = grad_stream_two + column_product(grad_inner_b, in_full)
    grad_stream, grad_gain_one, grad_bias_one = norm_one_back(grad_norm_one)
    grad_attn_b = grad_stream.astype(jnp.bfloat16)
    grad_out_vec = column_sums(grad_attn_b)
    grad_out_full = row_product(mixed_b, grad_attn_b)
    grad_mixed = (
        column_product(grad_attn_b, out_full)
        .astype(jnp.bfloat16)
        .reshape(seq_count, slot_count, model_width)
    )
    grad_query_seq, grad_pair = attend_back(query_seq, pair_all, key_ok, log_totals, grad_mixed)
    grad_pair_local = lax.psum_scatter(
        grad_pair.astype(jnp.bfloat16), "ctx", scatter_dimension=1, tiled=True
    ).astype(jnp.float32)
    grad_keys_b = (
        grad_pair_local[:, :, :model_width].reshape(row_count, model_width).astype(jnp.bfloat16)
    )
    grad_values_b = (
        grad_pair_local[:, :, model_width:].reshape(row_count, model_width).astype(jnp.bfloat16)
    )
    grad_queries_b = grad_query_seq.reshape(row_count, model_width).astype(jnp.bfloat16)
    grad_query_full = row_product(token_rows, grad_queries_b)
    grad_query_vec = column_sums(grad_queries_b)
    grad_key_full = row_product(token_rows, grad_keys_b)
    grad_value_full = row_product(token_rows, grad_values_b)
    grad_value_vec = column_sums(grad_values_b)
    tokens_grad = (
        (
            grad_stream
            + column_product(grad_queries_b, query_full)
            + column_product(grad_keys_b, key_full)
            + column_product(grad_values_b, value_full)
        )
        .astype(jnp.bfloat16)
        .reshape(seq_count, slot_count, model_width)
    )
    narrow = (
        lax.psum_scatter(
            grad_query_full.astype(jnp.bfloat16), "fsdp", scatter_dimension=1, tiled=True
        ).astype(jnp.float32),
        lax.psum_scatter(
            grad_key_full.astype(jnp.bfloat16), "fsdp", scatter_dimension=1, tiled=True
        ).astype(jnp.float32),
        lax.psum_scatter(
            grad_value_full.astype(jnp.bfloat16), "fsdp", scatter_dimension=1, tiled=True
        ).astype(jnp.float32),
        lax.psum_scatter(
            grad_out_full.astype(jnp.bfloat16), "fsdp", scatter_dimension=1, tiled=True
        ).astype(jnp.float32),
        lax.psum_scatter(
            grad_in_full.astype(jnp.bfloat16), "fsdp", scatter_dimension=1, tiled=True
        ).astype(jnp.float32),
        lax.psum_scatter(
            grad_down_full.astype(jnp.bfloat16), "fsdp", scatter_dimension=1, tiled=True
        ).astype(jnp.float32),
    )
    owned_grads = (
        lax.psum_scatter(
            narrow[0].astype(jnp.bfloat16), "ctx", scatter_dimension=0, tiled=True
        ).astype(jnp.float32),
        lax.psum_scatter(
            narrow[1].astype(jnp.bfloat16), "ctx", scatter_dimension=0, tiled=True
        ).astype(jnp.float32),
        lax.psum_scatter(
            narrow[2].astype(jnp.bfloat16), "ctx", scatter_dimension=0, tiled=True
        ).astype(jnp.float32),
        lax.psum_scatter(
            narrow[3].astype(jnp.bfloat16), "ctx", scatter_dimension=0, tiled=True
        ).astype(jnp.float32),
        lax.psum_scatter(
            narrow[4].astype(jnp.bfloat16), "ctx", scatter_dimension=0, tiled=True
        ).astype(jnp.float32),
        lax.psum_scatter(
            narrow[5].astype(jnp.bfloat16), "ctx", scatter_dimension=0, tiled=True
        ).astype(jnp.float32),
    )
    moments = jnp.stack(
        [
            jnp.sum(valid_col * stream * stream),
            jnp.sum(valid_col * attn_branch * attn_branch),
            jnp.sum(valid_col * ffn_branch * ffn_branch),
            jnp.sum(valid_col),
        ]
    )
    summed = lax.psum(
        (
            moments,
            grad_query_vec,
            grad_value_vec,
            grad_out_vec,
            grad_gain_one,
            grad_bias_one,
            grad_in_vec,
            grad_down_vec,
            grad_gain_two,
            grad_bias_two,
        ),
        ("ctx", "fsdp"),
    )
    width_shard = query_bias.shape[0]
    hidden_shard = in_bias.shape[0]

    def own_piece(vector_full, shard_len):
        return lax.dynamic_slice_in_dim(vector_full, ctx_index * shard_len, shard_len, 0)

    rms_values = jnp.sqrt(summed[0][:3] / (summed[0][3] * model_width))
    return (
        layer_out,
        tokens_grad,
        owned_grads[0],
        owned_grads[1],
        owned_grads[2],
        owned_grads[3],
        owned_grads[4],
        owned_grads[5],
        own_piece(summed[1], width_shard),
        own_piece(summed[2], width_shard),
        own_piece(summed[3], width_shard),
        own_piece(summed[4], width_shard),
        own_piece(summed[5], width_shard),
        own_piece(summed[6], hidden_shard),
        own_piece(summed[7], width_shard),
        own_piece(summed[8], width_shard),
        own_piece(summed[9], width_shard),
        rms_values,
    )


HEADS_HERE = 3
HEAD_COLS = HEADS_HERE * HEAD_DIM
rows_first = (((0,), (0,)), ((), ()))
lanes_both = (((1,), (1,)), ((), ()))
plain_contract = (((1,), (0,)), ((), ()))


def effort(microseconds):
    return pl.CostEstimate(
        flops=int(microseconds * 1e8), transcendentals=0, bytes_accessed=int(microseconds * 1e5)
    )


kernel_params = pltpu.CompilerParams(vmem_limit_bytes=24 * 1024 * 1024)


def product32(left_side, right_side, contract):
    return lax.dot_general(left_side, right_side, contract, preferred_element_type=jnp.float32)


def ctx_move(value, mask):
    return lax.ppermute(value, "ctx", [(i, i ^ mask) for i in range(16)])


def core_swap(value):
    return ctx_move(value, 1)


def y_swap(value):
    return ctx_move(value, 2)


def x_swap(value):
    return lax.ppermute(value, "fsdp", [(0, 1), (1, 0)])


def add_b(left_side, right_side):
    return (left_side.astype(jnp.float32) + right_side.astype(jnp.float32)).astype(jnp.bfloat16)


def row_sums(matrix_b):
    return jnp.sum(matrix_b.astype(jnp.float32), axis=0, keepdims=True)


def hold(*values):
    return lax.optimization_barrier(values)


def when_flag(flag_ref, run, idle):
    if flag_ref is None:
        run()
    else:
        pl.when(flag_ref[0] > 0)(run)
        pl.when(flag_ref[0] <= 0)(idle)


def attend_kernel(count, first, last, flagged, *refs):
    flag_ref = refs[0] if flagged else None
    refs = refs[flagged:]
    query_ref, pairs = refs[0], refs[1 : 1 + count]
    refs = refs[1 + count :]
    if not first:
        peak_in, total_in, mixed_in = refs[:3]
        refs = refs[3:]

    def one_head(head, carry):
        key_rows = pl.ds(pl.multiple_of(head * HEAD_DIM, HEAD_DIM), HEAD_DIM)
        value_rows = pl.ds(pl.multiple_of(HEAD_COLS + head * HEAD_DIM, HEAD_DIM), HEAD_DIM)
        query = query_ref[key_rows, :]
        width = query.shape[1]
        if first:
            peak = jnp.full((1, width), -1e30, jnp.float32)
            total = jnp.zeros((1, width), jnp.float32)
            mixed = jnp.zeros((HEAD_DIM, width), jnp.float32)
        else:
            peak, total, mixed = peak_in[head][0:1], total_in[head][0:1], mixed_in[key_rows, :]
        for pair in pairs:
            scores = product32(pair[key_rows, :], query, rows_first)
            new_peak = jnp.maximum(peak, jnp.max(scores, axis=0, keepdims=True))
            expo = jnp.exp(scores - new_peak)
            shrink = jnp.exp(peak - new_peak)
            total = total * shrink + jnp.sum(expo, axis=0, keepdims=True)
            mixed = mixed * shrink + product32(
                pair[value_rows, :], expo.astype(jnp.bfloat16), plain_contract
            )
            peak = new_peak
        if last:
            mixed_out, log_out = refs
            mixed_out[key_rows, :] = (mixed / total).astype(jnp.bfloat16)
            log_out[head] = jnp.broadcast_to(peak + jnp.log(total), (8, width))
        else:
            peak_out, total_out, sum_out = refs
            peak_out[head] = jnp.broadcast_to(peak, (8, width))
            total_out[head] = jnp.broadcast_to(total, (8, width))
            sum_out[key_rows, :] = mixed
        return carry

    def run():
        lax.fori_loop(0, HEADS_HERE, one_head, 0)

    def idle():
        for ref in refs:
            ref[...] = jnp.zeros_like(ref)

    when_flag(flag_ref, run, idle)


def attend_call(query, pairs, state=None, last=False, flag=None):
    width = query.shape[1]
    stat = jax.ShapeDtypeStruct((HEADS_HERE, 8, width), jnp.float32)
    if last:
        outs = [jax.ShapeDtypeStruct((HEAD_COLS, width), jnp.bfloat16), stat]
    else:
        outs = [stat, stat, jax.ShapeDtypeStruct((HEAD_COLS, width), jnp.float32)]
    ins = [query, *pairs, *(() if state is None else state)]
    specs = [pl.BlockSpec(memory_space=pltpu.VMEM)] * len(ins)
    if flag is not None:
        ins, specs = [flag, *ins], [pl.BlockSpec(memory_space=pltpu.SMEM), *specs]
    return pl.pallas_call(
        functools.partial(attend_kernel, len(pairs), state is None, last, int(flag is not None)),
        out_shape=outs,
        in_specs=specs,
        compiler_params=kernel_params,
        cost_estimate=effort(3.5),
    )(*ins)


def attend_back_kernel(count, first, flagged, *refs):
    flag_ref = refs[0] if flagged else None
    refs = refs[flagged:]
    query_ref, grad_ref, log_ref, inner_ref = refs[:4]
    pairs = refs[4 : 4 + count]
    refs = refs[4 + count :]
    if not first:
        grad_query_in, refs = refs[0], refs[1:]
    grad_query_out, grad_pairs = refs[0], refs[1 : 1 + count]
    held, sems = refs[1 + count :]
    hbm_pairs, pairs = pairs, [held.at[i] for i in range(count)]

    def one_head(head, carry):
        key_rows = pl.ds(pl.multiple_of(head * HEAD_DIM, HEAD_DIM), HEAD_DIM)
        value_rows = pl.ds(pl.multiple_of(HEAD_COLS + head * HEAD_DIM, HEAD_DIM), HEAD_DIM)
        query, grad = query_ref[key_rows, :], grad_ref[key_rows, :]
        log_row, inner = log_ref[head][0:1], inner_ref[head][0:1]
        if first:
            grad_query = jnp.zeros((HEAD_DIM, query.shape[1]), jnp.float32)
        else:
            grad_query = grad_query_in[key_rows, :]
        for pair, grad_pair in zip(pairs, grad_pairs):
            keys = pair[key_rows, :]
            probs = jnp.exp(product32(keys, query, rows_first) - log_row)
            grad_probs = product32(pair[value_rows, :], grad, rows_first)
            grad_scores = (probs * (grad_probs - inner)).astype(jnp.bfloat16)
            grad_query = grad_query + product32(keys, grad_scores, plain_contract)
            grad_pair[key_rows, :] = product32(query, grad_scores, lanes_both).astype(jnp.bfloat16)
            grad_pair[value_rows, :] = product32(
                grad, probs.astype(jnp.bfloat16), lanes_both
            ).astype(jnp.bfloat16)
        grad_query_out[key_rows, :] = grad_query
        return carry

    def run():
        copies = [
            pltpu.make_async_copy(hbm, held.at[i], sems.at[i]) for i, hbm in enumerate(hbm_pairs)
        ]
        for copy in copies:
            copy.start()
        for copy in copies:
            copy.wait()
        lax.fori_loop(0, HEADS_HERE, one_head, 0)

    def idle():
        for ref in (grad_query_out, *grad_pairs):
            ref[...] = jnp.zeros_like(ref)

    when_flag(flag_ref, run, idle)


def attend_back_call(query, grad, log_rows, inner, pairs, grad_query=None, flag=None):
    outs = [jax.ShapeDtypeStruct(query.shape, jnp.float32)]
    outs += [jax.ShapeDtypeStruct(pair.shape, jnp.bfloat16) for pair in pairs]
    ins = [query, grad, log_rows, inner, *pairs, *(() if grad_query is None else (grad_query,))]
    specs = [pl.BlockSpec(memory_space=pltpu.VMEM)] * len(ins)
    specs[4 : 4 + len(pairs)] = [pl.BlockSpec(memory_space=pl.ANY)] * len(pairs)
    if flag is not None:
        ins, specs = [flag, *ins], [pl.BlockSpec(memory_space=pltpu.SMEM), *specs]
    return pl.pallas_call(
        functools.partial(
            attend_back_kernel, len(pairs), grad_query is None, int(flag is not None)
        ),
        out_shape=outs,
        in_specs=specs,
        scratch_shapes=[
            pltpu.VMEM((len(pairs), *pairs[0].shape), jnp.bfloat16),
            pltpu.SemaphoreType.DMA((len(pairs),)),
        ],
        compiler_params=kernel_params,
        cost_estimate=effort(10.0),
    )(*ins)


def pack_kernel(me_ref, *refs):
    given, (rows_ref, keep_ref, send_ref, in_keep, in_send) = refs[:4], refs[4:9]
    held, sems = refs[9:13], refs[13]
    copies = [
        pltpu.make_async_copy(source, target, sems.at[i])
        for i, (source, target) in enumerate(zip(given, held))
    ]
    for copy in copies:
        copy.start()
    for copy in copies:
        copy.wait()
    y_low, core_low = (me_ref[0] & 2) == 0, (me_ref[0] & 1) == 0
    for i, ref in enumerate(held[:3]):
        low, high = ref[:, :192], ref[:, 192:]
        keep_ref[0:48, 192 * i : 192 * (i + 1)] = jnp.where(y_low, low, high)
        send_ref[0:48, 192 * i : 192 * (i + 1)] = jnp.where(y_low, high, low)
    keep_ref[48:56, :] = rows_ref[...]
    send_ref[48:56, :] = rows_ref[...]
    for k in range(4):
        even = held[3][:, 384 * k : 384 * k + 192]
        odd = held[3][:, 384 * k + 192 : 384 * (k + 1)]
        in_keep[:, 192 * k : 192 * (k + 1)] = jnp.where(core_low, even, odd)
        in_send[:, 192 * k : 192 * (k + 1)] = jnp.where(core_low, odd, even)


def pack_call(me, weights, rows):
    return pl.pallas_call(
        pack_kernel,
        out_shape=[
            jax.ShapeDtypeStruct(shape, jnp.bfloat16)
            for shape in ((56, 576), (56, 576), (48, 768), (48, 768))
        ],
        in_specs=[
            pl.BlockSpec(memory_space=pltpu.SMEM),
            *[pl.BlockSpec(memory_space=pl.ANY)] * 4,
            pl.BlockSpec(memory_space=pltpu.VMEM),
        ],
        scratch_shapes=[
            *(pltpu.VMEM(weight.shape, jnp.bfloat16) for weight in weights),
            pltpu.SemaphoreType.DMA((4,)),
        ],
        compiler_params=kernel_params,
        cost_estimate=effort(400.0),
    )(me, *weights, rows)


def place_qkv_kernel(me_ref, own_ref, far_ref, mats_ref, wide_ref, heads_ref, hidden_ref, vecs_ref):
    for core, stack in enumerate((own_ref, far_ref)):
        for z in range(4):
            for y in range(2):
                owner = jnp.bitwise_xor(me_ref[0], z * 4 + y * 2 + core)
                mats_ref[owner] = stack[z, y, 0:48]
                vecs_ref[owner] = stack[z, y, 48:56].astype(jnp.float32)
    core_low = (me_ref[0] & 1) == 0
    for i in range(16):
        wide_ref[:, 48 * i : 48 * (i + 1)] = vecs_ref[i, :, 0:48]
    for i in range(8):
        hidden_ref[:, 192 * i : 192 * (i + 1)] = jnp.where(
            core_low, vecs_ref[2 * i, :, 128:320], vecs_ref[2 * i + 1, :, 128:320]
        )
    column = 2 * me_ref[1] + ((me_ref[0] >> 1) & 1)
    for i in range(4):

        @pl.when(column == i)
        def _():
            heads_ref[...] = wide_ref[:, 192 * i : 192 * (i + 1)]


def place_in_kernel(me_ref, own_ref, far_ref, in_ref, out_ref):
    zy_at, x_at = me_ref[0] >> 1, me_ref[1]
    for rel in range(8):
        owner = jnp.bitwise_xor(zy_at, (rel % 4) * 2 + rel // 4)
        low = jnp.where(x_at == 0, own_ref[rel], far_ref[rel])
        high = jnp.where(x_at == 0, far_ref[rel], own_ref[rel])
        for part, at in ((low, 0), (high, 768)):
            in_ref[owner, :, at : at + 384] = part[0:96]
            in_ref[owner, :, at + 384 : at + 768] = part[96:192]
        out_ref[owner, :, 0:384] = low[192:240]
        out_ref[owner, :, 384:768] = high[192:240]


def place_down_kernel(me_ref, own_ref, far_ref, down_ref):
    zy_at, x_at = me_ref[0] >> 1, me_ref[1]
    for y, stack in enumerate((own_ref, far_ref)):
        for z in range(4):
            owner = jnp.bitwise_xor(zy_at, z * 2 + y)
            down_ref[owner, :, 0:384] = jnp.where(x_at == 0, stack[0, z], stack[1, z])
            down_ref[owner, :, 384:768] = jnp.where(x_at == 0, stack[1, z], stack[0, z])


def vectors_kernel(me_ref, *refs):
    rows, (query_ref, hidden_ref), moments, out_ref = refs[:7], refs[7:9], refs[9:13], refs[13]
    out_ref[...] = jnp.zeros_like(out_ref)
    core = me_ref[0] & 1
    column = 2 * me_ref[1] + ((me_ref[0] >> 1) & 1)
    totals = [jnp.sum(ref[...], axis=1, keepdims=True) for ref in moments]
    for i in range(16):
        for row, ref in enumerate(rows):
            out_ref[i, row : row + 1, 0:48] = ref[0:1, 48 * i : 48 * (i + 1)]
        part = query_ref[0:1, 48 * (i % 4) : 48 * (i % 4 + 1)]
        out_ref[i, 7:8, 0:48] = jnp.where(column == i // 4, part, 0.0)
        part = hidden_ref[0:1, 192 * (i // 2) : 192 * (i // 2 + 1)]
        out_ref[i, 0:1, 128:320] = jnp.where(core == i % 2, part, 0.0)
        for row, total in enumerate(totals):
            out_ref[i, row + 1 : row + 2, 128:256] = jnp.broadcast_to(total, (1, 128))


def place_call(kernel, me, stacks, shapes, more=(), scratch=(), cost=2.0):
    return pl.pallas_call(
        kernel,
        out_shape=[jax.ShapeDtypeStruct(shape, jnp.bfloat16) for shape in shapes]
        + [jax.ShapeDtypeStruct(shape, jnp.float32) for shape in more],
        scratch_shapes=[pltpu.VMEM(shape, jnp.float32) for shape in scratch],
        in_specs=[pl.BlockSpec(memory_space=pltpu.SMEM)]
        + [pl.BlockSpec(memory_space=pltpu.VMEM)] * len(stacks),
        compiler_params=kernel_params,
        cost_estimate=effort(cost),
    )(me, *stacks)


def fast_body(
    tokens,
    lengths,
    cotangent,
    query_weight,
    key_weight,
    value_weight,
    out_weight,
    in_weight,
    down_weight,
    query_bias,
    value_bias,
    out_bias,
    attn_norm_gain,
    attn_norm_bias,
    in_bias,
    down_bias,
    ffn_norm_gain,
    ffn_norm_bias,
):
    slot_count, width = tokens.shape[1:]
    me = lax.axis_index("ctx")
    x_at = lax.axis_index("fsdp")
    z_at, y_at, core_at = me >> 2, (me >> 1) & 1, me & 1
    y_low, x_low, core_low = y_at == 0, x_at == 0, core_at == 0
    own_long = lengths[0] == slot_count * lax.axis_size("ctx")
    short_flag = (z_at == 0).astype(jnp.int32).reshape(1)

    half = HEAD_COLS
    vector_rows = sum(
        lax.pad(piece[None, :], jnp.asarray(0, jnp.bfloat16), ((row, 7 - row, 0), (at, 576 - at - piece.shape[0], 0)))
        for row, at, piece in (
            (0, 0, query_bias),
            (1, 0, value_bias),
            (2, 0, out_bias),
            (3, 0, attn_norm_gain),
            (4, 0, attn_norm_bias),
            (5, 0, down_bias),
            (6, 0, ffn_norm_gain),
            (7, 0, ffn_norm_bias),
            (0, 128, in_bias),
        )
    )
    where_me = jnp.stack([me, x_at]).astype(jnp.int32)
    keep_cols, send_cols, in_keep, in_send = pack_call(
        where_me, (query_weight, key_weight, value_weight, in_weight), vector_rows
    )
    token_rows = tokens[0]
    in_got = core_swap(in_send)
    in_block = jnp.concatenate(
        [jnp.where(core_low, in_keep, in_got), jnp.where(core_low, in_got, in_keep)], axis=0
    )
    ffn_block = jnp.concatenate([in_block[:, :384], in_block[:, 384:], out_weight, down_weight])
    other_rows = x_swap(token_rows)
    long_own = jnp.where(own_long, token_rows, other_rows)
    short_own = jnp.where(own_long, other_rows, token_rows)
    got_cols, ffn_one, long_own, short_own = hold(
        y_swap(send_cols), ctx_move(ffn_block, 4), long_own, short_own
    )
    own_block = jnp.stack([keep_cols, got_cols])
    ffn_two = ctx_move(ffn_block, 8)
    z_one, z_two, long_far, short_far = hold(
        ctx_move(own_block, 4), ctx_move(own_block, 8), y_swap(long_own), y_swap(short_own)
    )
    z_three, ffn_two = hold(ctx_move(z_two, 4), ffn_two)
    ffn_three = ctx_move(ffn_two, 4)
    z_stack = jnp.stack([own_block, z_one, z_two, z_three])
    qkv_weight, wide, heads, hidden = place_call(
        place_qkv_kernel,
        where_me,
        (z_stack, core_swap(z_stack)),
        ((16, 48, 576),),
        ((8, 768), (8, half), (8, 1536)),
        ((16, 8, 576),),
    )
    qkv_weight = qkv_weight.reshape(768, 576)
    out_vec, gain_one, bias_one, down_vec, gain_two, bias_two = (
        wide[row : row + 1] for row in range(2, 8)
    )
    in_vec = hidden[:1]
    columns = heads.T
    query_add, value_add = columns[:, 0:1], columns[:, 1:2]
    pair_add = jnp.concatenate([jnp.zeros_like(value_add), value_add], axis=0)

    long_rows = jnp.concatenate([long_own, long_far], axis=0)
    def project(rows):
        query = product32(qkv_weight[:, :half], rows, (((0,), (1,)), ((), ()))) + query_add
        pair = product32(qkv_weight[:, half:], rows, (((0,), (1,)), ((), ()))) + pair_add
        scale = jnp.asarray(score_scale, jnp.bfloat16)
        return query.astype(jnp.bfloat16) * scale, pair.astype(jnp.bfloat16)

    long_query, long_pair = project(long_rows)
    kv_two, kv_one = ctx_move(long_pair, 8), ctx_move(long_pair, 4)
    long_pair_far = core_swap(long_pair)
    state = attend_call(long_query, (long_pair, long_pair_far))
    short_rows = jnp.concatenate([short_own, short_far], axis=0)
    short_query, short_pair = project(short_rows)
    kv_one, ffn_three, short_query, short_pair, *state = hold(
        kv_one, ffn_three, short_query, short_pair, *state
    )
    kv_one_far = core_swap(kv_one)
    ffn_stack = jnp.stack([ffn_block, ffn_one, ffn_two, ffn_three])
    in_stack, down_stack = ffn_stack[:, :240], ffn_stack[:, 240:]
    in_y, down_x = y_swap(in_stack), x_swap(down_stack)
    state = attend_call(long_query, (kv_one, kv_one_far), state)
    kv_two, in_y, down_x, *state = hold(kv_two, in_y, down_x, *state)
    kv_three = ctx_move(kv_two, 4)
    kv_two_far = core_swap(kv_two)
    short_pairs = (short_pair, core_swap(short_pair))
    in_stack = jnp.concatenate([in_stack, in_y], axis=0)
    down_stack = jnp.stack([down_stack, down_x])
    in_stack, down_stack, short_query, *state = hold(in_stack, down_stack, short_query, *state)
    in_far, down_far = x_swap(in_stack), y_swap(down_stack)
    state = attend_call(long_query, (kv_two, kv_two_far), state)
    short_mixed, short_log = attend_call(short_query, short_pairs, last=True, flag=short_flag)
    kv_three, short_mixed, *state = hold(kv_three, short_mixed, *state)
    kv_three_far = core_swap(kv_three)
    long_mixed, long_log = attend_call(long_query, (kv_three, kv_three_far), state, last=True)
    pairs = (
        (long_pair, long_pair_far),
        (kv_one, kv_one_far),
        (kv_two, kv_two_far),
        (kv_three, kv_three_far),
    )

    rows_here = slot_count
    sent = jnp.concatenate([long_mixed[:, rows_here:], short_mixed[:, rows_here:]], axis=0)
    got = y_swap(sent)
    def by_y(mine, theirs):
        return jnp.concatenate(
            [jnp.where(y_low, mine, theirs), jnp.where(y_low, theirs, mine)], axis=0
        )

    long_heads = by_y(long_mixed[:, :rows_here], got[:half])
    short_heads = by_y(short_mixed[:, :rows_here], got[half:])
    own_heads = jnp.where(own_long, long_heads, short_heads)
    sent = jnp.where(own_long, short_heads, long_heads)
    sent, in_far, down_far = hold(sent, in_far, down_far)
    far_heads = x_swap(sent)
    in_all, out_core = place_call(
        place_in_kernel,
        where_me,
        (in_stack, in_far),
        ((8, 96, 1536), (8, 48, 768)),
    )
    (down_all,) = place_call(
        place_down_kernel,
        where_me,
        (down_stack, down_far),
        ((8, 192, 768),),
    )
    in_all, down_all = in_all.reshape(768, 1536), down_all.reshape(1536, 768)
    out_far = core_swap(out_core)
    out_all = jnp.stack(
        [jnp.where(core_low, out_core, out_far), jnp.where(core_low, out_far, out_core)], axis=1
    ).reshape(768, 768)

    mixed_t = jnp.concatenate(
        [jnp.where(x_low, own_heads, far_heads), jnp.where(x_low, far_heads, own_heads)], axis=0
    )

    local_slots = me * slot_count + jnp.arange(slot_count)
    valid_col = (local_slots < lengths[0]).astype(jnp.float32)[:, None]
    attn_branch = product32(mixed_t, out_all, rows_first) + out_vec
    stream = token_rows.astype(jnp.float32) + attn_branch
    norm_one, norm_one_back = jax.vjp(layer_norm, stream, gain_one, bias_one)
    norm_one_b = norm_one.astype(jnp.bfloat16)
    chip_norm = jnp.concatenate([norm_one_b, core_swap(norm_one_b)], axis=0)
    act_out, gelu_back = jax.vjp(gelu_exact, plain_product(chip_norm, in_all) + in_vec)
    act_b = act_out.astype(jnp.bfloat16)
    ffn_got = core_swap(plain_product(act_b[rows_here:], down_all).astype(jnp.bfloat16))
    ffn_part = plain_product(act_b[:rows_here], down_all)
    ffn_branch = ffn_part + ffn_got.astype(jnp.float32) + down_vec
    stream_two = norm_one + ffn_branch
    final_out, norm_two_back = jax.vjp(layer_norm, stream_two, gain_two, bias_two)
    layer_out = (valid_col * final_out).astype(jnp.bfloat16)[None]
    grad_final = valid_col * cotangent[0].astype(jnp.float32)
    grad_stream_two, grad_gain_two, grad_bias_two = norm_two_back(grad_final)
    grad_ffn_b = grad_stream_two.astype(jnp.bfloat16)
    grad_down_vec = row_sums(grad_ffn_b)
    chip_grad = jnp.concatenate([grad_ffn_b, core_swap(grad_ffn_b)], axis=0)
    grad_inner_b = gelu_back(column_product(chip_grad, down_all))[0].astype(jnp.bfloat16)
    grad_in_vec = row_sums(grad_inner_b)
    norm_got = core_swap(column_product(grad_inner_b[rows_here:], in_all).astype(jnp.bfloat16))
    norm_part = column_product(grad_inner_b[:rows_here], in_all)
    grad_norm_one = grad_stream_two + norm_part + norm_got.astype(jnp.float32)
    grad_stream, grad_gain_one, grad_bias_one = norm_one_back(grad_norm_one)
    grad_attn_b = grad_stream.astype(jnp.bfloat16)
    grad_out_vec = row_sums(grad_attn_b)
    grad_mixed_t = product32(out_all, grad_attn_b, lanes_both).astype(jnp.bfloat16)
    ones = jnp.ones((8, slot_count), jnp.bfloat16)
    grad_value_vec = product32(ones, grad_mixed_t, lanes_both)[:1]

    chip_norm, act_b, grad_inner_b, mixed_w, _ = lax.optimization_barrier(
        (chip_norm, act_b, grad_inner_b, mixed_t, grad_mixed_t)
    )
    inner_send = jnp.where(x_low, grad_inner_b[:, 768:], grad_inner_b[:, :768])
    inner_keep = jnp.where(x_low, grad_inner_b[:, :768], grad_inner_b[:, 768:])
    def with_out(in_part, out_part):
        in_part = in_part.astype(jnp.bfloat16).reshape(4, 2, 96, 768)
        return jnp.concatenate([in_part[..., :384], in_part[..., 384:], out_part], axis=2)

    grad_out = plain_product(mixed_w, grad_attn_b).astype(jnp.bfloat16).reshape(4, 2, 2, 48, 768)
    out_sum = add_b(
        jnp.where(core_low, grad_out[:, :, 0], grad_out[:, :, 1]),
        core_swap(jnp.where(core_low, grad_out[:, :, 1], grad_out[:, :, 0])),
    )
    in_send = with_out(
        row_product(chip_norm, inner_send),
        jnp.where(x_low, out_sum[..., 384:], out_sum[..., :384]),
    )
    in_keep_grad = with_out(
        row_product(chip_norm, inner_keep),
        jnp.where(x_low, out_sum[..., :384], out_sum[..., 384:]),
    )
    grad_down = row_product(act_b, chip_grad).astype(jnp.bfloat16).reshape(4, 2, 192, 768)
    down_send = jnp.where(y_low, grad_down[:, 1], grad_down[:, 0])
    down_keep = jnp.where(y_low, grad_down[:, 0], grad_down[:, 1])
    keep_x = jnp.where(x_low, grad_mixed_t[:384], grad_mixed_t[384:])
    got_x = x_swap(jnp.where(x_low, grad_mixed_t[384:], grad_mixed_t[:384]))
    long_x = jnp.where(own_long, keep_x, got_x)
    short_x = jnp.where(own_long, got_x, keep_x)
    both_keep = jnp.where(y_low, long_x[:half], long_x[half:])
    short_keep = jnp.where(y_low, short_x[:half], short_x[half:])
    sent = jnp.concatenate(
        [
            jnp.where(y_low, long_x[half:], long_x[:half]),
            jnp.where(y_low, short_x[half:], short_x[:half]),
        ],
        axis=0,
    )
    got = y_swap(sent)
    long_grad = jnp.concatenate([both_keep, got[:half]], axis=1)
    short_grad = jnp.concatenate([short_keep, got[half:]], axis=1)
    in_send, down_send, long_grad, _ = hold(in_send, down_send, long_grad, got)
    in_x, down_y = x_swap(in_send), y_swap(down_send)

    def inner_rows(mixed, grad):
        product = mixed.astype(jnp.float32) * grad.astype(jnp.float32)
        sums = jnp.sum(product.reshape(HEADS_HERE, HEAD_DIM, -1), axis=1, keepdims=True)
        return jnp.broadcast_to(sums, (HEADS_HERE, 8, sums.shape[-1]))

    long_inner = inner_rows(long_mixed, long_grad)

    grad_query, *grads = attend_back_call(
        long_query, long_grad, long_log, long_inner, sum(pairs[::-1], ())
    )
    near, far = grads[::2], grads[1::2]
    short_query_b, grad_query = hold(short_query, grad_query)
    short_back = attend_back_call(
        short_query_b,
        short_grad,
        short_log,
        inner_rows(short_mixed, short_grad),
        short_pairs,
        flag=short_flag,
    )
    *far, grad_query, in_x, down_y, short_query_g, short_near, short_far = hold(
        *(core_swap(part) for part in far), grad_query, in_x, down_y, *short_back
    )
    three, two, one = (add_b(near[i], far[i]) for i in range(3))
    near_own, far_own = near[3], far[3]
    in_sum = add_b(in_keep_grad, in_x)
    down_sum = add_b(down_keep, down_y)
    three_hop, one_got = ctx_move(three, 4), ctx_move(one, 4)
    two_got = ctx_move(add_b(two, three_hop), 8)
    in_send = jnp.where(y_low, in_sum[:, 1], in_sum[:, 0])
    down_send = jnp.where(x_low, down_sum[..., 384:], down_sum[..., :384])
    in_send, down_send, short_far = hold(in_send, down_send, short_far)
    in_y, down_x = y_swap(in_send), x_swap(down_send)
    short_pair_grad = add_b(short_near, core_swap(short_far))
    stream, attn_branch, ffn_branch, in_y = hold(stream, attn_branch, ffn_branch, in_y)
    (
        grad_value_vec,
        grad_out_vec,
        grad_gain_one,
        grad_bias_one,
        grad_down_vec,
        grad_gain_two,
        grad_bias_two,
        grad_in_vec,
        in_y,
    ) = hold(
        grad_value_vec,
        grad_out_vec,
        grad_gain_one,
        grad_bias_one,
        grad_down_vec,
        grad_gain_two,
        grad_bias_two,
        grad_in_vec,
        in_y,
    )
    long_query_grad = (grad_query * score_scale).astype(jnp.bfloat16)
    short_query_grad = (short_query_g * score_scale).astype(jnp.bfloat16)
    ones_wide = jnp.ones((8, 2 * slot_count), jnp.bfloat16)
    query_sums = product32(ones_wide, long_query_grad, lanes_both) + product32(
        ones_wide, short_query_grad, lanes_both
    )
    (owner_sums,) = place_call(
        vectors_kernel,
        where_me,
        (
            grad_value_vec,
            grad_out_vec,
            grad_gain_one,
            grad_bias_one,
            grad_down_vec,
            grad_gain_two,
            grad_bias_two,
            query_sums,
            grad_in_vec,
            jnp.sum(valid_col * stream * stream, axis=0, keepdims=True),
            jnp.sum(valid_col * attn_branch * attn_branch, axis=0, keepdims=True),
            jnp.sum(valid_col * ffn_branch * ffn_branch, axis=0, keepdims=True),
            jnp.broadcast_to(jnp.sum(valid_col, axis=0, keepdims=True) / 128, (1, 128)),
        ),
        (),
        ((16, 8, 384),),
    )
    owner_sums = owner_sums.astype(jnp.bfloat16)
    owner_sums = add_b(owner_sums, x_swap(owner_sums)).reshape(4, 2, 2, 8, 384)
    owner_sums = jnp.pad(owner_sums, ((0, 0), (0, 0), (0, 0), (0, 0), (0, 192)))

    def back_rows(grads):
        return product32(grads, qkv_weight, (((0,), (1,)), ((), ())))

    short_all = jnp.concatenate([short_query_grad, short_pair_grad], axis=0)
    short_rows_back = back_rows(short_all)
    short_got = y_swap(short_rows_back[rows_here:].astype(jnp.bfloat16))
    in_sum = add_b(jnp.where(y_low, in_sum[:, 0], in_sum[:, 1]), in_y)
    down_sum = add_b(jnp.where(x_low, down_sum[..., :384], down_sum[..., 384:]), down_x)
    ffn_sum = jnp.concatenate([in_sum, down_sum], axis=1)
    two_got, one_got, ffn_sum, owner_sums, short_got, short_rows_back = hold(
        two_got, one_got, ffn_sum, owner_sums, short_got, short_rows_back
    )
    long_pair_grad = near_own.astype(jnp.float32)
    for got_part in (far_own, one_got, two_got):
        long_pair_grad = long_pair_grad + got_part.astype(jnp.float32)
    long_pair_grad = long_pair_grad.astype(jnp.bfloat16)
    long_all = jnp.concatenate([long_query_grad, long_pair_grad], axis=0)
    long_back = back_rows(long_all)
    long_back, long_all = hold(long_back, long_all)
    long_got = y_swap(long_back[rows_here:].astype(jnp.bfloat16)).astype(jnp.float32)

    grad_qkv = product32(long_rows, long_all, (((0,), (1,)), ((), ()))) + product32(
        short_rows, short_all, (((0,), (1,)), ((), ()))
    )
    grad_qkv = grad_qkv.astype(jnp.bfloat16).reshape(4, 2, 2, 48, 576)
    grad_qkv = jnp.concatenate([grad_qkv, owner_sums], axis=3)
    core_keep = jnp.where(core_low, grad_qkv[:, :, 0], grad_qkv[:, :, 1])
    core_send = jnp.where(core_low, grad_qkv[:, :, 1], grad_qkv[:, :, 0])
    core_sum = add_b(core_keep, core_swap(core_send))

    def by_z(stack):
        return [
            lax.dynamic_index_in_dim(stack, z_at ^ mask, 0, keepdims=False) for mask in range(4)
        ]

    own_sum, one_part, two_part, three_part = by_z(core_sum)
    one_part = ctx_move(one_part, 4)
    two_part = ctx_move(add_b(two_part, ctx_move(three_part, 4)), 8)
    own_sum = sum(part.astype(jnp.float32) for part in (own_sum, one_part, two_part))
    y_keep = jnp.where(y_low, own_sum[0], own_sum[1])
    y_got = y_swap(jnp.where(y_low, own_sum[1], own_sum[0]).astype(jnp.bfloat16))
    own_part, one_part, two_part, three_part = by_z(ffn_sum)
    one_part = ctx_move(one_part, 4)
    two_part = ctx_move(add_b(two_part, ctx_move(three_part, 4)), 8)
    one_part, two_part, y_got = hold(one_part, two_part, y_got)
    ffn_owned = sum(part.astype(jnp.float32) for part in (own_part, one_part, two_part))
    y_got = y_got.astype(jnp.float32)
    vector_sums = y_keep[48:] + y_got[48:]
    y_keep, y_got = y_keep[:48], y_got[:48]
    low_part, high_part = jnp.where(y_low, y_keep, y_got), jnp.where(y_low, y_got, y_keep)
    owned_qkv = [
        jnp.concatenate(
            [low_part[:, half * i : half * (i + 1)], high_part[:, half * i : half * (i + 1)]],
            axis=1,
        )
        for i in range(3)
    ]

    in_owned = jnp.concatenate([ffn_owned[:96], ffn_owned[96:192]], axis=1)
    in_owned = in_owned.astype(jnp.bfloat16).reshape(2, 48, 768)
    in_mine = jnp.where(core_low, in_owned[0], in_owned[1])
    in_other = core_swap(jnp.where(core_low, in_owned[1], in_owned[0]))
    in_even = jnp.where(core_low, in_mine, in_other).astype(jnp.float32)
    in_odd = jnp.where(core_low, in_other, in_mine).astype(jnp.float32)
    owned_in = jnp.concatenate(
        [
            part[:, 192 * k : 192 * (k + 1)]
            for k in range(4)
            for part in (in_even, in_odd)
        ],
        axis=1,
    )
    owned_out, owned_down = ffn_owned[192:240], ffn_owned[240:]

    short_part = short_rows_back[:rows_here] + short_got.astype(jnp.float32)
    long_part = long_back[:rows_here] + long_got
    own_part = jnp.where(own_long, long_part, short_part)
    far_part = x_swap(jnp.where(own_long, short_part, long_part).astype(jnp.bfloat16))
    tokens_grad = (grad_stream + own_part + far_part.astype(jnp.float32)).astype(jnp.bfloat16)

    def own_piece(row):
        return vector_sums[row, :48]

    rms_values = jnp.sqrt(vector_sums[1:4, 128] / (vector_sums[4, 128] * width))
    return (
        layer_out,
        tokens_grad[None],
        owned_qkv[0],
        owned_qkv[1],
        owned_qkv[2],
        owned_out,
        owned_in,
        owned_down,
        vector_sums[7, :48],
        own_piece(0),
        own_piece(1),
        own_piece(2),
        own_piece(3),
        vector_sums[0, 128:320],
        own_piece(4),
        own_piece(5),
        own_piece(6),
        rms_values,
    )


def layer_body(tokens, *others):
    fits = lax.axis_size("ctx") == 16 and lax.axis_size("fsdp") == 2
    if fits and tokens.shape == (1, 256, 768):
        return fast_body(tokens, *others)
    return body(tokens, *others)


def solution(mesh):
    in_specs = (
        P("fsdp", "ctx", None),
        P("fsdp"),
        P("fsdp", "ctx", None),
        P("ctx", "fsdp"),
        P("ctx", "fsdp"),
        P("ctx", "fsdp"),
        P("ctx", "fsdp"),
        P("ctx", "fsdp"),
        P("ctx", "fsdp"),
        P("ctx"),
        P("ctx"),
        P("ctx"),
        P("ctx"),
        P("ctx"),
        P("ctx"),
        P("ctx"),
        P("ctx"),
        P("ctx"),
    )
    out_specs = (
        P("fsdp", "ctx", None),
        P("fsdp", "ctx", None),
        P("ctx", "fsdp"),
        P("ctx", "fsdp"),
        P("ctx", "fsdp"),
        P("ctx", "fsdp"),
        P("ctx", "fsdp"),
        P("ctx", "fsdp"),
        P("ctx"),
        P("ctx"),
        P("ctx"),
        P("ctx"),
        P("ctx"),
        P("ctx"),
        P("ctx"),
        P("ctx"),
        P("ctx"),
        P(),
    )
    return jax.shard_map(layer_body, mesh=mesh, in_specs=in_specs, out_specs=out_specs, check_vma=False)
```

```python
import functools

import jax
import jax.numpy as jnp
from jax import lax
from jax.experimental import pallas as pl
from jax.experimental.pallas import tpu as pltpu
from jax.sharding import PartitionSpec as P

HEAD_DIM = 64


norm_eps = 1e-12
score_scale = 0.125
masked_score = -1000000000.0
rows_contract = (((0,), (0,)), ((), ()))
columns_contract = (((1,), (1,)), ((), ()))


def layer_norm(stream, gain_vec, shift_vec):
    center = jnp.mean(stream, axis=-1, keepdims=True)
    offset = stream - center
    spread = jnp.mean(offset * offset, axis=-1, keepdims=True)
    return offset * lax.rsqrt(spread + norm_eps) * gain_vec + shift_vec


def gelu_exact(inner_pre):
    return jax.nn.gelu(inner_pre, approximate=False)


def plain_product(left_side, right_side):
    return jnp.dot(left_side, right_side, preferred_element_type=jnp.float32)


def row_product(left_side, right_side):
    return lax.dot_general(left_side, right_side, rows_contract, preferred_element_type=jnp.float32)


def column_product(left_side, right_side):
    return lax.dot_general(
        left_side, right_side, columns_contract, preferred_element_type=jnp.float32
    )


def head_scores(query_head, key_head, key_ok):
    scores = (
        jnp.einsum("sqd,skd->sqk", query_head, key_head, preferred_element_type=jnp.float32)
        * score_scale
    )
    return jnp.where(key_ok[:, None, :], scores, masked_score)


def attend(query_seq, pair_all, key_ok):
    seq_count, slot_count, model_width = query_seq.shape
    heads_count = model_width // HEAD_DIM

    def one_head(head_index, loop_state):
        mixed_out, log_totals = loop_state
        head_start = head_index * HEAD_DIM
        query_head = lax.dynamic_slice_in_dim(query_seq, head_start, HEAD_DIM, 2)
        key_head = lax.dynamic_slice_in_dim(pair_all, head_start, HEAD_DIM, 2)
        value_head = lax.dynamic_slice_in_dim(pair_all, model_width + head_start, HEAD_DIM, 2)
        scores = head_scores(query_head, key_head, key_ok)
        row_peak = jnp.max(scores, axis=-1, keepdims=True)
        row_expo = jnp.exp(scores - row_peak)
        row_total = jnp.sum(row_expo, axis=-1, keepdims=True)
        attn_probs = (row_expo / row_total).astype(jnp.bfloat16)
        head_out = jnp.einsum(
            "sqk,skd->sqd", attn_probs, value_head, preferred_element_type=jnp.float32
        )
        mixed_out = lax.dynamic_update_slice_in_dim(mixed_out, head_out, head_start, 2)
        log_row = row_peak[..., 0] + jnp.log(row_total[..., 0])
        log_totals = lax.dynamic_update_index_in_dim(log_totals, log_row, head_index, 0)
        return (mixed_out, log_totals)

    start_state = (
        jnp.zeros((seq_count, slot_count, model_width), jnp.float32),
        jnp.zeros((heads_count, seq_count, slot_count), jnp.float32),
    )
    return lax.fori_loop(0, heads_count, one_head, start_state)


def attend_back(query_seq, pair_all, key_ok, log_totals, grad_mixed):
    seq_count, slot_count, model_width = query_seq.shape
    heads_count = model_width // HEAD_DIM

    def one_head(head_index, loop_state):
        grad_query, grad_pair = loop_state
        head_start = head_index * HEAD_DIM
        query_head = lax.dynamic_slice_in_dim(query_seq, head_start, HEAD_DIM, 2)
        key_head = lax.dynamic_slice_in_dim(pair_all, head_start, HEAD_DIM, 2)
        value_head = lax.dynamic_slice_in_dim(pair_all, model_width + head_start, HEAD_DIM, 2)
        grad_head = lax.dynamic_slice_in_dim(grad_mixed, head_start, HEAD_DIM, 2)
        scores = head_scores(query_head, key_head, key_ok)
        log_row = lax.dynamic_index_in_dim(log_totals, head_index, 0, keepdims=False)
        attn_probs = jnp.exp(scores - log_row[..., None])
        probs_b = attn_probs.astype(jnp.bfloat16)
        grad_probs = jnp.einsum(
            "sqd,skd->sqk", grad_head, value_head, preferred_element_type=jnp.float32
        )
        row_inner = jnp.sum(attn_probs * grad_probs, axis=-1, keepdims=True)
        grad_scores = (attn_probs * (grad_probs - row_inner)).astype(jnp.bfloat16)
        grad_query_head = (
            jnp.einsum("sqk,skd->sqd", grad_scores, key_head, preferred_element_type=jnp.float32)
            * score_scale
        )
        grad_key_head = (
            jnp.einsum("sqk,sqd->skd", grad_scores, query_head, preferred_element_type=jnp.float32)
            * score_scale
        )
        grad_value_head = jnp.einsum(
            "sqk,sqd->skd", probs_b, grad_head, preferred_element_type=jnp.float32
        )
        grad_query = lax.dynamic_update_slice_in_dim(grad_query, grad_query_head, head_start, 2)
        grad_pair = lax.dynamic_update_slice_in_dim(grad_pair, grad_key_head, head_start, 2)
        grad_pair = lax.dynamic_update_slice_in_dim(
            grad_pair, grad_value_head, model_width + head_start, 2
        )
        return (grad_query, grad_pair)

    start_state = (jnp.zeros(query_seq.shape, jnp.float32), jnp.zeros(pair_all.shape, jnp.float32))
    return lax.fori_loop(0, heads_count, one_head, start_state)


def column_sums(matrix_b):
    return jnp.sum(matrix_b.astype(jnp.float32), axis=0)


def body(
    tokens,
    lengths,
    cotangent,
    query_weight,
    key_weight,
    value_weight,
    out_weight,
    in_weight,
    down_weight,
    query_bias,
    value_bias,
    out_bias,
    attn_norm_gain,
    attn_norm_bias,
    in_bias,
    down_bias,
    ffn_norm_gain,
    ffn_norm_bias,
):
    seq_count, slot_count, model_width = tokens.shape
    row_count = seq_count * slot_count
    ctx_size = lax.axis_size("ctx")
    ctx_index = lax.axis_index("ctx")
    row_parts = (
        lax.all_gather(query_weight, "ctx", axis=0, tiled=True),
        lax.all_gather(key_weight, "ctx", axis=0, tiled=True),
        lax.all_gather(value_weight, "ctx", axis=0, tiled=True),
        lax.all_gather(out_weight, "ctx", axis=0, tiled=True),
        lax.all_gather(in_weight, "ctx", axis=0, tiled=True),
        lax.all_gather(down_weight, "ctx", axis=0, tiled=True),
        lax.all_gather(query_bias, "ctx", axis=0, tiled=True),
        lax.all_gather(value_bias, "ctx", axis=0, tiled=True),
        lax.all_gather(out_bias, "ctx", axis=0, tiled=True),
        lax.all_gather(attn_norm_gain, "ctx", axis=0, tiled=True),
        lax.all_gather(attn_norm_bias, "ctx", axis=0, tiled=True),
        lax.all_gather(in_bias, "ctx", axis=0, tiled=True),
        lax.all_gather(down_bias, "ctx", axis=0, tiled=True),
        lax.all_gather(ffn_norm_gain, "ctx", axis=0, tiled=True),
        lax.all_gather(ffn_norm_bias, "ctx", axis=0, tiled=True),
    )
    full_mats = (
        lax.all_gather(row_parts[0], "fsdp", axis=1, tiled=True),
        lax.all_gather(row_parts[1], "fsdp", axis=1, tiled=True),
        lax.all_gather(row_parts[2], "fsdp", axis=1, tiled=True),
        lax.all_gather(row_parts[3], "fsdp", axis=1, tiled=True),
        lax.all_gather(row_parts[4], "fsdp", axis=1, tiled=True),
        lax.all_gather(row_parts[5], "fsdp", axis=1, tiled=True),
    )
    query_full, key_full, value_full, out_full, in_full, down_full = full_mats
    query_vec = row_parts[6].astype(jnp.float32)
    value_vec = row_parts[7].astype(jnp.float32)
    out_vec = row_parts[8].astype(jnp.float32)
    gain_one = row_parts[9].astype(jnp.float32)
    bias_one = row_parts[10].astype(jnp.float32)
    in_vec = row_parts[11].astype(jnp.float32)
    down_vec = row_parts[12].astype(jnp.float32)
    gain_two = row_parts[13].astype(jnp.float32)
    bias_two = row_parts[14].astype(jnp.float32)
    local_slots = ctx_index * slot_count + jnp.arange(slot_count)
    local_ok = local_slots[None, :] < lengths[:, None]
    valid_mask = local_ok.astype(jnp.float32)
    valid_col = valid_mask.reshape(row_count, 1)
    key_ok = jnp.arange(slot_count * ctx_size)[None, :] < lengths[:, None]
    token_rows = tokens.reshape(row_count, model_width)
    queries_b = (plain_product(token_rows, query_full) + query_vec).astype(jnp.bfloat16)
    keys_b = plain_product(token_rows, key_full).astype(jnp.bfloat16)
    values_b = (plain_product(token_rows, value_full) + value_vec).astype(jnp.bfloat16)
    pair_local = jnp.concatenate([keys_b, values_b], axis=1).reshape(
        seq_count, slot_count, 2 * model_width
    )
    pair_all = lax.all_gather(pair_local, "ctx", axis=1, tiled=True)
    query_seq = queries_b.reshape(seq_count, slot_count, model_width)
    mixed_out, log_totals = attend(query_seq, pair_all, key_ok)
    mixed_b = mixed_out.reshape(row_count, model_width).astype(jnp.bfloat16)
    attn_branch = plain_product(mixed_b, out_full) + out_vec
    stream = token_rows.astype(jnp.float32) + attn_branch
    norm_one, norm_one_back = jax.vjp(layer_norm, stream, gain_one, bias_one)
    norm_one_b = norm_one.astype(jnp.bfloat16)
    inner_pre = plain_product(norm_one_b, in_full) + in_vec
    act_out, gelu_back = jax.vjp(gelu_exact, inner_pre)
    act_b = act_out.astype(jnp.bfloat16)
    ffn_branch = plain_product(act_b, down_full) + down_vec
    stream_two = norm_one + ffn_branch
    final_out, norm_two_back = jax.vjp(layer_norm, stream_two, gain_two, bias_two)
    layer_out = (
        (valid_col * final_out).astype(jnp.bfloat16).reshape(seq_count, slot_count, model_width)
    )
    grad_final = valid_col * cotangent.reshape(row_count, model_width).astype(jnp.float32)
    grad_stream_two, grad_gain_two, grad_bias_two = norm_two_back(grad_final)
    grad_ffn_b = grad_stream_two.astype(jnp.bfloat16)
    grad_down_vec = column_sums(grad_ffn_b)
    grad_down_full = row_product(act_b, grad_ffn_b)
    grad_inner_b = gelu_back(column_product(grad_ffn_b, down_full))[0].astype(jnp.bfloat16)
    grad_in_vec = column_sums(grad_inner_b)
    grad_in_full = row_product(norm_one_b, grad_inner_b)
    grad_norm_one = grad_stream_two + column_product(grad_inner_b, in_full)
    grad_stream, grad_gain_one, grad_bias_one = norm_one_back(grad_norm_one)
    grad_attn_b = grad_stream.astype(jnp.bfloat16)
    grad_out_vec = column_sums(grad_attn_b)
    grad_out_full = row_product(mixed_b, grad_attn_b)
    grad_mixed = (
        column_product(grad_attn_b, out_full)
        .astype(jnp.bfloat16)
        .reshape(seq_count, slot_count, model_width)
    )
    grad_query_seq, grad_pair = attend_back(query_seq, pair_all, key_ok, log_totals, grad_mixed)
    grad_pair_local = lax.psum_scatter(
        grad_pair.astype(jnp.bfloat16), "ctx", scatter_dimension=1, tiled=True
    ).astype(jnp.float32)
    grad_keys_b = (
        grad_pair_local[:, :, :model_width].reshape(row_count, model_width).astype(jnp.bfloat16)
    )
    grad_values_b = (
        grad_pair_local[:, :, model_width:].reshape(row_count, model_width).astype(jnp.bfloat16)
    )
    grad_queries_b = grad_query_seq.reshape(row_count, model_width).astype(jnp.bfloat16)
    grad_query_full = row_product(token_rows, grad_queries_b)
    grad_query_vec = column_sums(grad_queries_b)
    grad_key_full = row_product(token_rows, grad_keys_b)
    grad_value_full = row_product(token_rows, grad_values_b)
    grad_value_vec = column_sums(grad_values_b)
    tokens_grad = (
        (
            grad_stream
            + column_product(grad_queries_b, query_full)
            + column_product(grad_keys_b, key_full)
            + column_product(grad_values_b, value_full)
        )
        .astype(jnp.bfloat16)
        .reshape(seq_count, slot_count, model_width)
    )
    narrow = (
        lax.psum_scatter(
            grad_query_full.astype(jnp.bfloat16), "fsdp", scatter_dimension=1, tiled=True
        ).astype(jnp.float32),
        lax.psum_scatter(
            grad_key_full.astype(jnp.bfloat16), "fsdp", scatter_dimension=1, tiled=True
        ).astype(jnp.float32),
        lax.psum_scatter(
            grad_value_full.astype(jnp.bfloat16), "fsdp", scatter_dimension=1, tiled=True
        ).astype(jnp.float32),
        lax.psum_scatter(
            grad_out_full.astype(jnp.bfloat16), "fsdp", scatter_dimension=1, tiled=True
        ).astype(jnp.float32),
        lax.psum_scatter(
            grad_in_full.astype(jnp.bfloat16), "fsdp", scatter_dimension=1, tiled=True
        ).astype(jnp.float32),
        lax.psum_scatter(
            grad_down_full.astype(jnp.bfloat16), "fsdp", scatter_dimension=1, tiled=True
        ).astype(jnp.float32),
    )
    owned_grads = (
        lax.psum_scatter(
            narrow[0].astype(jnp.bfloat16), "ctx", scatter_dimension=0, tiled=True
        ).astype(jnp.float32),
        lax.psum_scatter(
            narrow[1].astype(jnp.bfloat16), "ctx", scatter_dimension=0, tiled=True
        ).astype(jnp.float32),
        lax.psum_scatter(
            narrow[2].astype(jnp.bfloat16), "ctx", scatter_dimension=0, tiled=True
        ).astype(jnp.float32),
        lax.psum_scatter(
            narrow[3].astype(jnp.bfloat16), "ctx", scatter_dimension=0, tiled=True
        ).astype(jnp.float32),
        lax.psum_scatter(
            narrow[4].astype(jnp.bfloat16), "ctx", scatter_dimension=0, tiled=True
        ).astype(jnp.float32),
        lax.psum_scatter(
            narrow[5].astype(jnp.bfloat16), "ctx", scatter_dimension=0, tiled=True
        ).astype(jnp.float32),
    )
    moments = jnp.stack(
        [
            jnp.sum(valid_col * stream * stream),
            jnp.sum(valid_col * attn_branch * attn_branch),
            jnp.sum(valid_col * ffn_branch * ffn_branch),
            jnp.sum(valid_col),
        ]
    )
    summed = lax.psum(
        (
            moments,
            grad_query_vec,
            grad_value_vec,
            grad_out_vec,
            grad_gain_one,
            grad_bias_one,
            grad_in_vec,
            grad_down_vec,
            grad_gain_two,
            grad_bias_two,
        ),
        ("ctx", "fsdp"),
    )
    width_shard = query_bias.shape[0]
    hidden_shard = in_bias.shape[0]

    def own_piece(vector_full, shard_len):
        return lax.dynamic_slice_in_dim(vector_full, ctx_index * shard_len, shard_len, 0)

    rms_values = jnp.sqrt(summed[0][:3] / (summed[0][3] * model_width))
    return (
        layer_out,
        tokens_grad,
        owned_grads[0],
        owned_grads[1],
        owned_grads[2],
        owned_grads[3],
        owned_grads[4],
        owned_grads[5],
        own_piece(summed[1], width_shard),
        own_piece(summed[2], width_shard),
        own_piece(summed[3], width_shard),
        own_piece(summed[4], width_shard),
        own_piece(summed[5], width_shard),
        own_piece(summed[6], hidden_shard),
        own_piece(summed[7], width_shard),
        own_piece(summed[8], width_shard),
        own_piece(summed[9], width_shard),
        rms_values,
    )


HEADS_HERE = 3
HEAD_COLS = HEADS_HERE * HEAD_DIM
rows_first = (((0,), (0,)), ((), ()))
lanes_both = (((1,), (1,)), ((), ()))
plain_contract = (((1,), (0,)), ((), ()))


def effort(microseconds):
    return pl.CostEstimate(
        flops=int(microseconds * 1e8), transcendentals=0, bytes_accessed=int(microseconds * 1e5)
    )


kernel_params = pltpu.CompilerParams(vmem_limit_bytes=24 * 1024 * 1024)


def product32(left_side, right_side, contract):
    return lax.dot_general(left_side, right_side, contract, preferred_element_type=jnp.float32)


def ctx_move(value, mask):
    return lax.ppermute(value, "ctx", [(i, i ^ mask) for i in range(16)])


def core_swap(value):
    return ctx_move(value, 1)


def y_swap(value):
    return ctx_move(value, 2)


def x_swap(value):
    return lax.ppermute(value, "fsdp", [(0, 1), (1, 0)])


def add_b(left_side, right_side):
    return (left_side.astype(jnp.float32) + right_side.astype(jnp.float32)).astype(jnp.bfloat16)


def row_sums(matrix_b):
    return jnp.sum(matrix_b.astype(jnp.float32), axis=0, keepdims=True)


def hold(*values):
    return lax.optimization_barrier(values)


def when_flag(flag_ref, run, idle):
    if flag_ref is None:
        run()
    else:
        pl.when(flag_ref[0] > 0)(run)
        pl.when(flag_ref[0] <= 0)(idle)


def attend_kernel(count, first, last, flagged, *refs):
    flag_ref = refs[0] if flagged else None
    refs = refs[flagged:]
    query_ref, pairs = refs[0], refs[1 : 1 + count]
    refs = refs[1 + count :]
    if not first:
        peak_in, total_in, mixed_in = refs[:3]
        refs = refs[3:]

    def one_head(head, carry):
        key_rows = pl.ds(pl.multiple_of(head * HEAD_DIM, HEAD_DIM), HEAD_DIM)
        value_rows = pl.ds(pl.multiple_of(HEAD_COLS + head * HEAD_DIM, HEAD_DIM), HEAD_DIM)
        query = query_ref[key_rows, :]
        width = query.shape[1]
        if first:
            peak = jnp.full((1, width), -1e30, jnp.float32)
            total = jnp.zeros((1, width), jnp.float32)
            mixed = jnp.zeros((HEAD_DIM, width), jnp.float32)
        else:
            peak, total, mixed = peak_in[head][0:1], total_in[head][0:1], mixed_in[key_rows, :]
        for pair in pairs:
            scores = product32(pair[key_rows, :], query, rows_first)
            new_peak = jnp.maximum(peak, jnp.max(scores, axis=0, keepdims=True))
            expo = jnp.exp(scores - new_peak)
            shrink = jnp.exp(peak - new_peak)
            total = total * shrink + jnp.sum(expo, axis=0, keepdims=True)
            mixed = mixed * shrink + product32(
                pair[value_rows, :], expo.astype(jnp.bfloat16), plain_contract
            )
            peak = new_peak
        if last:
            mixed_out, log_out = refs
            mixed_out[key_rows, :] = (mixed / total).astype(jnp.bfloat16)
            log_out[head] = jnp.broadcast_to(peak + jnp.log(total), (8, width))
        else:
            peak_out, total_out, sum_out = refs
            peak_out[head] = jnp.broadcast_to(peak, (8, width))
            total_out[head] = jnp.broadcast_to(total, (8, width))
            sum_out[key_rows, :] = mixed
        return carry

    def run():
        lax.fori_loop(0, HEADS_HERE, one_head, 0)

    def idle():
        for ref in refs:
            ref[...] = jnp.zeros_like(ref)

    when_flag(flag_ref, run, idle)


def attend_call(query, pairs, state=None, last=False, flag=None):
    width = query.shape[1]
    stat = jax.ShapeDtypeStruct((HEADS_HERE, 8, width), jnp.float32)
    if last:
        outs = [jax.ShapeDtypeStruct((HEAD_COLS, width), jnp.bfloat16), stat]
    else:
        outs = [stat, stat, jax.ShapeDtypeStruct((HEAD_COLS, width), jnp.float32)]
    ins = [query, *pairs, *(() if state is None else state)]
    specs = [pl.BlockSpec(memory_space=pltpu.VMEM)] * len(ins)
    if flag is not None:
        ins, specs = [flag, *ins], [pl.BlockSpec(memory_space=pltpu.SMEM), *specs]
    return pl.pallas_call(
        functools.partial(attend_kernel, len(pairs), state is None, last, int(flag is not None)),
        out_shape=outs,
        in_specs=specs,
        compiler_params=kernel_params,
        cost_estimate=effort(3.5),
    )(*ins)


def attend_back_kernel(count, first, flagged, *refs):
    flag_ref = refs[0] if flagged else None
    refs = refs[flagged:]
    query_ref, grad_ref, log_ref, mixed_ref = refs[:4]
    pairs = refs[4 : 4 + count]
    refs = refs[4 + count :]
    if not first:
        grad_query_in, refs = refs[0], refs[1:]
    grad_query_out, grad_pairs = refs[0], refs[1 : 1 + count]
    held, sems = refs[1 + count :]
    hbm_pairs, pairs = pairs, [held.at[i] for i in range(count)]

    def one_head(head, carry):
        key_rows = pl.ds(pl.multiple_of(head * HEAD_DIM, HEAD_DIM), HEAD_DIM)
        value_rows = pl.ds(pl.multiple_of(HEAD_COLS + head * HEAD_DIM, HEAD_DIM), HEAD_DIM)
        query, grad = query_ref[key_rows, :], grad_ref[key_rows, :]
        log_row = log_ref[head][0:1]
        inner = jnp.sum(
            mixed_ref[key_rows, :].astype(jnp.float32) * grad.astype(jnp.float32),
            axis=0,
            keepdims=True,
        )
        if first:
            grad_query = jnp.zeros((HEAD_DIM, query.shape[1]), jnp.float32)
        else:
            grad_query = grad_query_in[key_rows, :]
        for pair, grad_pair in zip(pairs, grad_pairs):
            keys = pair[key_rows, :]
            probs = jnp.exp(product32(keys, query, rows_first) - log_row)
            grad_probs = product32(pair[value_rows, :], grad, rows_first)
            grad_scores = (probs * (grad_probs - inner)).astype(jnp.bfloat16)
            grad_query = grad_query + product32(keys, grad_scores, plain_contract)
            grad_pair[key_rows, :] = product32(query, grad_scores, lanes_both).astype(jnp.bfloat16)
            grad_pair[value_rows, :] = product32(
                grad, probs.astype(jnp.bfloat16), lanes_both
            ).astype(jnp.bfloat16)
        grad_query_out[key_rows, :] = grad_query
        return carry

    def run():
        copies = [
            pltpu.make_async_copy(hbm, held.at[i], sems.at[i]) for i, hbm in enumerate(hbm_pairs)
        ]
        for copy in copies:
            copy.start()
        for copy in copies:
            copy.wait()
        lax.fori_loop(0, HEADS_HERE, one_head, 0)

    def idle():
        for ref in (grad_query_out, *grad_pairs):
            ref[...] = jnp.zeros_like(ref)

    when_flag(flag_ref, run, idle)


def attend_back_call(query, grad, log_rows, mixed, pairs, grad_query=None, flag=None):
    outs = [jax.ShapeDtypeStruct(query.shape, jnp.float32)]
    outs += [jax.ShapeDtypeStruct(pair.shape, jnp.bfloat16) for pair in pairs]
    ins = [query, grad, log_rows, mixed, *pairs, *(() if grad_query is None else (grad_query,))]
    specs = [pl.BlockSpec(memory_space=pltpu.VMEM)] * len(ins)
    specs[4 : 4 + len(pairs)] = [pl.BlockSpec(memory_space=pl.ANY)] * len(pairs)
    if flag is not None:
        ins, specs = [flag, *ins], [pl.BlockSpec(memory_space=pltpu.SMEM), *specs]
    return pl.pallas_call(
        functools.partial(
            attend_back_kernel, len(pairs), grad_query is None, int(flag is not None)
        ),
        out_shape=outs,
        in_specs=specs,
        scratch_shapes=[
            pltpu.VMEM((len(pairs), *pairs[0].shape), jnp.bfloat16),
            pltpu.SemaphoreType.DMA((len(pairs),)),
        ],
        compiler_params=kernel_params,
        cost_estimate=effort(10.0),
    )(*ins)


def pack_kernel(me_ref, *refs):
    given, (rows_ref, keep_ref, send_ref, in_keep, in_send) = refs[:4], refs[4:9]
    held, sems = refs[9:13], refs[13]
    copies = [
        pltpu.make_async_copy(source, target, sems.at[i])
        for i, (source, target) in enumerate(zip(given, held))
    ]
    for copy in copies:
        copy.start()
    for copy in copies:
        copy.wait()
    y_low, core_low = (me_ref[0] & 2) == 0, (me_ref[0] & 1) == 0
    for i, ref in enumerate(held[:3]):
        low, high = ref[:, :192], ref[:, 192:]
        keep_ref[0:48, 192 * i : 192 * (i + 1)] = jnp.where(y_low, low, high)
        send_ref[0:48, 192 * i : 192 * (i + 1)] = jnp.where(y_low, high, low)
    keep_ref[48:56, :] = rows_ref[...]
    send_ref[48:56, :] = rows_ref[...]
    for k in range(4):
        even = held[3][:, 384 * k : 384 * k + 192]
        odd = held[3][:, 384 * k + 192 : 384 * (k + 1)]
        in_keep[:, 192 * k : 192 * (k + 1)] = jnp.where(core_low, even, odd)
        in_send[:, 192 * k : 192 * (k + 1)] = jnp.where(core_low, odd, even)


def pack_call(me, weights, rows):
    return pl.pallas_call(
        pack_kernel,
        out_shape=[
            jax.ShapeDtypeStruct(shape, jnp.bfloat16)
            for shape in ((56, 576), (56, 576), (48, 768), (48, 768))
        ],
        in_specs=[
            pl.BlockSpec(memory_space=pltpu.SMEM),
            *[pl.BlockSpec(memory_space=pl.ANY)] * 4,
            pl.BlockSpec(memory_space=pltpu.VMEM),
        ],
        scratch_shapes=[
            *(pltpu.VMEM(weight.shape, jnp.bfloat16) for weight in weights),
            pltpu.SemaphoreType.DMA((4,)),
        ],
        compiler_params=kernel_params,
        cost_estimate=effort(400.0),
    )(me, *weights, rows)


def place_qkv_kernel(me_ref, own_ref, far_ref, mats_ref, wide_ref, heads_ref, hidden_ref, vecs_ref):
    for core, stack in enumerate((own_ref, far_ref)):
        for z in range(4):
            for y in range(2):
                owner = jnp.bitwise_xor(me_ref[0], z * 4 + y * 2 + core)
                mats_ref[owner] = stack[z, y, 0:48]
                vecs_ref[owner] = stack[z, y, 48:56].astype(jnp.float32)
    core_low = (me_ref[0] & 1) == 0
    for i in range(16):
        wide_ref[:, 48 * i : 48 * (i + 1)] = vecs_ref[i, :, 0:48]
    for i in range(8):
        hidden_ref[:, 192 * i : 192 * (i + 1)] = jnp.where(
            core_low, vecs_ref[2 * i, :, 128:320], vecs_ref[2 * i + 1, :, 128:320]
        )
    column = 2 * me_ref[1] + ((me_ref[0] >> 1) & 1)
    for i in range(4):

        @pl.when(column == i)
        def _():
            heads_ref[...] = wide_ref[:, 192 * i : 192 * (i + 1)]


def place_in_kernel(me_ref, one_own, one_far, two_own, two_far, in_ref, out_ref):
    zy_at, x_low = me_ref[0] >> 1, me_ref[1] == 0
    for y, stack in enumerate((two_own, two_far)):
        for z in range(4):
            owner = jnp.bitwise_xor(zy_at, z * 2 + y)
            own, far = one_own[4 * y + z], one_far[4 * y + z]
            low, high = jnp.where(x_low, own, far), jnp.where(x_low, far, own)
            in_ref[owner, :, 0:384], in_ref[owner, :, 768:1152] = low[0:96], high[0:96]
            out_ref[owner, :, 0:384], out_ref[owner, :, 384:768] = low[96:144], high[96:144]
            own, far = stack[0, z], stack[1, z]
            in_ref[owner, :, 384:768] = jnp.where(x_low, own, far)
            in_ref[owner, :, 1152:1536] = jnp.where(x_low, far, own)


def place_down_kernel(me_ref, one_own, one_far, two_own, two_far, down_ref):
    zy_at, x_low = me_ref[0] >> 1, me_ref[1] == 0
    for y, stack in enumerate((two_own, two_far)):
        for z in range(4):
            owner = jnp.bitwise_xor(zy_at, z * 2 + y)
            own, far = one_own[4 * y + z], one_far[4 * y + z]
            down_ref[owner, 0:96, 0:384] = jnp.where(x_low, own, far)
            down_ref[owner, 0:96, 384:768] = jnp.where(x_low, far, own)
            own, far = stack[0, z], stack[1, z]
            down_ref[owner, 96:192, 0:384] = jnp.where(x_low, own, far)
            down_ref[owner, 96:192, 384:768] = jnp.where(x_low, far, own)


def vectors_kernel(me_ref, *refs):
    rows, (query_ref, hidden_ref), moments, out_ref = refs[:7], refs[7:9], refs[9:13], refs[13]
    out_ref[...] = jnp.zeros_like(out_ref)
    core = me_ref[0] & 1
    column = 2 * me_ref[1] + ((me_ref[0] >> 1) & 1)
    totals = [jnp.sum(ref[...], axis=1, keepdims=True) for ref in moments]
    for i in range(16):
        for row, ref in enumerate(rows):
            out_ref[i, row : row + 1, 0:48] = ref[0:1, 48 * i : 48 * (i + 1)]
        part = query_ref[0:1, 48 * (i % 4) : 48 * (i % 4 + 1)]
        out_ref[i, 7:8, 0:48] = jnp.where(column == i // 4, part, 0.0)
        part = hidden_ref[0:1, 192 * (i // 2) : 192 * (i // 2 + 1)]
        out_ref[i, 0:1, 128:320] = jnp.where(core == i % 2, part, 0.0)
        for row, total in enumerate(totals):
            out_ref[i, row + 1 : row + 2, 128:256] = jnp.broadcast_to(total, (1, 128))


def place_call(kernel, me, stacks, shapes, more=(), scratch=(), cost=2.0):
    return pl.pallas_call(
        kernel,
        out_shape=[jax.ShapeDtypeStruct(shape, jnp.bfloat16) for shape in shapes]
        + [jax.ShapeDtypeStruct(shape, jnp.float32) for shape in more],
        scratch_shapes=[pltpu.VMEM(shape, jnp.float32) for shape in scratch],
        in_specs=[pl.BlockSpec(memory_space=pltpu.SMEM)]
        + [pl.BlockSpec(memory_space=pltpu.VMEM)] * len(stacks),
        compiler_params=kernel_params,
        cost_estimate=effort(cost),
    )(me, *stacks)


def fast_body(
    tokens,
    lengths,
    cotangent,
    query_weight,
    key_weight,
    value_weight,
    out_weight,
    in_weight,
    down_weight,
    query_bias,
    value_bias,
    out_bias,
    attn_norm_gain,
    attn_norm_bias,
    in_bias,
    down_bias,
    ffn_norm_gain,
    ffn_norm_bias,
):
    slot_count, width = tokens.shape[1:]
    me = lax.axis_index("ctx")
    x_at = lax.axis_index("fsdp")
    z_at, y_at, core_at = me >> 2, (me >> 1) & 1, me & 1
    y_low, x_low, core_low = y_at == 0, x_at == 0, core_at == 0
    own_long = lengths[0] == slot_count * lax.axis_size("ctx")
    short_flag = (z_at == 0).astype(jnp.int32).reshape(1)

    half = HEAD_COLS
    vector_rows = sum(
        lax.pad(piece[None, :], jnp.asarray(0, jnp.bfloat16), ((row, 7 - row, 0), (at, 576 - at - piece.shape[0], 0)))
        for row, at, piece in (
            (0, 0, query_bias),
            (1, 0, value_bias),
            (2, 0, out_bias),
            (3, 0, attn_norm_gain),
            (4, 0, attn_norm_bias),
            (5, 0, down_bias),
            (6, 0, ffn_norm_gain),
            (7, 0, ffn_norm_bias),
            (0, 128, in_bias),
        )
    )
    where_me = jnp.stack([me, x_at]).astype(jnp.int32)
    keep_cols, send_cols, in_keep, in_send = pack_call(
        where_me, (query_weight, key_weight, value_weight, in_weight), vector_rows
    )
    token_rows = tokens[0]
    in_got = core_swap(in_send)
    in_block = jnp.concatenate(
        [jnp.where(core_low, in_keep, in_got), jnp.where(core_low, in_got, in_keep)], axis=0
    )
    ffn_block = jnp.concatenate([in_block[:, :384], out_weight, in_block[:, 384:], down_weight])
    other_rows = x_swap(token_rows)
    long_own = jnp.where(own_long, token_rows, other_rows)
    short_own = jnp.where(own_long, other_rows, token_rows)
    got_cols, ffn_one, long_own, short_own = hold(
        y_swap(send_cols), ctx_move(ffn_block, 4), long_own, short_own
    )
    own_block = jnp.stack([keep_cols, got_cols])
    ffn_two = ctx_move(ffn_block, 8)
    z_one, z_two, long_far, short_own = hold(
        ctx_move(own_block, 4), ctx_move(own_block, 8), y_swap(long_own), short_own
    )
    z_three, ffn_two = hold(ctx_move(z_two, 4), ffn_two)
    ffn_three = ctx_move(ffn_two, 4)
    z_stack = jnp.stack([own_block, z_one, z_two, z_three])
    qkv_weight, wide, heads, hidden = place_call(
        place_qkv_kernel,
        where_me,
        (z_stack, core_swap(z_stack)),
        ((16, 48, 576),),
        ((8, 768), (8, half), (8, 1536)),
        ((16, 8, 576),),
    )
    qkv_weight = qkv_weight.reshape(768, 576)
    out_vec, gain_one, bias_one, down_vec, gain_two, bias_two = (
        wide[row : row + 1] for row in range(2, 8)
    )
    in_vec = hidden[:1]
    columns = heads.T
    query_add, value_add = columns[:, 0:1], columns[:, 1:2]
    pair_add = jnp.concatenate([jnp.zeros_like(value_add), value_add], axis=0)

    long_rows = jnp.concatenate([long_own, long_far], axis=0)
    def project(rows):
        query = product32(qkv_weight[:, :half], rows, (((0,), (1,)), ((), ()))) + query_add
        pair = product32(qkv_weight[:, half:], rows, (((0,), (1,)), ((), ()))) + pair_add
        scale = jnp.asarray(score_scale, jnp.bfloat16)
        return query.astype(jnp.bfloat16) * scale, pair.astype(jnp.bfloat16)

    long_query, long_pair = project(long_rows)
    kv_two, kv_one = ctx_move(long_pair, 8), ctx_move(long_pair, 4)
    long_pair_far = core_swap(long_pair)
    short_own, long_pair_far = hold(short_own, long_pair_far)
    short_far = y_swap(short_own)
    state = attend_call(long_query, (long_pair, long_pair_far))
    short_rows = jnp.concatenate([short_own, short_far], axis=0)
    short_query, short_pair = project(short_rows)
    short_pairs = (short_pair, core_swap(short_pair))
    short_mixed, short_log = attend_call(short_query, short_pairs, last=True, flag=short_flag)
    ffn_stack = jnp.stack([ffn_block, ffn_one, ffn_two, ffn_three])
    in_one, in_two = ffn_stack[:, :144], ffn_stack[:, 144:240]
    in_one_y, in_two_x = y_swap(in_one), x_swap(in_two)
    kv_one, kv_two, in_one_y, in_two_x, short_mixed, *state = hold(
        kv_one, kv_two, in_one_y, in_two_x, short_mixed, *state
    )
    kv_three = ctx_move(kv_two, 4)
    in_one, in_two = jnp.concatenate([in_one, in_one_y], axis=0), jnp.stack([in_two, in_two_x])
    in_one_far, in_two_far = x_swap(in_one), y_swap(in_two)
    kv_one_far, kv_two_far = core_swap(kv_one), core_swap(kv_two)
    state = attend_call(long_query, (kv_one, kv_one_far), state)
    state = attend_call(long_query, (kv_two, kv_two_far), state)
    kv_three, *state = hold(kv_three, *state)
    kv_three_far = core_swap(kv_three)
    long_mixed, long_log = attend_call(long_query, (kv_three, kv_three_far), state, last=True)
    pairs = (
        (long_pair, long_pair_far),
        (kv_one, kv_one_far),
        (kv_two, kv_two_far),
        (kv_three, kv_three_far),
    )

    rows_here = slot_count
    sent = jnp.concatenate([long_mixed[:, rows_here:], short_mixed[:, rows_here:]], axis=0)
    sent, in_one_far, in_two_far = hold(sent, in_one_far, in_two_far)
    got = y_swap(sent)
    def by_y(mine, theirs):
        return jnp.concatenate(
            [jnp.where(y_low, mine, theirs), jnp.where(y_low, theirs, mine)], axis=0
        )

    long_heads = by_y(long_mixed[:, :rows_here], got[:half])
    short_heads = by_y(short_mixed[:, :rows_here], got[half:])
    own_heads = jnp.where(own_long, long_heads, short_heads)
    sent = jnp.where(own_long, short_heads, long_heads)
    far_heads = x_swap(sent)
    in_all, out_core = place_call(
        place_in_kernel,
        where_me,
        (in_one, in_one_far, in_two, in_two_far),
        ((8, 96, 1536), (8, 48, 768)),
    )
    down_one, down_two = ffn_stack[:, 240:336], ffn_stack[:, 336:]
    down_one, down_two, _ = hold(down_one, down_two, sent)
    down_one_y, down_two_x = hold(y_swap(down_one), x_swap(down_two))
    down_one = jnp.concatenate([down_one, down_one_y], axis=0)
    down_two = jnp.stack([down_two, down_two_x])
    (down_all,) = place_call(
        place_down_kernel,
        where_me,
        (down_one, x_swap(down_one), down_two, y_swap(down_two)),
        ((8, 192, 768),),
    )
    in_all, down_all = in_all.reshape(768, 1536), down_all.reshape(1536, 768)
    out_far = core_swap(out_core)
    out_all = jnp.stack(
        [jnp.where(core_low, out_core, out_far), jnp.where(core_low, out_far, out_core)], axis=1
    ).reshape(768, 768)

    mixed_t = jnp.concatenate(
        [jnp.where(x_low, own_heads, far_heads), jnp.where(x_low, far_heads, own_heads)], axis=0
    )

    local_slots = me * slot_count + jnp.arange(slot_count)
    valid_col = (local_slots < lengths[0]).astype(jnp.float32)[:, None]
    attn_branch = product32(mixed_t, out_all, rows_first) + out_vec
    stream = token_rows.astype(jnp.float32) + attn_branch
    norm_one, norm_one_back = jax.vjp(layer_norm, stream, gain_one, bias_one)
    norm_one_b = norm_one.astype(jnp.bfloat16)
    chip_norm = jnp.concatenate([norm_one_b, core_swap(norm_one_b)], axis=0)
    act_out, gelu_back = jax.vjp(gelu_exact, plain_product(chip_norm, in_all) + in_vec)
    act_b = act_out.astype(jnp.bfloat16)
    ffn_got = core_swap(plain_product(act_b[rows_here:], down_all).astype(jnp.bfloat16))
    ffn_part = plain_product(act_b[:rows_here], down_all)
    ffn_branch = ffn_part + ffn_got.astype(jnp.float32) + down_vec
    stream_two = norm_one + ffn_branch
    final_out, norm_two_back = jax.vjp(layer_norm, stream_two, gain_two, bias_two)
    layer_out = (valid_col * final_out).astype(jnp.bfloat16)[None]
    grad_final = valid_col * cotangent[0].astype(jnp.float32)
    grad_stream_two, grad_gain_two, grad_bias_two = norm_two_back(grad_final)
    grad_ffn_b = grad_stream_two.astype(jnp.bfloat16)
    grad_down_vec = row_sums(grad_ffn_b)
    chip_grad = jnp.concatenate([grad_ffn_b, core_swap(grad_ffn_b)], axis=0)
    grad_inner_b = gelu_back(column_product(chip_grad, down_all))[0].astype(jnp.bfloat16)
    grad_in_vec = row_sums(grad_inner_b)
    norm_got = core_swap(column_product(grad_inner_b[rows_here:], in_all).astype(jnp.bfloat16))
    norm_part = column_product(grad_inner_b[:rows_here], in_all)
    grad_norm_one = grad_stream_two + norm_part + norm_got.astype(jnp.float32)
    grad_stream, grad_gain_one, grad_bias_one = norm_one_back(grad_norm_one)
    grad_attn_b = grad_stream.astype(jnp.bfloat16)
    grad_out_vec = row_sums(grad_attn_b)
    grad_mixed_t = product32(out_all, grad_attn_b, lanes_both).astype(jnp.bfloat16)
    ones = jnp.ones((8, slot_count), jnp.bfloat16)
    grad_value_vec = product32(ones, grad_mixed_t, lanes_both)[:1]

    chip_norm, act_b, grad_inner_b, mixed_w, _ = lax.optimization_barrier(
        (chip_norm, act_b, grad_inner_b, mixed_t, grad_mixed_t)
    )
    inner_send = jnp.where(x_low, grad_inner_b[:, 768:], grad_inner_b[:, :768])
    inner_keep = jnp.where(x_low, grad_inner_b[:, :768], grad_inner_b[:, 768:])
    def with_out(in_part, out_part):
        in_part = in_part.astype(jnp.bfloat16).reshape(4, 2, 96, 768)
        return jnp.concatenate([in_part[..., :384], in_part[..., 384:], out_part], axis=2)

    grad_out = plain_product(mixed_w, grad_attn_b).astype(jnp.bfloat16).reshape(4, 2, 2, 48, 768)
    out_sum = add_b(
        jnp.where(core_low, grad_out[:, :, 0], grad_out[:, :, 1]),
        core_swap(jnp.where(core_low, grad_out[:, :, 1], grad_out[:, :, 0])),
    )
    in_send = with_out(
        row_product(chip_norm, inner_send),
        jnp.where(x_low, out_sum[..., 384:], out_sum[..., :384]),
    )
    in_keep_grad = with_out(
        row_product(chip_norm, inner_keep),
        jnp.where(x_low, out_sum[..., :384], out_sum[..., 384:]),
    )
    grad_down = row_product(act_b, chip_grad).astype(jnp.bfloat16).reshape(4, 2, 192, 768)
    down_send = jnp.where(y_low, grad_down[:, 1], grad_down[:, 0])
    down_keep = jnp.where(y_low, grad_down[:, 0], grad_down[:, 1])
    keep_x = jnp.where(x_low, grad_mixed_t[:384], grad_mixed_t[384:])
    got_x = x_swap(jnp.where(x_low, grad_mixed_t[384:], grad_mixed_t[:384]))
    long_x = jnp.where(own_long, keep_x, got_x)
    short_x = jnp.where(own_long, got_x, keep_x)
    both_keep = jnp.where(y_low, long_x[:half], long_x[half:])
    short_keep = jnp.where(y_low, short_x[:half], short_x[half:])
    sent = jnp.concatenate(
        [
            jnp.where(y_low, long_x[half:], long_x[:half]),
            jnp.where(y_low, short_x[half:], short_x[:half]),
        ],
        axis=0,
    )
    got = y_swap(sent)
    long_grad = jnp.concatenate([both_keep, got[:half]], axis=1)
    short_grad = jnp.concatenate([short_keep, got[half:]], axis=1)
    in_send, down_send, long_grad, _ = hold(in_send, down_send, long_grad, got)
    in_x, down_y = x_swap(in_send), y_swap(down_send)


    grad_query, *grads = attend_back_call(
        long_query, long_grad, long_log, long_mixed, sum(pairs[::-1], ())
    )
    near, far = grads[::2], grads[1::2]
    short_query_b, grad_query = hold(short_query, grad_query)
    short_back = attend_back_call(
        short_query_b,
        short_grad,
        short_log,
        short_mixed,
        short_pairs,
        flag=short_flag,
    )
    *far, grad_query, in_x, down_y, short_query_g, short_near, short_far = hold(
        *(core_swap(part) for part in far), grad_query, in_x, down_y, *short_back
    )
    three, two, one = (add_b(near[i], far[i]) for i in range(3))
    near_own, far_own = near[3], far[3]
    in_sum = add_b(in_keep_grad, in_x)
    down_sum = add_b(down_keep, down_y)
    three_hop, one_got = ctx_move(three, 4), ctx_move(one, 4)
    two_got = ctx_move(add_b(two, three_hop), 8)
    in_send = jnp.where(y_low, in_sum[:, 1], in_sum[:, 0])
    down_send = jnp.where(x_low, down_sum[..., 384:], down_sum[..., :384])
    in_send, down_send, short_far = hold(in_send, down_send, short_far)
    in_y, down_x = y_swap(in_send), x_swap(down_send)
    short_pair_grad = add_b(short_near, core_swap(short_far))
    stream, attn_branch, ffn_branch, in_y = hold(stream, attn_branch, ffn_branch, in_y)
    (
        grad_value_vec,
        grad_out_vec,
        grad_gain_one,
        grad_bias_one,
        grad_down_vec,
        grad_gain_two,
        grad_bias_two,
        grad_in_vec,
        in_y,
    ) = hold(
        grad_value_vec,
        grad_out_vec,
        grad_gain_one,
        grad_bias_one,
        grad_down_vec,
        grad_gain_two,
        grad_bias_two,
        grad_in_vec,
        in_y,
    )
    long_query_grad = (grad_query * score_scale).astype(jnp.bfloat16)
    short_query_grad = (short_query_g * score_scale).astype(jnp.bfloat16)
    ones_wide = jnp.ones((8, 2 * slot_count), jnp.bfloat16)
    query_sums = product32(ones_wide, long_query_grad, lanes_both) + product32(
        ones_wide, short_query_grad, lanes_both
    )
    (owner_sums,) = place_call(
        vectors_kernel,
        where_me,
        (
            grad_value_vec,
            grad_out_vec,
            grad_gain_one,
            grad_bias_one,
            grad_down_vec,
            grad_gain_two,
            grad_bias_two,
            query_sums,
            grad_in_vec,
            jnp.sum(valid_col * stream * stream, axis=0, keepdims=True),
            jnp.sum(valid_col * attn_branch * attn_branch, axis=0, keepdims=True),
            jnp.sum(valid_col * ffn_branch * ffn_branch, axis=0, keepdims=True),
            jnp.broadcast_to(jnp.sum(valid_col, axis=0, keepdims=True) / 128, (1, 128)),
        ),
        (),
        ((16, 8, 384),),
    )
    owner_sums = owner_sums.astype(jnp.bfloat16)
    owner_sums = add_b(owner_sums, x_swap(owner_sums)).reshape(4, 2, 2, 8, 384)
    owner_sums = jnp.pad(owner_sums, ((0, 0), (0, 0), (0, 0), (0, 0), (0, 192)))

    def back_rows(grads):
        return product32(grads, qkv_weight, (((0,), (1,)), ((), ())))

    short_all = jnp.concatenate([short_query_grad, short_pair_grad], axis=0)
    short_rows_back = back_rows(short_all)
    short_got = y_swap(short_rows_back[rows_here:].astype(jnp.bfloat16))
    in_sum = add_b(jnp.where(y_low, in_sum[:, 0], in_sum[:, 1]), in_y)
    down_sum = add_b(jnp.where(x_low, down_sum[..., :384], down_sum[..., 384:]), down_x)
    ffn_sum = jnp.concatenate([in_sum, down_sum], axis=1)
    two_got, one_got, ffn_sum, owner_sums, short_got, short_rows_back = hold(
        two_got, one_got, ffn_sum, owner_sums, short_got, short_rows_back
    )
    long_pair_grad = near_own.astype(jnp.float32)
    for got_part in (far_own, one_got, two_got):
        long_pair_grad = long_pair_grad + got_part.astype(jnp.float32)
    long_pair_grad = long_pair_grad.astype(jnp.bfloat16)
    long_all = jnp.concatenate([long_query_grad, long_pair_grad], axis=0)
    long_back = back_rows(long_all)
    long_back, long_all = hold(long_back, long_all)
    long_got = y_swap(long_back[rows_here:].astype(jnp.bfloat16)).astype(jnp.float32)

    grad_qkv = product32(long_rows, long_all, (((0,), (1,)), ((), ()))) + product32(
        short_rows, short_all, (((0,), (1,)), ((), ()))
    )
    grad_qkv = grad_qkv.astype(jnp.bfloat16).reshape(4, 2, 2, 48, 576)
    grad_qkv = jnp.concatenate([grad_qkv, owner_sums], axis=3)
    core_keep = jnp.where(core_low, grad_qkv[:, :, 0], grad_qkv[:, :, 1])
    core_send = jnp.where(core_low, grad_qkv[:, :, 1], grad_qkv[:, :, 0])
    core_sum = add_b(core_keep, core_swap(core_send))

    def by_z(stack):
        return [
            lax.dynamic_index_in_dim(stack, z_at ^ mask, 0, keepdims=False) for mask in range(4)
        ]

    own_sum, one_part, two_part, three_part = by_z(core_sum)
    one_part, three_part = ctx_move(one_part, 4), ctx_move(three_part, 4)
    two_part, qkv_hop = hold(add_b(two_part, three_part), three_part)
    two_part = ctx_move(two_part, 8)
    own_sum = sum(part.astype(jnp.float32) for part in (own_sum, one_part, two_part))
    y_keep = jnp.where(y_low, own_sum[0], own_sum[1])
    y_got = y_swap(jnp.where(y_low, own_sum[1], own_sum[0]).astype(jnp.bfloat16))
    own_part, one_part, two_part, three_part = by_z(ffn_sum)
    one_part, _ = hold(one_part, qkv_hop)
    one_part = ctx_move(one_part, 4)
    two_part = ctx_move(add_b(two_part, ctx_move(three_part, 4)), 8)
    one_part, two_part, y_got = hold(one_part, two_part, y_got)
    ffn_owned = sum(part.astype(jnp.float32) for part in (own_part, one_part, two_part))
    y_got = y_got.astype(jnp.float32)
    vector_sums = y_keep[48:] + y_got[48:]
    y_keep, y_got = y_keep[:48], y_got[:48]
    low_part, high_part = jnp.where(y_low, y_keep, y_got), jnp.where(y_low, y_got, y_keep)
    owned_qkv = [
        jnp.concatenate(
            [low_part[:, half * i : half * (i + 1)], high_part[:, half * i : half * (i + 1)]],
            axis=1,
        )
        for i in range(3)
    ]

    in_owned = jnp.concatenate([ffn_owned[:96], ffn_owned[96:192]], axis=1)
    in_owned = in_owned.astype(jnp.bfloat16).reshape(2, 48, 768)
    in_mine = jnp.where(core_low, in_owned[0], in_owned[1])
    in_other = core_swap(jnp.where(core_low, in_owned[1], in_owned[0]))
    in_even = jnp.where(core_low, in_mine, in_other).astype(jnp.float32)
    in_odd = jnp.where(core_low, in_other, in_mine).astype(jnp.float32)
    owned_in = jnp.concatenate(
        [
            part[:, 192 * k : 192 * (k + 1)]
            for k in range(4)
            for part in (in_even, in_odd)
        ],
        axis=1,
    )
    owned_out, owned_down = ffn_owned[192:240], ffn_owned[240:]

    short_part = short_rows_back[:rows_here] + short_got.astype(jnp.float32)
    long_part = long_back[:rows_here] + long_got
    own_part = jnp.where(own_long, long_part, short_part)
    far_part = x_swap(jnp.where(own_long, short_part, long_part).astype(jnp.bfloat16))
    tokens_grad = (grad_stream + own_part + far_part.astype(jnp.float32)).astype(jnp.bfloat16)

    def own_piece(row):
        return vector_sums[row, :48]

    rms_values = jnp.sqrt(vector_sums[1:4, 128] / (vector_sums[4, 128] * width))
    return (
        layer_out,
        tokens_grad[None],
        owned_qkv[0],
        owned_qkv[1],
        owned_qkv[2],
        owned_out,
        owned_in,
        owned_down,
        vector_sums[7, :48],
        own_piece(0),
        own_piece(1),
        own_piece(2),
        own_piece(3),
        vector_sums[0, 128:320],
        own_piece(4),
        own_piece(5),
        own_piece(6),
        rms_values,
    )


def layer_body(tokens, *others):
    fits = lax.axis_size("ctx") == 16 and lax.axis_size("fsdp") == 2
    if fits and tokens.shape == (1, 256, 768):
        return fast_body(tokens, *others)
    return body(tokens, *others)


def solution(mesh):
    in_specs = (
        P("fsdp", "ctx", None),
        P("fsdp"),
        P("fsdp", "ctx", None),
        P("ctx", "fsdp"),
        P("ctx", "fsdp"),
        P("ctx", "fsdp"),
        P("ctx", "fsdp"),
        P("ctx", "fsdp"),
        P("ctx", "fsdp"),
        P("ctx"),
        P("ctx"),
        P("ctx"),
        P("ctx"),
        P("ctx"),
        P("ctx"),
        P("ctx"),
        P("ctx"),
        P("ctx"),
    )
    out_specs = (
        P("fsdp", "ctx", None),
        P("fsdp", "ctx", None),
        P("ctx", "fsdp"),
        P("ctx", "fsdp"),
        P("ctx", "fsdp"),
        P("ctx", "fsdp"),
        P("ctx", "fsdp"),
        P("ctx", "fsdp"),
        P("ctx"),
        P("ctx"),
        P("ctx"),
        P("ctx"),
        P("ctx"),
        P("ctx"),
        P("ctx"),
        P("ctx"),
        P("ctx"),
        P(),
    )
    return jax.shard_map(layer_body, mesh=mesh, in_specs=in_specs, out_specs=out_specs, check_vma=False)
```

```python
import functools

import jax
import jax.numpy as jnp
from jax import lax
from jax.experimental import pallas as pl
from jax.experimental.pallas import tpu as pltpu
from jax.sharding import PartitionSpec as P

HEAD_DIM = 64


norm_eps = 1e-12
score_scale = 0.125
masked_score = -1000000000.0
rows_contract = (((0,), (0,)), ((), ()))
columns_contract = (((1,), (1,)), ((), ()))


def layer_norm(stream, gain_vec, shift_vec):
    center = jnp.mean(stream, axis=-1, keepdims=True)
    offset = stream - center
    spread = jnp.mean(offset * offset, axis=-1, keepdims=True)
    return offset * lax.rsqrt(spread + norm_eps) * gain_vec + shift_vec


def gelu_exact(inner_pre):
    return jax.nn.gelu(inner_pre, approximate=False)


def plain_product(left_side, right_side):
    return jnp.dot(left_side, right_side, preferred_element_type=jnp.float32)


def row_product(left_side, right_side):
    return lax.dot_general(left_side, right_side, rows_contract, preferred_element_type=jnp.float32)


def column_product(left_side, right_side):
    return lax.dot_general(
        left_side, right_side, columns_contract, preferred_element_type=jnp.float32
    )


def head_scores(query_head, key_head, key_ok):
    scores = (
        jnp.einsum("sqd,skd->sqk", query_head, key_head, preferred_element_type=jnp.float32)
        * score_scale
    )
    return jnp.where(key_ok[:, None, :], scores, masked_score)


def attend(query_seq, pair_all, key_ok):
    seq_count, slot_count, model_width = query_seq.shape
    heads_count = model_width // HEAD_DIM

    def one_head(head_index, loop_state):
        mixed_out, log_totals = loop_state
        head_start = head_index * HEAD_DIM
        query_head = lax.dynamic_slice_in_dim(query_seq, head_start, HEAD_DIM, 2)
        key_head = lax.dynamic_slice_in_dim(pair_all, head_start, HEAD_DIM, 2)
        value_head = lax.dynamic_slice_in_dim(pair_all, model_width + head_start, HEAD_DIM, 2)
        scores = head_scores(query_head, key_head, key_ok)
        row_peak = jnp.max(scores, axis=-1, keepdims=True)
        row_expo = jnp.exp(scores - row_peak)
        row_total = jnp.sum(row_expo, axis=-1, keepdims=True)
        attn_probs = (row_expo / row_total).astype(jnp.bfloat16)
        head_out = jnp.einsum(
            "sqk,skd->sqd", attn_probs, value_head, preferred_element_type=jnp.float32
        )
        mixed_out = lax.dynamic_update_slice_in_dim(mixed_out, head_out, head_start, 2)
        log_row = row_peak[..., 0] + jnp.log(row_total[..., 0])
        log_totals = lax.dynamic_update_index_in_dim(log_totals, log_row, head_index, 0)
        return (mixed_out, log_totals)

    start_state = (
        jnp.zeros((seq_count, slot_count, model_width), jnp.float32),
        jnp.zeros((heads_count, seq_count, slot_count), jnp.float32),
    )
    return lax.fori_loop(0, heads_count, one_head, start_state)


def attend_back(query_seq, pair_all, key_ok, log_totals, grad_mixed):
    seq_count, slot_count, model_width = query_seq.shape
    heads_count = model_width // HEAD_DIM

    def one_head(head_index, loop_state):
        grad_query, grad_pair = loop_state
        head_start = head_index * HEAD_DIM
        query_head = lax.dynamic_slice_in_dim(query_seq, head_start, HEAD_DIM, 2)
        key_head = lax.dynamic_slice_in_dim(pair_all, head_start, HEAD_DIM, 2)
        value_head = lax.dynamic_slice_in_dim(pair_all, model_width + head_start, HEAD_DIM, 2)
        grad_head = lax.dynamic_slice_in_dim(grad_mixed, head_start, HEAD_DIM, 2)
        scores = head_scores(query_head, key_head, key_ok)
        log_row = lax.dynamic_index_in_dim(log_totals, head_index, 0, keepdims=False)
        attn_probs = jnp.exp(scores - log_row[..., None])
        probs_b = attn_probs.astype(jnp.bfloat16)
        grad_probs = jnp.einsum(
            "sqd,skd->sqk", grad_head, value_head, preferred_element_type=jnp.float32
        )
        row_inner = jnp.sum(attn_probs * grad_probs, axis=-1, keepdims=True)
        grad_scores = (attn_probs * (grad_probs - row_inner)).astype(jnp.bfloat16)
        grad_query_head = (
            jnp.einsum("sqk,skd->sqd", grad_scores, key_head, preferred_element_type=jnp.float32)
            * score_scale
        )
        grad_key_head = (
            jnp.einsum("sqk,sqd->skd", grad_scores, query_head, preferred_element_type=jnp.float32)
            * score_scale
        )
        grad_value_head = jnp.einsum(
            "sqk,sqd->skd", probs_b, grad_head, preferred_element_type=jnp.float32
        )
        grad_query = lax.dynamic_update_slice_in_dim(grad_query, grad_query_head, head_start, 2)
        grad_pair = lax.dynamic_update_slice_in_dim(grad_pair, grad_key_head, head_start, 2)
        grad_pair = lax.dynamic_update_slice_in_dim(
            grad_pair, grad_value_head, model_width + head_start, 2
        )
        return (grad_query, grad_pair)

    start_state = (jnp.zeros(query_seq.shape, jnp.float32), jnp.zeros(pair_all.shape, jnp.float32))
    return lax.fori_loop(0, heads_count, one_head, start_state)


def column_sums(matrix_b):
    return jnp.sum(matrix_b.astype(jnp.float32), axis=0)


def body(
    tokens,
    lengths,
    cotangent,
    query_weight,
    key_weight,
    value_weight,
    out_weight,
    in_weight,
    down_weight,
    query_bias,
    value_bias,
    out_bias,
    attn_norm_gain,
    attn_norm_bias,
    in_bias,
    down_bias,
    ffn_norm_gain,
    ffn_norm_bias,
):
    seq_count, slot_count, model_width = tokens.shape
    row_count = seq_count * slot_count
    ctx_size = lax.axis_size("ctx")
    ctx_index = lax.axis_index("ctx")
    row_parts = (
        lax.all_gather(query_weight, "ctx", axis=0, tiled=True),
        lax.all_gather(key_weight, "ctx", axis=0, tiled=True),
        lax.all_gather(value_weight, "ctx", axis=0, tiled=True),
        lax.all_gather(out_weight, "ctx", axis=0, tiled=True),
        lax.all_gather(in_weight, "ctx", axis=0, tiled=True),
        lax.all_gather(down_weight, "ctx", axis=0, tiled=True),
        lax.all_gather(query_bias, "ctx", axis=0, tiled=True),
        lax.all_gather(value_bias, "ctx", axis=0, tiled=True),
        lax.all_gather(out_bias, "ctx", axis=0, tiled=True),
        lax.all_gather(attn_norm_gain, "ctx", axis=0, tiled=True),
        lax.all_gather(attn_norm_bias, "ctx", axis=0, tiled=True),
        lax.all_gather(in_bias, "ctx", axis=0, tiled=True),
        lax.all_gather(down_bias, "ctx", axis=0, tiled=True),
        lax.all_gather(ffn_norm_gain, "ctx", axis=0, tiled=True),
        lax.all_gather(ffn_norm_bias, "ctx", axis=0, tiled=True),
    )
    full_mats = (
        lax.all_gather(row_parts[0], "fsdp", axis=1, tiled=True),
        lax.all_gather(row_parts[1], "fsdp", axis=1, tiled=True),
        lax.all_gather(row_parts[2], "fsdp", axis=1, tiled=True),
        lax.all_gather(row_parts[3], "fsdp", axis=1, tiled=True),
        lax.all_gather(row_parts[4], "fsdp", axis=1, tiled=True),
        lax.all_gather(row_parts[5], "fsdp", axis=1, tiled=True),
    )
    query_full, key_full, value_full, out_full, in_full, down_full = full_mats
    query_vec = row_parts[6].astype(jnp.float32)
    value_vec = row_parts[7].astype(jnp.float32)
    out_vec = row_parts[8].astype(jnp.float32)
    gain_one = row_parts[9].astype(jnp.float32)
    bias_one = row_parts[10].astype(jnp.float32)
    in_vec = row_parts[11].astype(jnp.float32)
    down_vec = row_parts[12].astype(jnp.float32)
    gain_two = row_parts[13].astype(jnp.float32)
    bias_two = row_parts[14].astype(jnp.float32)
    local_slots = ctx_index * slot_count + jnp.arange(slot_count)
    local_ok = local_slots[None, :] < lengths[:, None]
    valid_mask = local_ok.astype(jnp.float32)
    valid_col = valid_mask.reshape(row_count, 1)
    key_ok = jnp.arange(slot_count * ctx_size)[None, :] < lengths[:, None]
    token_rows = tokens.reshape(row_count, model_width)
    queries_b = (plain_product(token_rows, query_full) + query_vec).astype(jnp.bfloat16)
    keys_b = plain_product(token_rows, key_full).astype(jnp.bfloat16)
    values_b = (plain_product(token_rows, value_full) + value_vec).astype(jnp.bfloat16)
    pair_local = jnp.concatenate([keys_b, values_b], axis=1).reshape(
        seq_count, slot_count, 2 * model_width
    )
    pair_all = lax.all_gather(pair_local, "ctx", axis=1, tiled=True)
    query_seq = queries_b.reshape(seq_count, slot_count, model_width)
    mixed_out, log_totals = attend(query_seq, pair_all, key_ok)
    mixed_b = mixed_out.reshape(row_count, model_width).astype(jnp.bfloat16)
    attn_branch = plain_product(mixed_b, out_full) + out_vec
    stream = token_rows.astype(jnp.float32) + attn_branch
    norm_one, norm_one_back = jax.vjp(layer_norm, stream, gain_one, bias_one)
    norm_one_b = norm_one.astype(jnp.bfloat16)
    inner_pre = plain_product(norm_one_b, in_full) + in_vec
    act_out, gelu_back = jax.vjp(gelu_exact, inner_pre)
    act_b = act_out.astype(jnp.bfloat16)
    ffn_branch = plain_product(act_b, down_full) + down_vec
    stream_two = norm_one + ffn_branch
    final_out, norm_two_back = jax.vjp(layer_norm, stream_two, gain_two, bias_two)
    layer_out = (
        (valid_col * final_out).astype(jnp.bfloat16).reshape(seq_count, slot_count, model_width)
    )
    grad_final = valid_col * cotangent.reshape(row_count, model_width).astype(jnp.float32)
    grad_stream_two, grad_gain_two, grad_bias_two = norm_two_back(grad_final)
    grad_ffn_b = grad_stream_two.astype(jnp.bfloat16)
    grad_down_vec = column_sums(grad_ffn_b)
    grad_down_full = row_product(act_b, grad_ffn_b)
    grad_inner_b = gelu_back(column_product(grad_ffn_b, down_full))[0].astype(jnp.bfloat16)
    grad_in_vec = column_sums(grad_inner_b)
    grad_in_full = row_product(norm_one_b, grad_inner_b)
    grad_norm_one = grad_stream_two + column_product(grad_inner_b, in_full)
    grad_stream, grad_gain_one, grad_bias_one = norm_one_back(grad_norm_one)
    grad_attn_b = grad_stream.astype(jnp.bfloat16)
    grad_out_vec = column_sums(grad_attn_b)
    grad_out_full = row_product(mixed_b, grad_attn_b)
    grad_mixed = (
        column_product(grad_attn_b, out_full)
        .astype(jnp.bfloat16)
        .reshape(seq_count, slot_count, model_width)
    )
    grad_query_seq, grad_pair = attend_back(query_seq, pair_all, key_ok, log_totals, grad_mixed)
    grad_pair_local = lax.psum_scatter(
        grad_pair.astype(jnp.bfloat16), "ctx", scatter_dimension=1, tiled=True
    ).astype(jnp.float32)
    grad_keys_b = (
        grad_pair_local[:, :, :model_width].reshape(row_count, model_width).astype(jnp.bfloat16)
    )
    grad_values_b = (
        grad_pair_local[:, :, model_width:].reshape(row_count, model_width).astype(jnp.bfloat16)
    )
    grad_queries_b = grad_query_seq.reshape(row_count, model_width).astype(jnp.bfloat16)
    grad_query_full = row_product(token_rows, grad_queries_b)
    grad_query_vec = column_sums(grad_queries_b)
    grad_key_full = row_product(token_rows, grad_keys_b)
    grad_value_full = row_product(token_rows, grad_values_b)
    grad_value_vec = column_sums(grad_values_b)
    tokens_grad = (
        (
            grad_stream
            + column_product(grad_queries_b, query_full)
            + column_product(grad_keys_b, key_full)
            + column_product(grad_values_b, value_full)
        )
        .astype(jnp.bfloat16)
        .reshape(seq_count, slot_count, model_width)
    )
    narrow = (
        lax.psum_scatter(
            grad_query_full.astype(jnp.bfloat16), "fsdp", scatter_dimension=1, tiled=True
        ).astype(jnp.float32),
        lax.psum_scatter(
            grad_key_full.astype(jnp.bfloat16), "fsdp", scatter_dimension=1, tiled=True
        ).astype(jnp.float32),
        lax.psum_scatter(
            grad_value_full.astype(jnp.bfloat16), "fsdp", scatter_dimension=1, tiled=True
        ).astype(jnp.float32),
        lax.psum_scatter(
            grad_out_full.astype(jnp.bfloat16), "fsdp", scatter_dimension=1, tiled=True
        ).astype(jnp.float32),
        lax.psum_scatter(
            grad_in_full.astype(jnp.bfloat16), "fsdp", scatter_dimension=1, tiled=True
        ).astype(jnp.float32),
        lax.psum_scatter(
            grad_down_full.astype(jnp.bfloat16), "fsdp", scatter_dimension=1, tiled=True
        ).astype(jnp.float32),
    )
    owned_grads = (
        lax.psum_scatter(
            narrow[0].astype(jnp.bfloat16), "ctx", scatter_dimension=0, tiled=True
        ).astype(jnp.float32),
        lax.psum_scatter(
            narrow[1].astype(jnp.bfloat16), "ctx", scatter_dimension=0, tiled=True
        ).astype(jnp.float32),
        lax.psum_scatter(
            narrow[2].astype(jnp.bfloat16), "ctx", scatter_dimension=0, tiled=True
        ).astype(jnp.float32),
        lax.psum_scatter(
            narrow[3].astype(jnp.bfloat16), "ctx", scatter_dimension=0, tiled=True
        ).astype(jnp.float32),
        lax.psum_scatter(
            narrow[4].astype(jnp.bfloat16), "ctx", scatter_dimension=0, tiled=True
        ).astype(jnp.float32),
        lax.psum_scatter(
            narrow[5].astype(jnp.bfloat16), "ctx", scatter_dimension=0, tiled=True
        ).astype(jnp.float32),
    )
    moments = jnp.stack(
        [
            jnp.sum(valid_col * stream * stream),
            jnp.sum(valid_col * attn_branch * attn_branch),
            jnp.sum(valid_col * ffn_branch * ffn_branch),
            jnp.sum(valid_col),
        ]
    )
    summed = lax.psum(
        (
            moments,
            grad_query_vec,
            grad_value_vec,
            grad_out_vec,
            grad_gain_one,
            grad_bias_one,
            grad_in_vec,
            grad_down_vec,
            grad_gain_two,
            grad_bias_two,
        ),
        ("ctx", "fsdp"),
    )
    width_shard = query_bias.shape[0]
    hidden_shard = in_bias.shape[0]

    def own_piece(vector_full, shard_len):
        return lax.dynamic_slice_in_dim(vector_full, ctx_index * shard_len, shard_len, 0)

    rms_values = jnp.sqrt(summed[0][:3] / (summed[0][3] * model_width))
    return (
        layer_out,
        tokens_grad,
        owned_grads[0],
        owned_grads[1],
        owned_grads[2],
        owned_grads[3],
        owned_grads[4],
        owned_grads[5],
        own_piece(summed[1], width_shard),
        own_piece(summed[2], width_shard),
        own_piece(summed[3], width_shard),
        own_piece(summed[4], width_shard),
        own_piece(summed[5], width_shard),
        own_piece(summed[6], hidden_shard),
        own_piece(summed[7], width_shard),
        own_piece(summed[8], width_shard),
        own_piece(summed[9], width_shard),
        rms_values,
    )


HEADS_HERE = 3
HEAD_COLS = HEADS_HERE * HEAD_DIM
rows_first = (((0,), (0,)), ((), ()))
lanes_both = (((1,), (1,)), ((), ()))
plain_contract = (((1,), (0,)), ((), ()))


def effort(microseconds):
    return pl.CostEstimate(
        flops=int(microseconds * 1e8), transcendentals=0, bytes_accessed=int(microseconds * 1e5)
    )


kernel_params = pltpu.CompilerParams(vmem_limit_bytes=24 * 1024 * 1024)


def product32(left_side, right_side, contract):
    return lax.dot_general(left_side, right_side, contract, preferred_element_type=jnp.float32)


def ctx_move(value, mask):
    return lax.ppermute(value, "ctx", [(i, i ^ mask) for i in range(16)])


def core_swap(value):
    return ctx_move(value, 1)


def y_swap(value):
    return ctx_move(value, 2)


def x_swap(value):
    return lax.ppermute(value, "fsdp", [(0, 1), (1, 0)])


def add_b(left_side, right_side):
    return (left_side.astype(jnp.float32) + right_side.astype(jnp.float32)).astype(jnp.bfloat16)


def row_sums(matrix_b):
    return jnp.sum(matrix_b.astype(jnp.float32), axis=0, keepdims=True)


def hold(*values):
    return lax.optimization_barrier(values)


def when_flag(flag_ref, run, idle):
    if flag_ref is None:
        run()
    else:
        pl.when(flag_ref[0] > 0)(run)
        pl.when(flag_ref[0] <= 0)(idle)


def attend_kernel(count, first, last, flagged, *refs):
    flag_ref = refs[0] if flagged else None
    refs = refs[flagged:]
    query_ref, pairs = refs[0], refs[1 : 1 + count]
    refs = refs[1 + count :]
    if not first:
        peak_in, total_in, mixed_in = refs[:3]
        refs = refs[3:]

    def one_head(head, carry):
        key_rows = pl.ds(pl.multiple_of(head * HEAD_DIM, HEAD_DIM), HEAD_DIM)
        value_rows = pl.ds(pl.multiple_of(HEAD_COLS + head * HEAD_DIM, HEAD_DIM), HEAD_DIM)
        query = query_ref[key_rows, :]
        width = query.shape[1]
        if first:
            peak = jnp.full((1, width), -1e30, jnp.float32)
            total = jnp.zeros((1, width), jnp.float32)
            mixed = jnp.zeros((HEAD_DIM, width), jnp.float32)
        else:
            peak, total, mixed = peak_in[head][0:1], total_in[head][0:1], mixed_in[key_rows, :]
        for pair in pairs:
            scores = product32(pair[key_rows, :], query, rows_first)
            new_peak = jnp.maximum(peak, jnp.max(scores, axis=0, keepdims=True))
            expo = jnp.exp(scores - new_peak)
            shrink = jnp.exp(peak - new_peak)
            total = total * shrink + jnp.sum(expo, axis=0, keepdims=True)
            mixed = mixed * shrink + product32(
                pair[value_rows, :], expo.astype(jnp.bfloat16), plain_contract
            )
            peak = new_peak
        if last:
            mixed_out, log_out = refs
            mixed_out[key_rows, :] = (mixed / total).astype(jnp.bfloat16)
            log_out[head] = jnp.broadcast_to(peak + jnp.log(total), (8, width))
        else:
            peak_out, total_out, sum_out = refs
            peak_out[head] = jnp.broadcast_to(peak, (8, width))
            total_out[head] = jnp.broadcast_to(total, (8, width))
            sum_out[key_rows, :] = mixed
        return carry

    def run():
        lax.fori_loop(0, HEADS_HERE, one_head, 0)

    def idle():
        for ref in refs:
            ref[...] = jnp.zeros_like(ref)

    when_flag(flag_ref, run, idle)


def attend_call(query, pairs, state=None, last=False, flag=None):
    width = query.shape[1]
    stat = jax.ShapeDtypeStruct((HEADS_HERE, 8, width), jnp.float32)
    if last:
        outs = [jax.ShapeDtypeStruct((HEAD_COLS, width), jnp.bfloat16), stat]
    else:
        outs = [stat, stat, jax.ShapeDtypeStruct((HEAD_COLS, width), jnp.float32)]
    ins = [query, *pairs, *(() if state is None else state)]
    specs = [pl.BlockSpec(memory_space=pltpu.VMEM)] * len(ins)
    if flag is not None:
        ins, specs = [flag, *ins], [pl.BlockSpec(memory_space=pltpu.SMEM), *specs]
    return pl.pallas_call(
        functools.partial(attend_kernel, len(pairs), state is None, last, int(flag is not None)),
        out_shape=outs,
        in_specs=specs,
        compiler_params=kernel_params,
        cost_estimate=effort(3.5),
    )(*ins)


def attend_back_kernel(count, first, flagged, *refs):
    flag_ref = refs[0] if flagged else None
    refs = refs[flagged:]
    query_ref, grad_ref, log_ref, mixed_ref = refs[:4]
    pairs = refs[4 : 4 + count]
    refs = refs[4 + count :]
    if not first:
        grad_query_in, refs = refs[0], refs[1:]
    grad_query_out, grad_pairs = refs[0], refs[1 : 1 + count]
    held, sems = refs[1 + count :]
    hbm_pairs, pairs = pairs, [held.at[i] for i in range(count)]

    def one_head(head, carry):
        key_rows = pl.ds(pl.multiple_of(head * HEAD_DIM, HEAD_DIM), HEAD_DIM)
        value_rows = pl.ds(pl.multiple_of(HEAD_COLS + head * HEAD_DIM, HEAD_DIM), HEAD_DIM)
        query, grad = query_ref[key_rows, :], grad_ref[key_rows, :]
        log_row = log_ref[head][0:1]
        inner = jnp.sum(
            mixed_ref[key_rows, :].astype(jnp.float32) * grad.astype(jnp.float32),
            axis=0,
            keepdims=True,
        )
        if first:
            grad_query = jnp.zeros((HEAD_DIM, query.shape[1]), jnp.float32)
        else:
            grad_query = grad_query_in[key_rows, :]
        for pair, grad_pair in zip(pairs, grad_pairs):
            keys = pair[key_rows, :]
            probs = jnp.exp(product32(keys, query, rows_first) - log_row)
            grad_probs = product32(pair[value_rows, :], grad, rows_first)
            grad_scores = (probs * (grad_probs - inner)).astype(jnp.bfloat16)
            grad_query = grad_query + product32(keys, grad_scores, plain_contract)
            grad_pair[key_rows, :] = product32(query, grad_scores, lanes_both).astype(jnp.bfloat16)
            grad_pair[value_rows, :] = product32(
                grad, probs.astype(jnp.bfloat16), lanes_both
            ).astype(jnp.bfloat16)
        grad_query_out[key_rows, :] = grad_query
        return carry

    def run():
        copies = [
            pltpu.make_async_copy(hbm, held.at[i], sems.at[i]) for i, hbm in enumerate(hbm_pairs)
        ]
        for copy in copies:
            copy.start()
        for copy in copies:
            copy.wait()
        lax.fori_loop(0, HEADS_HERE, one_head, 0)

    def idle():
        for ref in (grad_query_out, *grad_pairs):
            ref[...] = jnp.zeros_like(ref)

    when_flag(flag_ref, run, idle)


def attend_back_call(query, grad, log_rows, mixed, pairs, grad_query=None, flag=None):
    outs = [jax.ShapeDtypeStruct(query.shape, jnp.float32)]
    outs += [jax.ShapeDtypeStruct(pair.shape, jnp.bfloat16) for pair in pairs]
    ins = [query, grad, log_rows, mixed, *pairs, *(() if grad_query is None else (grad_query,))]
    specs = [pl.BlockSpec(memory_space=pltpu.VMEM)] * len(ins)
    specs[4 : 4 + len(pairs)] = [pl.BlockSpec(memory_space=pl.ANY)] * len(pairs)
    if flag is not None:
        ins, specs = [flag, *ins], [pl.BlockSpec(memory_space=pltpu.SMEM), *specs]
    return pl.pallas_call(
        functools.partial(
            attend_back_kernel, len(pairs), grad_query is None, int(flag is not None)
        ),
        out_shape=outs,
        in_specs=specs,
        scratch_shapes=[
            pltpu.VMEM((len(pairs), *pairs[0].shape), jnp.bfloat16),
            pltpu.SemaphoreType.DMA((len(pairs),)),
        ],
        compiler_params=kernel_params,
        cost_estimate=effort(10.0),
    )(*ins)


def pack_kernel(me_ref, *refs):
    given, (rows_ref, keep_ref, send_ref, in_keep, in_send) = refs[:4], refs[4:9]
    held, sems = refs[9:13], refs[13]
    copies = [
        pltpu.make_async_copy(source, target, sems.at[i])
        for i, (source, target) in enumerate(zip(given, held))
    ]
    for copy in copies:
        copy.start()
    for copy in copies:
        copy.wait()
    y_low, core_low = (me_ref[0] & 2) == 0, (me_ref[0] & 1) == 0
    for i, ref in enumerate(held[:3]):
        low, high = ref[:, :192], ref[:, 192:]
        keep_ref[0:48, 192 * i : 192 * (i + 1)] = jnp.where(y_low, low, high)
        send_ref[0:48, 192 * i : 192 * (i + 1)] = jnp.where(y_low, high, low)
    keep_ref[48:56, :] = rows_ref[...]
    send_ref[48:56, :] = rows_ref[...]
    for k in range(4):
        even = held[3][:, 384 * k : 384 * k + 192]
        odd = held[3][:, 384 * k + 192 : 384 * (k + 1)]
        in_keep[:, 192 * k : 192 * (k + 1)] = jnp.where(core_low, even, odd)
        in_send[:, 192 * k : 192 * (k + 1)] = jnp.where(core_low, odd, even)


def pack_call(me, weights, rows):
    return pl.pallas_call(
        pack_kernel,
        out_shape=[
            jax.ShapeDtypeStruct(shape, jnp.bfloat16)
            for shape in ((56, 576), (56, 576), (48, 768), (48, 768))
        ],
        in_specs=[
            pl.BlockSpec(memory_space=pltpu.SMEM),
            *[pl.BlockSpec(memory_space=pl.ANY)] * 4,
            pl.BlockSpec(memory_space=pltpu.VMEM),
        ],
        scratch_shapes=[
            *(pltpu.VMEM(weight.shape, jnp.bfloat16) for weight in weights),
            pltpu.SemaphoreType.DMA((4,)),
        ],
        compiler_params=kernel_params,
        cost_estimate=effort(400.0),
    )(me, *weights, rows)


def place_qkv_kernel(me_ref, own_ref, far_ref, mats_ref, wide_ref, heads_ref, hidden_ref, vecs_ref):
    for core, stack in enumerate((own_ref, far_ref)):
        for z in range(4):
            for y in range(2):
                owner = jnp.bitwise_xor(me_ref[0], z * 4 + y * 2 + core)
                mats_ref[owner] = stack[z, y, 0:48]
                vecs_ref[owner] = stack[z, y, 48:56].astype(jnp.float32)
    core_low = (me_ref[0] & 1) == 0
    for i in range(16):
        wide_ref[:, 48 * i : 48 * (i + 1)] = vecs_ref[i, :, 0:48]
    for i in range(8):
        hidden_ref[:, 192 * i : 192 * (i + 1)] = jnp.where(
            core_low, vecs_ref[2 * i, :, 128:320], vecs_ref[2 * i + 1, :, 128:320]
        )
    column = 2 * me_ref[1] + ((me_ref[0] >> 1) & 1)
    for i in range(4):

        @pl.when(column == i)
        def _():
            heads_ref[...] = wide_ref[:, 192 * i : 192 * (i + 1)]


def place_in_kernel(me_ref, one_own, one_far, two_own, two_far, in_ref, out_ref):
    zy_at, x_low = me_ref[0] >> 1, me_ref[1] == 0
    for y, stack in enumerate((two_own, two_far)):
        for z in range(4):
            owner = jnp.bitwise_xor(zy_at, z * 2 + y)
            own, far = one_own[4 * y + z], one_far[4 * y + z]
            low, high = jnp.where(x_low, own, far), jnp.where(x_low, far, own)
            in_ref[owner, :, 0:384], in_ref[owner, :, 768:1152] = low[0:96], high[0:96]
            out_ref[owner, :, 0:384], out_ref[owner, :, 384:768] = low[96:144], high[96:144]
            own, far = stack[0, z], stack[1, z]
            in_ref[owner, :, 384:768] = jnp.where(x_low, own, far)
            in_ref[owner, :, 1152:1536] = jnp.where(x_low, far, own)


def place_down_kernel(me_ref, one_own, one_far, two_own, two_far, down_ref):
    zy_at, x_low = me_ref[0] >> 1, me_ref[1] == 0
    for y, stack in enumerate((two_own, two_far)):
        for z in range(4):
            owner = jnp.bitwise_xor(zy_at, z * 2 + y)
            own, far = one_own[4 * y + z], one_far[4 * y + z]
            down_ref[owner, 0:96, 0:384] = jnp.where(x_low, own, far)
            down_ref[owner, 0:96, 384:768] = jnp.where(x_low, far, own)
            own, far = stack[0, z], stack[1, z]
            down_ref[owner, 96:192, 0:384] = jnp.where(x_low, own, far)
            down_ref[owner, 96:192, 384:768] = jnp.where(x_low, far, own)


def vectors_kernel(me_ref, *refs):
    rows, (query_ref, hidden_ref), moments, out_ref = refs[:7], refs[7:9], refs[9:13], refs[13]
    out_ref[...] = jnp.zeros_like(out_ref)
    core = me_ref[0] & 1
    column = 2 * me_ref[1] + ((me_ref[0] >> 1) & 1)
    totals = [jnp.sum(ref[...], axis=1, keepdims=True) for ref in moments]
    for i in range(16):
        for row, ref in enumerate(rows):
            out_ref[i, row : row + 1, 0:48] = ref[0:1, 48 * i : 48 * (i + 1)]
        part = query_ref[0:1, 48 * (i % 4) : 48 * (i % 4 + 1)]
        out_ref[i, 7:8, 0:48] = jnp.where(column == i // 4, part, 0.0)
        part = hidden_ref[0:1, 192 * (i // 2) : 192 * (i // 2 + 1)]
        out_ref[i, 0:1, 128:320] = jnp.where(core == i % 2, part, 0.0)
        for row, total in enumerate(totals):
            out_ref[i, row + 1 : row + 2, 128:256] = jnp.broadcast_to(total, (1, 128))


def place_call(kernel, me, stacks, shapes, more=(), scratch=(), cost=2.0):
    return pl.pallas_call(
        kernel,
        out_shape=[jax.ShapeDtypeStruct(shape, jnp.bfloat16) for shape in shapes]
        + [jax.ShapeDtypeStruct(shape, jnp.float32) for shape in more],
        scratch_shapes=[pltpu.VMEM(shape, jnp.float32) for shape in scratch],
        in_specs=[pl.BlockSpec(memory_space=pltpu.SMEM)]
        + [pl.BlockSpec(memory_space=pltpu.VMEM)] * len(stacks),
        compiler_params=kernel_params,
        cost_estimate=effort(cost),
    )(me, *stacks)


def fast_body(
    tokens,
    lengths,
    cotangent,
    query_weight,
    key_weight,
    value_weight,
    out_weight,
    in_weight,
    down_weight,
    query_bias,
    value_bias,
    out_bias,
    attn_norm_gain,
    attn_norm_bias,
    in_bias,
    down_bias,
    ffn_norm_gain,
    ffn_norm_bias,
):
    slot_count, width = tokens.shape[1:]
    me = lax.axis_index("ctx")
    x_at = lax.axis_index("fsdp")
    z_at, y_at, core_at = me >> 2, (me >> 1) & 1, me & 1
    y_low, x_low, core_low = y_at == 0, x_at == 0, core_at == 0
    own_long = lengths[0] == slot_count * lax.axis_size("ctx")
    short_flag = (z_at == 0).astype(jnp.int32).reshape(1)

    half = HEAD_COLS
    vector_rows = sum(
        lax.pad(piece[None, :], jnp.asarray(0, jnp.bfloat16), ((row, 7 - row, 0), (at, 576 - at - piece.shape[0], 0)))
        for row, at, piece in (
            (0, 0, query_bias),
            (1, 0, value_bias),
            (2, 0, out_bias),
            (3, 0, attn_norm_gain),
            (4, 0, attn_norm_bias),
            (5, 0, down_bias),
            (6, 0, ffn_norm_gain),
            (7, 0, ffn_norm_bias),
            (0, 128, in_bias),
        )
    )
    where_me = jnp.stack([me, x_at]).astype(jnp.int32)
    keep_cols, send_cols, in_keep, in_send = pack_call(
        where_me, (query_weight, key_weight, value_weight, in_weight), vector_rows
    )
    token_rows = tokens[0]
    in_got = core_swap(in_send)
    in_block = jnp.concatenate(
        [jnp.where(core_low, in_keep, in_got), jnp.where(core_low, in_got, in_keep)], axis=0
    )
    ffn_block = jnp.concatenate([in_block[:, :384], out_weight, in_block[:, 384:], down_weight])
    other_rows = x_swap(token_rows)
    long_own = jnp.where(own_long, token_rows, other_rows)
    short_own = jnp.where(own_long, other_rows, token_rows)
    got_cols, ffn_one, long_own, short_own = hold(
        y_swap(send_cols), ctx_move(ffn_block, 4), long_own, short_own
    )
    own_block = jnp.stack([keep_cols, got_cols])
    ffn_two = ctx_move(ffn_block, 8)
    z_one, z_two, long_far, short_own = hold(
        ctx_move(own_block, 4), ctx_move(own_block, 8), y_swap(long_own), short_own
    )
    z_three, ffn_two = hold(ctx_move(z_two, 4), ffn_two)
    ffn_three = ctx_move(ffn_two, 4)
    z_stack = jnp.stack([own_block, z_one, z_two, z_three])
    qkv_weight, wide, heads, hidden = place_call(
        place_qkv_kernel,
        where_me,
        (z_stack, core_swap(z_stack)),
        ((16, 48, 576),),
        ((8, 768), (8, half), (8, 1536)),
        ((16, 8, 576),),
    )
    qkv_weight = qkv_weight.reshape(768, 576)
    out_vec, gain_one, bias_one, down_vec, gain_two, bias_two = (
        wide[row : row + 1] for row in range(2, 8)
    )
    in_vec = hidden[:1]
    columns = heads.T
    query_add, value_add = columns[:, 0:1], columns[:, 1:2]
    pair_add = jnp.concatenate([jnp.zeros_like(value_add), value_add], axis=0)

    long_rows = jnp.concatenate([long_own, long_far], axis=0)
    def project(rows):
        query = product32(qkv_weight[:, :half], rows, (((0,), (1,)), ((), ()))) + query_add
        pair = product32(qkv_weight[:, half:], rows, (((0,), (1,)), ((), ()))) + pair_add
        scale = jnp.asarray(score_scale, jnp.bfloat16)
        return query.astype(jnp.bfloat16) * scale, pair.astype(jnp.bfloat16)

    long_query, long_pair = project(long_rows)
    short_own, _ = hold(short_own, z_three)
    short_far = y_swap(short_own)
    long_pair, ffn_three, short_far = hold(long_pair, ffn_three, short_far)
    kv_two, kv_one = ctx_move(long_pair, 8), ctx_move(long_pair, 4)
    long_pair_far = core_swap(long_pair)
    state = attend_call(long_query, (long_pair, long_pair_far))
    short_rows = jnp.concatenate([short_own, short_far], axis=0)
    short_query, short_pair = project(short_rows)
    short_pairs = (short_pair, core_swap(short_pair))
    short_mixed, short_log = attend_call(short_query, short_pairs, last=True, flag=short_flag)
    ffn_stack = jnp.stack([ffn_block, ffn_one, ffn_two, ffn_three])
    in_one, in_two = ffn_stack[:, :144], ffn_stack[:, 144:240]
    in_one_y, in_two_x = y_swap(in_one), x_swap(in_two)
    kv_one, kv_two, in_one_y, in_two_x, short_mixed, *state = hold(
        kv_one, kv_two, in_one_y, in_two_x, short_mixed, *state
    )
    kv_three = ctx_move(kv_two, 4)
    in_one, in_two = jnp.concatenate([in_one, in_one_y], axis=0), jnp.stack([in_two, in_two_x])
    in_one_far, in_two_far = x_swap(in_one), y_swap(in_two)
    kv_one_far, kv_two_far = core_swap(kv_one), core_swap(kv_two)
    state = attend_call(long_query, (kv_one, kv_one_far), state)
    state = attend_call(long_query, (kv_two, kv_two_far), state)
    kv_three, *state = hold(kv_three, *state)
    kv_three_far = core_swap(kv_three)
    long_mixed, long_log = attend_call(long_query, (kv_three, kv_three_far), state, last=True)
    pairs = (
        (long_pair, long_pair_far),
        (kv_one, kv_one_far),
        (kv_two, kv_two_far),
        (kv_three, kv_three_far),
    )

    rows_here = slot_count
    sent = jnp.concatenate([long_mixed[:, rows_here:], short_mixed[:, rows_here:]], axis=0)
    sent, in_one_far, in_two_far = hold(sent, in_one_far, in_two_far)
    got = y_swap(sent)
    def by_y(mine, theirs):
        return jnp.concatenate(
            [jnp.where(y_low, mine, theirs), jnp.where(y_low, theirs, mine)], axis=0
        )

    long_heads = by_y(long_mixed[:, :rows_here], got[:half])
    short_heads = by_y(short_mixed[:, :rows_here], got[half:])
    own_heads = jnp.where(own_long, long_heads, short_heads)
    sent = jnp.where(own_long, short_heads, long_heads)
    far_heads = x_swap(sent)
    in_all, out_core = place_call(
        place_in_kernel,
        where_me,
        (in_one, in_one_far, in_two, in_two_far),
        ((8, 96, 1536), (8, 48, 768)),
    )
    down_one, down_two = ffn_stack[:, 240:336], ffn_stack[:, 336:]
    down_one, down_two, _ = hold(down_one, down_two, sent)
    down_one_y, down_two_x = hold(y_swap(down_one), x_swap(down_two))
    down_one = jnp.concatenate([down_one, down_one_y], axis=0)
    down_two = jnp.stack([down_two, down_two_x])
    (down_all,) = place_call(
        place_down_kernel,
        where_me,
        (down_one, x_swap(down_one), down_two, y_swap(down_two)),
        ((8, 192, 768),),
    )
    in_all, down_all = in_all.reshape(768, 1536), down_all.reshape(1536, 768)
    out_far = core_swap(out_core)
    out_all = jnp.stack(
        [jnp.where(core_low, out_core, out_far), jnp.where(core_low, out_far, out_core)], axis=1
    ).reshape(768, 768)

    mixed_t = jnp.concatenate(
        [jnp.where(x_low, own_heads, far_heads), jnp.where(x_low, far_heads, own_heads)], axis=0
    )

    local_slots = me * slot_count + jnp.arange(slot_count)
    valid_col = (local_slots < lengths[0]).astype(jnp.float32)[:, None]
    attn_branch = product32(mixed_t, out_all, rows_first) + out_vec
    stream = token_rows.astype(jnp.float32) + attn_branch
    norm_one, norm_one_back = jax.vjp(layer_norm, stream, gain_one, bias_one)
    norm_one_b = norm_one.astype(jnp.bfloat16)
    chip_norm = jnp.concatenate([norm_one_b, core_swap(norm_one_b)], axis=0)
    act_out, gelu_back = jax.vjp(gelu_exact, plain_product(chip_norm, in_all) + in_vec)
    act_b = act_out.astype(jnp.bfloat16)
    ffn_got = core_swap(plain_product(act_b[rows_here:], down_all).astype(jnp.bfloat16))
    ffn_part = plain_product(act_b[:rows_here], down_all)
    ffn_branch = ffn_part + ffn_got.astype(jnp.float32) + down_vec
    stream_two = norm_one + ffn_branch
    final_out, norm_two_back = jax.vjp(layer_norm, stream_two, gain_two, bias_two)
    layer_out = (valid_col * final_out).astype(jnp.bfloat16)[None]
    grad_final = valid_col * cotangent[0].astype(jnp.float32)
    grad_stream_two, grad_gain_two, grad_bias_two = norm_two_back(grad_final)
    grad_ffn_b = grad_stream_two.astype(jnp.bfloat16)
    grad_down_vec = row_sums(grad_ffn_b)
    chip_grad = jnp.concatenate([grad_ffn_b, core_swap(grad_ffn_b)], axis=0)
    grad_inner_b = gelu_back(column_product(chip_grad, down_all))[0].astype(jnp.bfloat16)
    grad_in_vec = row_sums(grad_inner_b)
    norm_got = core_swap(column_product(grad_inner_b[rows_here:], in_all).astype(jnp.bfloat16))
    norm_part = column_product(grad_inner_b[:rows_here], in_all)
    grad_norm_one = grad_stream_two + norm_part + norm_got.astype(jnp.float32)
    grad_stream, grad_gain_one, grad_bias_one = norm_one_back(grad_norm_one)
    grad_attn_b = grad_stream.astype(jnp.bfloat16)
    grad_out_vec = row_sums(grad_attn_b)
    grad_mixed_t = product32(out_all, grad_attn_b, lanes_both).astype(jnp.bfloat16)
    ones = jnp.ones((8, slot_count), jnp.bfloat16)
    grad_value_vec = product32(ones, grad_mixed_t, lanes_both)[:1]

    chip_norm, act_b, grad_inner_b, mixed_w, _ = lax.optimization_barrier(
        (chip_norm, act_b, grad_inner_b, mixed_t, grad_mixed_t)
    )
    inner_send = jnp.where(x_low, grad_inner_b[:, 768:], grad_inner_b[:, :768])
    inner_keep = jnp.where(x_low, grad_inner_b[:, :768], grad_inner_b[:, 768:])
    def with_out(in_part, out_part):
        in_part = in_part.astype(jnp.bfloat16).reshape(4, 2, 96, 768)
        return jnp.concatenate([in_part[..., :384], in_part[..., 384:], out_part], axis=2)

    grad_out = plain_product(mixed_w, grad_attn_b).astype(jnp.bfloat16).reshape(4, 2, 2, 48, 768)
    out_sum = add_b(
        jnp.where(core_low, grad_out[:, :, 0], grad_out[:, :, 1]),
        core_swap(jnp.where(core_low, grad_out[:, :, 1], grad_out[:, :, 0])),
    )
    in_send = with_out(
        row_product(chip_norm, inner_send),
        jnp.where(x_low, out_sum[..., 384:], out_sum[..., :384]),
    )
    in_keep_grad = with_out(
        row_product(chip_norm, inner_keep),
        jnp.where(x_low, out_sum[..., :384], out_sum[..., 384:]),
    )
    grad_down = row_product(act_b, chip_grad).astype(jnp.bfloat16).reshape(4, 2, 192, 768)
    down_send = jnp.where(y_low, grad_down[:, 1], grad_down[:, 0])
    down_keep = jnp.where(y_low, grad_down[:, 0], grad_down[:, 1])
    keep_x = jnp.where(x_low, grad_mixed_t[:384], grad_mixed_t[384:])
    got_x = x_swap(jnp.where(x_low, grad_mixed_t[384:], grad_mixed_t[:384]))
    long_x = jnp.where(own_long, keep_x, got_x)
    short_x = jnp.where(own_long, got_x, keep_x)
    both_keep = jnp.where(y_low, long_x[:half], long_x[half:])
    short_keep = jnp.where(y_low, short_x[:half], short_x[half:])
    sent = jnp.concatenate(
        [
            jnp.where(y_low, long_x[half:], long_x[:half]),
            jnp.where(y_low, short_x[half:], short_x[:half]),
        ],
        axis=0,
    )
    got = y_swap(sent)
    long_grad = jnp.concatenate([both_keep, got[:half]], axis=1)
    short_grad = jnp.concatenate([short_keep, got[half:]], axis=1)
    in_send, down_send, long_grad, _ = hold(in_send, down_send, long_grad, got)
    in_x, down_y = x_swap(in_send), y_swap(down_send)


    grad_query, *grads = attend_back_call(
        long_query, long_grad, long_log, long_mixed, sum(pairs[::-1], ())
    )
    near, far = grads[::2], grads[1::2]
    short_query_b, grad_query = hold(short_query, grad_query)
    short_back = attend_back_call(
        short_query_b,
        short_grad,
        short_log,
        short_mixed,
        short_pairs,
        flag=short_flag,
    )
    *far, grad_query, in_x, down_y, short_query_g, short_near, short_far = hold(
        *(core_swap(part) for part in far), grad_query, in_x, down_y, *short_back
    )
    three, two, one = (add_b(near[i], far[i]) for i in range(3))
    near_own, far_own = near[3], far[3]
    in_sum = add_b(in_keep_grad, in_x)
    down_sum = add_b(down_keep, down_y)
    three_hop, one_got = ctx_move(three, 4), ctx_move(one, 4)
    two_got = ctx_move(add_b(two, three_hop), 8)
    in_send = jnp.where(y_low, in_sum[:, 1], in_sum[:, 0])
    down_send = jnp.where(x_low, down_sum[..., 384:], down_sum[..., :384])
    in_send, down_send, short_far = hold(in_send, down_send, short_far)
    in_y, down_x = y_swap(in_send), x_swap(down_send)
    short_pair_grad = add_b(short_near, core_swap(short_far))
    stream, attn_branch, ffn_branch, in_y = hold(stream, attn_branch, ffn_branch, in_y)
    (
        grad_value_vec,
        grad_out_vec,
        grad_gain_one,
        grad_bias_one,
        grad_down_vec,
        grad_gain_two,
        grad_bias_two,
        grad_in_vec,
        in_y,
    ) = hold(
        grad_value_vec,
        grad_out_vec,
        grad_gain_one,
        grad_bias_one,
        grad_down_vec,
        grad_gain_two,
        grad_bias_two,
        grad_in_vec,
        in_y,
    )
    long_query_grad = (grad_query * score_scale).astype(jnp.bfloat16)
    short_query_grad = (short_query_g * score_scale).astype(jnp.bfloat16)
    ones_wide = jnp.ones((8, 2 * slot_count), jnp.bfloat16)
    query_sums = product32(ones_wide, long_query_grad, lanes_both) + product32(
        ones_wide, short_query_grad, lanes_both
    )
    (owner_sums,) = place_call(
        vectors_kernel,
        where_me,
        (
            grad_value_vec,
            grad_out_vec,
            grad_gain_one,
            grad_bias_one,
            grad_down_vec,
            grad_gain_two,
            grad_bias_two,
            query_sums,
            grad_in_vec,
            jnp.sum(valid_col * stream * stream, axis=0, keepdims=True),
            jnp.sum(valid_col * attn_branch * attn_branch, axis=0, keepdims=True),
            jnp.sum(valid_col * ffn_branch * ffn_branch, axis=0, keepdims=True),
            jnp.broadcast_to(jnp.sum(valid_col, axis=0, keepdims=True) / 128, (1, 128)),
        ),
        (),
        ((16, 8, 384),),
    )
    owner_sums = owner_sums.astype(jnp.bfloat16)
    owner_sums = add_b(owner_sums, x_swap(owner_sums)).reshape(4, 2, 2, 8, 384)
    owner_sums = jnp.pad(owner_sums, ((0, 0), (0, 0), (0, 0), (0, 0), (0, 192)))

    def back_rows(grads):
        return product32(grads, qkv_weight, (((0,), (1,)), ((), ())))

    short_all = jnp.concatenate([short_query_grad, short_pair_grad], axis=0)
    short_rows_back = back_rows(short_all)
    short_got = y_swap(short_rows_back[rows_here:].astype(jnp.bfloat16))
    in_sum = add_b(jnp.where(y_low, in_sum[:, 0], in_sum[:, 1]), in_y)
    down_sum = add_b(jnp.where(x_low, down_sum[..., :384], down_sum[..., 384:]), down_x)
    ffn_sum = jnp.concatenate([in_sum, down_sum], axis=1)
    def by_z(stack):
        return [
            lax.dynamic_index_in_dim(stack, z_at ^ mask, 0, keepdims=False) for mask in range(4)
        ]

    ffn_own, ffn_first, ffn_second, ffn_third = by_z(ffn_sum)
    ffn_third = ctx_move(ffn_third, 4)
    two_got, one_got, ffn_own, ffn_first, ffn_second, ffn_third = hold(
        two_got, one_got, ffn_own, ffn_first, ffn_second, ffn_third
    )
    two_got, owner_sums, short_got, short_rows_back = hold(
        two_got, owner_sums, short_got, short_rows_back
    )
    ffn_second = add_b(ffn_second, ffn_third)
    long_pair_grad = near_own.astype(jnp.float32)
    for got_part in (far_own, one_got, two_got):
        long_pair_grad = long_pair_grad + got_part.astype(jnp.float32)
    long_pair_grad = long_pair_grad.astype(jnp.bfloat16)
    long_all = jnp.concatenate([long_query_grad, long_pair_grad], axis=0)
    long_back = back_rows(long_all)
    long_back, long_all = hold(long_back, long_all)
    long_got = y_swap(long_back[rows_here:].astype(jnp.bfloat16)).astype(jnp.float32)

    grad_qkv = product32(long_rows, long_all, (((0,), (1,)), ((), ()))) + product32(
        short_rows, short_all, (((0,), (1,)), ((), ()))
    )
    grad_qkv = grad_qkv.astype(jnp.bfloat16).reshape(4, 2, 2, 48, 576)
    grad_qkv = jnp.concatenate([grad_qkv, owner_sums], axis=3)
    core_keep = jnp.where(core_low, grad_qkv[:, :, 0], grad_qkv[:, :, 1])
    core_send = jnp.where(core_low, grad_qkv[:, :, 1], grad_qkv[:, :, 0])
    core_sum = add_b(core_keep, core_swap(core_send))

    own_sum, one_part, two_part, three_part = by_z(core_sum)
    one_part, three_part = ctx_move(one_part, 4), ctx_move(three_part, 4)
    two_part, qkv_hop = hold(add_b(two_part, three_part), three_part)
    two_part = ctx_move(two_part, 8)
    own_sum = sum(part.astype(jnp.float32) for part in (own_sum, one_part, two_part))
    y_keep = jnp.where(y_low, own_sum[0], own_sum[1])
    y_got = y_swap(jnp.where(y_low, own_sum[1], own_sum[0]).astype(jnp.bfloat16))
    own_part = ffn_own
    ffn_first, _ = hold(ffn_first, qkv_hop)
    one_part, two_part = ctx_move(ffn_first, 4), ctx_move(ffn_second, 8)
    one_part, two_part, y_keep = hold(one_part, two_part, y_keep)
    ffn_owned = sum(part.astype(jnp.float32) for part in (own_part, one_part, two_part))
    y_got = y_got.astype(jnp.float32)
    vector_sums = y_keep[48:] + y_got[48:]
    y_keep, y_got = y_keep[:48], y_got[:48]
    low_part, high_part = jnp.where(y_low, y_keep, y_got), jnp.where(y_low, y_got, y_keep)
    owned_qkv = [
        jnp.concatenate(
            [low_part[:, half * i : half * (i + 1)], high_part[:, half * i : half * (i + 1)]],
            axis=1,
        )
        for i in range(3)
    ]

    in_owned = jnp.concatenate([ffn_owned[:96], ffn_owned[96:192]], axis=1)
    in_owned = in_owned.astype(jnp.bfloat16).reshape(2, 48, 768)
    in_mine = jnp.where(core_low, in_owned[0], in_owned[1])
    in_other = core_swap(jnp.where(core_low, in_owned[1], in_owned[0]))
    in_even = jnp.where(core_low, in_mine, in_other).astype(jnp.float32)
    in_odd = jnp.where(core_low, in_other, in_mine).astype(jnp.float32)
    owned_in = jnp.concatenate(
        [
            part[:, 192 * k : 192 * (k + 1)]
            for k in range(4)
            for part in (in_even, in_odd)
        ],
        axis=1,
    )
    owned_out, owned_down = ffn_owned[192:240], ffn_owned[240:]

    short_part = short_rows_back[:rows_here] + short_got.astype(jnp.float32)
    long_part = long_back[:rows_here] + long_got
    own_part = jnp.where(own_long, long_part, short_part)
    far_part = x_swap(jnp.where(own_long, short_part, long_part).astype(jnp.bfloat16))
    tokens_grad = (grad_stream + own_part + far_part.astype(jnp.float32)).astype(jnp.bfloat16)

    def own_piece(row):
        return vector_sums[row, :48]

    rms_values = jnp.sqrt(vector_sums[1:4, 128] / (vector_sums[4, 128] * width))
    return (
        layer_out,
        tokens_grad[None],
        owned_qkv[0],
        owned_qkv[1],
        owned_qkv[2],
        owned_out,
        owned_in,
        owned_down,
        vector_sums[7, :48],
        own_piece(0),
        own_piece(1),
        own_piece(2),
        own_piece(3),
        vector_sums[0, 128:320],
        own_piece(4),
        own_piece(5),
        own_piece(6),
        rms_values,
    )


def layer_body(tokens, *others):
    fits = lax.axis_size("ctx") == 16 and lax.axis_size("fsdp") == 2
    if fits and tokens.shape == (1, 256, 768):
        return fast_body(tokens, *others)
    return body(tokens, *others)


def solution(mesh):
    in_specs = (
        P("fsdp", "ctx", None),
        P("fsdp"),
        P("fsdp", "ctx", None),
        P("ctx", "fsdp"),
        P("ctx", "fsdp"),
        P("ctx", "fsdp"),
        P("ctx", "fsdp"),
        P("ctx", "fsdp"),
        P("ctx", "fsdp"),
        P("ctx"),
        P("ctx"),
        P("ctx"),
        P("ctx"),
        P("ctx"),
        P("ctx"),
        P("ctx"),
        P("ctx"),
        P("ctx"),
    )
    out_specs = (
        P("fsdp", "ctx", None),
        P("fsdp", "ctx", None),
        P("ctx", "fsdp"),
        P("ctx", "fsdp"),
        P("ctx", "fsdp"),
        P("ctx", "fsdp"),
        P("ctx", "fsdp"),
        P("ctx", "fsdp"),
        P("ctx"),
        P("ctx"),
        P("ctx"),
        P("ctx"),
        P("ctx"),
        P("ctx"),
        P("ctx"),
        P("ctx"),
        P("ctx"),
        P(),
    )
    return jax.shard_map(layer_body, mesh=mesh, in_specs=in_specs, out_specs=out_specs, check_vma=False)
```

```python
import functools

import jax
import jax.numpy as jnp
from jax import lax
from jax.experimental import pallas as pl
from jax.experimental.pallas import tpu as pltpu
from jax.sharding import PartitionSpec as P

HEAD_DIM = 64


norm_eps = 1e-12
score_scale = 0.125
masked_score = -1000000000.0
rows_contract = (((0,), (0,)), ((), ()))
columns_contract = (((1,), (1,)), ((), ()))


def layer_norm(stream, gain_vec, shift_vec):
    center = jnp.mean(stream, axis=-1, keepdims=True)
    offset = stream - center
    spread = jnp.mean(offset * offset, axis=-1, keepdims=True)
    return offset * lax.rsqrt(spread + norm_eps) * gain_vec + shift_vec


def gelu_exact(inner_pre):
    return jax.nn.gelu(inner_pre, approximate=False)


def plain_product(left_side, right_side):
    return jnp.dot(left_side, right_side, preferred_element_type=jnp.float32)


def row_product(left_side, right_side):
    return lax.dot_general(left_side, right_side, rows_contract, preferred_element_type=jnp.float32)


def column_product(left_side, right_side):
    return lax.dot_general(
        left_side, right_side, columns_contract, preferred_element_type=jnp.float32
    )


def head_scores(query_head, key_head, key_ok):
    scores = (
        jnp.einsum("sqd,skd->sqk", query_head, key_head, preferred_element_type=jnp.float32)
        * score_scale
    )
    return jnp.where(key_ok[:, None, :], scores, masked_score)


def attend(query_seq, pair_all, key_ok):
    seq_count, slot_count, model_width = query_seq.shape
    heads_count = model_width // HEAD_DIM

    def one_head(head_index, loop_state):
        mixed_out, log_totals = loop_state
        head_start = head_index * HEAD_DIM
        query_head = lax.dynamic_slice_in_dim(query_seq, head_start, HEAD_DIM, 2)
        key_head = lax.dynamic_slice_in_dim(pair_all, head_start, HEAD_DIM, 2)
        value_head = lax.dynamic_slice_in_dim(pair_all, model_width + head_start, HEAD_DIM, 2)
        scores = head_scores(query_head, key_head, key_ok)
        row_peak = jnp.max(scores, axis=-1, keepdims=True)
        row_expo = jnp.exp(scores - row_peak)
        row_total = jnp.sum(row_expo, axis=-1, keepdims=True)
        attn_probs = (row_expo / row_total).astype(jnp.bfloat16)
        head_out = jnp.einsum(
            "sqk,skd->sqd", attn_probs, value_head, preferred_element_type=jnp.float32
        )
        mixed_out = lax.dynamic_update_slice_in_dim(mixed_out, head_out, head_start, 2)
        log_row = row_peak[..., 0] + jnp.log(row_total[..., 0])
        log_totals = lax.dynamic_update_index_in_dim(log_totals, log_row, head_index, 0)
        return (mixed_out, log_totals)

    start_state = (
        jnp.zeros((seq_count, slot_count, model_width), jnp.float32),
        jnp.zeros((heads_count, seq_count, slot_count), jnp.float32),
    )
    return lax.fori_loop(0, heads_count, one_head, start_state)


def attend_back(query_seq, pair_all, key_ok, log_totals, grad_mixed):
    seq_count, slot_count, model_width = query_seq.shape
    heads_count = model_width // HEAD_DIM

    def one_head(head_index, loop_state):
        grad_query, grad_pair = loop_state
        head_start = head_index * HEAD_DIM
        query_head = lax.dynamic_slice_in_dim(query_seq, head_start, HEAD_DIM, 2)
        key_head = lax.dynamic_slice_in_dim(pair_all, head_start, HEAD_DIM, 2)
        value_head = lax.dynamic_slice_in_dim(pair_all, model_width + head_start, HEAD_DIM, 2)
        grad_head = lax.dynamic_slice_in_dim(grad_mixed, head_start, HEAD_DIM, 2)
        scores = head_scores(query_head, key_head, key_ok)
        log_row = lax.dynamic_index_in_dim(log_totals, head_index, 0, keepdims=False)
        attn_probs = jnp.exp(scores - log_row[..., None])
        probs_b = attn_probs.astype(jnp.bfloat16)
        grad_probs = jnp.einsum(
            "sqd,skd->sqk", grad_head, value_head, preferred_element_type=jnp.float32
        )
        row_inner = jnp.sum(attn_probs * grad_probs, axis=-1, keepdims=True)
        grad_scores = (attn_probs * (grad_probs - row_inner)).astype(jnp.bfloat16)
        grad_query_head = (
            jnp.einsum("sqk,skd->sqd", grad_scores, key_head, preferred_element_type=jnp.float32)
            * score_scale
        )
        grad_key_head = (
            jnp.einsum("sqk,sqd->skd", grad_scores, query_head, preferred_element_type=jnp.float32)
            * score_scale
        )
        grad_value_head = jnp.einsum(
            "sqk,sqd->skd", probs_b, grad_head, preferred_element_type=jnp.float32
        )
        grad_query = lax.dynamic_update_slice_in_dim(grad_query, grad_query_head, head_start, 2)
        grad_pair = lax.dynamic_update_slice_in_dim(grad_pair, grad_key_head, head_start, 2)
        grad_pair = lax.dynamic_update_slice_in_dim(
            grad_pair, grad_value_head, model_width + head_start, 2
        )
        return (grad_query, grad_pair)

    start_state = (jnp.zeros(query_seq.shape, jnp.float32), jnp.zeros(pair_all.shape, jnp.float32))
    return lax.fori_loop(0, heads_count, one_head, start_state)


def column_sums(matrix_b):
    return jnp.sum(matrix_b.astype(jnp.float32), axis=0)


def body(
    tokens,
    lengths,
    cotangent,
    query_weight,
    key_weight,
    value_weight,
    out_weight,
    in_weight,
    down_weight,
    query_bias,
    value_bias,
    out_bias,
    attn_norm_gain,
    attn_norm_bias,
    in_bias,
    down_bias,
    ffn_norm_gain,
    ffn_norm_bias,
):
    seq_count, slot_count, model_width = tokens.shape
    row_count = seq_count * slot_count
    ctx_size = lax.axis_size("ctx")
    ctx_index = lax.axis_index("ctx")
    row_parts = (
        lax.all_gather(query_weight, "ctx", axis=0, tiled=True),
        lax.all_gather(key_weight, "ctx", axis=0, tiled=True),
        lax.all_gather(value_weight, "ctx", axis=0, tiled=True),
        lax.all_gather(out_weight, "ctx", axis=0, tiled=True),
        lax.all_gather(in_weight, "ctx", axis=0, tiled=True),
        lax.all_gather(down_weight, "ctx", axis=0, tiled=True),
        lax.all_gather(query_bias, "ctx", axis=0, tiled=True),
        lax.all_gather(value_bias, "ctx", axis=0, tiled=True),
        lax.all_gather(out_bias, "ctx", axis=0, tiled=True),
        lax.all_gather(attn_norm_gain, "ctx", axis=0, tiled=True),
        lax.all_gather(attn_norm_bias, "ctx", axis=0, tiled=True),
        lax.all_gather(in_bias, "ctx", axis=0, tiled=True),
        lax.all_gather(down_bias, "ctx", axis=0, tiled=True),
        lax.all_gather(ffn_norm_gain, "ctx", axis=0, tiled=True),
        lax.all_gather(ffn_norm_bias, "ctx", axis=0, tiled=True),
    )
    full_mats = (
        lax.all_gather(row_parts[0], "fsdp", axis=1, tiled=True),
        lax.all_gather(row_parts[1], "fsdp", axis=1, tiled=True),
        lax.all_gather(row_parts[2], "fsdp", axis=1, tiled=True),
        lax.all_gather(row_parts[3], "fsdp", axis=1, tiled=True),
        lax.all_gather(row_parts[4], "fsdp", axis=1, tiled=True),
        lax.all_gather(row_parts[5], "fsdp", axis=1, tiled=True),
    )
    query_full, key_full, value_full, out_full, in_full, down_full = full_mats
    query_vec = row_parts[6].astype(jnp.float32)
    value_vec = row_parts[7].astype(jnp.float32)
    out_vec = row_parts[8].astype(jnp.float32)
    gain_one = row_parts[9].astype(jnp.float32)
    bias_one = row_parts[10].astype(jnp.float32)
    in_vec = row_parts[11].astype(jnp.float32)
    down_vec = row_parts[12].astype(jnp.float32)
    gain_two = row_parts[13].astype(jnp.float32)
    bias_two = row_parts[14].astype(jnp.float32)
    local_slots = ctx_index * slot_count + jnp.arange(slot_count)
    local_ok = local_slots[None, :] < lengths[:, None]
    valid_mask = local_ok.astype(jnp.float32)
    valid_col = valid_mask.reshape(row_count, 1)
    key_ok = jnp.arange(slot_count * ctx_size)[None, :] < lengths[:, None]
    token_rows = tokens.reshape(row_count, model_width)
    queries_b = (plain_product(token_rows, query_full) + query_vec).astype(jnp.bfloat16)
    keys_b = plain_product(token_rows, key_full).astype(jnp.bfloat16)
    values_b = (plain_product(token_rows, value_full) + value_vec).astype(jnp.bfloat16)
    pair_local = jnp.concatenate([keys_b, values_b], axis=1).reshape(
        seq_count, slot_count, 2 * model_width
    )
    pair_all = lax.all_gather(pair_local, "ctx", axis=1, tiled=True)
    query_seq = queries_b.reshape(seq_count, slot_count, model_width)
    mixed_out, log_totals = attend(query_seq, pair_all, key_ok)
    mixed_b = mixed_out.reshape(row_count, model_width).astype(jnp.bfloat16)
    attn_branch = plain_product(mixed_b, out_full) + out_vec
    stream = token_rows.astype(jnp.float32) + attn_branch
    norm_one, norm_one_back = jax.vjp(layer_norm, stream, gain_one, bias_one)
    norm_one_b = norm_one.astype(jnp.bfloat16)
    inner_pre = plain_product(norm_one_b, in_full) + in_vec
    act_out, gelu_back = jax.vjp(gelu_exact, inner_pre)
    act_b = act_out.astype(jnp.bfloat16)
    ffn_branch = plain_product(act_b, down_full) + down_vec
    stream_two = norm_one + ffn_branch
    final_out, norm_two_back = jax.vjp(layer_norm, stream_two, gain_two, bias_two)
    layer_out = (
        (valid_col * final_out).astype(jnp.bfloat16).reshape(seq_count, slot_count, model_width)
    )
    grad_final = valid_col * cotangent.reshape(row_count, model_width).astype(jnp.float32)
    grad_stream_two, grad_gain_two, grad_bias_two = norm_two_back(grad_final)
    grad_ffn_b = grad_stream_two.astype(jnp.bfloat16)
    grad_down_vec = column_sums(grad_ffn_b)
    grad_down_full = row_product(act_b, grad_ffn_b)
    grad_inner_b = gelu_back(column_product(grad_ffn_b, down_full))[0].astype(jnp.bfloat16)
    grad_in_vec = column_sums(grad_inner_b)
    grad_in_full = row_product(norm_one_b, grad_inner_b)
    grad_norm_one = grad_stream_two + column_product(grad_inner_b, in_full)
    grad_stream, grad_gain_one, grad_bias_one = norm_one_back(grad_norm_one)
    grad_attn_b = grad_stream.astype(jnp.bfloat16)
    grad_out_vec = column_sums(grad_attn_b)
    grad_out_full = row_product(mixed_b, grad_attn_b)
    grad_mixed = (
        column_product(grad_attn_b, out_full)
        .astype(jnp.bfloat16)
        .reshape(seq_count, slot_count, model_width)
    )
    grad_query_seq, grad_pair = attend_back(query_seq, pair_all, key_ok, log_totals, grad_mixed)
    grad_pair_local = lax.psum_scatter(
        grad_pair.astype(jnp.bfloat16), "ctx", scatter_dimension=1, tiled=True
    ).astype(jnp.float32)
    grad_keys_b = (
        grad_pair_local[:, :, :model_width].reshape(row_count, model_width).astype(jnp.bfloat16)
    )
    grad_values_b = (
        grad_pair_local[:, :, model_width:].reshape(row_count, model_width).astype(jnp.bfloat16)
    )
    grad_queries_b = grad_query_seq.reshape(row_count, model_width).astype(jnp.bfloat16)
    grad_query_full = row_product(token_rows, grad_queries_b)
    grad_query_vec = column_sums(grad_queries_b)
    grad_key_full = row_product(token_rows, grad_keys_b)
    grad_value_full = row_product(token_rows, grad_values_b)
    grad_value_vec = column_sums(grad_values_b)
    tokens_grad = (
        (
            grad_stream
            + column_product(grad_queries_b, query_full)
            + column_product(grad_keys_b, key_full)
            + column_product(grad_values_b, value_full)
        )
        .astype(jnp.bfloat16)
        .reshape(seq_count, slot_count, model_width)
    )
    narrow = (
        lax.psum_scatter(
            grad_query_full.astype(jnp.bfloat16), "fsdp", scatter_dimension=1, tiled=True
        ).astype(jnp.float32),
        lax.psum_scatter(
            grad_key_full.astype(jnp.bfloat16), "fsdp", scatter_dimension=1, tiled=True
        ).astype(jnp.float32),
        lax.psum_scatter(
            grad_value_full.astype(jnp.bfloat16), "fsdp", scatter_dimension=1, tiled=True
        ).astype(jnp.float32),
        lax.psum_scatter(
            grad_out_full.astype(jnp.bfloat16), "fsdp", scatter_dimension=1, tiled=True
        ).astype(jnp.float32),
        lax.psum_scatter(
            grad_in_full.astype(jnp.bfloat16), "fsdp", scatter_dimension=1, tiled=True
        ).astype(jnp.float32),
        lax.psum_scatter(
            grad_down_full.astype(jnp.bfloat16), "fsdp", scatter_dimension=1, tiled=True
        ).astype(jnp.float32),
    )
    owned_grads = (
        lax.psum_scatter(
            narrow[0].astype(jnp.bfloat16), "ctx", scatter_dimension=0, tiled=True
        ).astype(jnp.float32),
        lax.psum_scatter(
            narrow[1].astype(jnp.bfloat16), "ctx", scatter_dimension=0, tiled=True
        ).astype(jnp.float32),
        lax.psum_scatter(
            narrow[2].astype(jnp.bfloat16), "ctx", scatter_dimension=0, tiled=True
        ).astype(jnp.float32),
        lax.psum_scatter(
            narrow[3].astype(jnp.bfloat16), "ctx", scatter_dimension=0, tiled=True
        ).astype(jnp.float32),
        lax.psum_scatter(
            narrow[4].astype(jnp.bfloat16), "ctx", scatter_dimension=0, tiled=True
        ).astype(jnp.float32),
        lax.psum_scatter(
            narrow[5].astype(jnp.bfloat16), "ctx", scatter_dimension=0, tiled=True
        ).astype(jnp.float32),
    )
    moments = jnp.stack(
        [
            jnp.sum(valid_col * stream * stream),
            jnp.sum(valid_col * attn_branch * attn_branch),
            jnp.sum(valid_col * ffn_branch * ffn_branch),
            jnp.sum(valid_col),
        ]
    )
    summed = lax.psum(
        (
            moments,
            grad_query_vec,
            grad_value_vec,
            grad_out_vec,
            grad_gain_one,
            grad_bias_one,
            grad_in_vec,
            grad_down_vec,
            grad_gain_two,
            grad_bias_two,
        ),
        ("ctx", "fsdp"),
    )
    width_shard = query_bias.shape[0]
    hidden_shard = in_bias.shape[0]

    def own_piece(vector_full, shard_len):
        return lax.dynamic_slice_in_dim(vector_full, ctx_index * shard_len, shard_len, 0)

    rms_values = jnp.sqrt(summed[0][:3] / (summed[0][3] * model_width))
    return (
        layer_out,
        tokens_grad,
        owned_grads[0],
        owned_grads[1],
        owned_grads[2],
        owned_grads[3],
        owned_grads[4],
        owned_grads[5],
        own_piece(summed[1], width_shard),
        own_piece(summed[2], width_shard),
        own_piece(summed[3], width_shard),
        own_piece(summed[4], width_shard),
        own_piece(summed[5], width_shard),
        own_piece(summed[6], hidden_shard),
        own_piece(summed[7], width_shard),
        own_piece(summed[8], width_shard),
        own_piece(summed[9], width_shard),
        rms_values,
    )


HEADS_HERE = 3
HEAD_COLS = HEADS_HERE * HEAD_DIM
rows_first = (((0,), (0,)), ((), ()))
lanes_both = (((1,), (1,)), ((), ()))
plain_contract = (((1,), (0,)), ((), ()))


def effort(microseconds):
    return pl.CostEstimate(
        flops=int(microseconds * 1e8), transcendentals=0, bytes_accessed=int(microseconds * 1e5)
    )


kernel_params = pltpu.CompilerParams(vmem_limit_bytes=24 * 1024 * 1024)


def product32(left_side, right_side, contract):
    return lax.dot_general(left_side, right_side, contract, preferred_element_type=jnp.float32)


def ctx_move(value, mask):
    return lax.ppermute(value, "ctx", [(i, i ^ mask) for i in range(16)])


def core_swap(value):
    return ctx_move(value, 1)


def y_swap(value):
    return ctx_move(value, 2)


def x_swap(value):
    return lax.ppermute(value, "fsdp", [(0, 1), (1, 0)])


def add_b(left_side, right_side):
    return (left_side.astype(jnp.float32) + right_side.astype(jnp.float32)).astype(jnp.bfloat16)


def row_sums(matrix_b):
    return jnp.sum(matrix_b.astype(jnp.float32), axis=0, keepdims=True)


def hold(*values):
    return lax.optimization_barrier(values)


def when_flag(flag_ref, run, idle):
    if flag_ref is None:
        run()
    else:
        pl.when(flag_ref[0] > 0)(run)
        pl.when(flag_ref[0] <= 0)(idle)


def attend_kernel(count, first, last, flagged, *refs):
    flag_ref = refs[0] if flagged else None
    refs = refs[flagged:]
    query_ref, pairs = refs[0], refs[1 : 1 + count]
    refs = refs[1 + count :]
    if not first:
        peak_in, total_in, mixed_in = refs[:3]
        refs = refs[3:]

    def one_head(head, carry):
        key_rows = pl.ds(pl.multiple_of(head * HEAD_DIM, HEAD_DIM), HEAD_DIM)
        value_rows = pl.ds(pl.multiple_of(HEAD_COLS + head * HEAD_DIM, HEAD_DIM), HEAD_DIM)
        query = query_ref[key_rows, :]
        width = query.shape[1]
        if first:
            peak = jnp.full((1, width), -1e30, jnp.float32)
            total = jnp.zeros((1, width), jnp.float32)
            mixed = jnp.zeros((HEAD_DIM, width), jnp.float32)
        else:
            peak, total, mixed = peak_in[head][0:1], total_in[head][0:1], mixed_in[key_rows, :]
        for pair in pairs:
            scores = product32(pair[key_rows, :], query, rows_first)
            new_peak = jnp.maximum(peak, jnp.max(scores, axis=0, keepdims=True))
            expo = jnp.exp(scores - new_peak)
            shrink = jnp.exp(peak - new_peak)
            total = total * shrink + jnp.sum(expo, axis=0, keepdims=True)
            mixed = mixed * shrink + product32(
                pair[value_rows, :], expo.astype(jnp.bfloat16), plain_contract
            )
            peak = new_peak
        if last:
            mixed_out, log_out = refs
            mixed_out[key_rows, :] = (mixed / total).astype(jnp.bfloat16)
            log_out[head] = jnp.broadcast_to(peak + jnp.log(total), (8, width))
        else:
            peak_out, total_out, sum_out = refs
            peak_out[head] = jnp.broadcast_to(peak, (8, width))
            total_out[head] = jnp.broadcast_to(total, (8, width))
            sum_out[key_rows, :] = mixed
        return carry

    def run():
        lax.fori_loop(0, HEADS_HERE, one_head, 0)

    def idle():
        for ref in refs:
            ref[...] = jnp.zeros_like(ref)

    when_flag(flag_ref, run, idle)


def attend_call(query, pairs, state=None, last=False, flag=None):
    width = query.shape[1]
    stat = jax.ShapeDtypeStruct((HEADS_HERE, 8, width), jnp.float32)
    if last:
        outs = [jax.ShapeDtypeStruct((HEAD_COLS, width), jnp.bfloat16), stat]
    else:
        outs = [stat, stat, jax.ShapeDtypeStruct((HEAD_COLS, width), jnp.float32)]
    ins = [query, *pairs, *(() if state is None else state)]
    specs = [pl.BlockSpec(memory_space=pltpu.VMEM)] * len(ins)
    if flag is not None:
        ins, specs = [flag, *ins], [pl.BlockSpec(memory_space=pltpu.SMEM), *specs]
    return pl.pallas_call(
        functools.partial(attend_kernel, len(pairs), state is None, last, int(flag is not None)),
        out_shape=outs,
        in_specs=specs,
        compiler_params=kernel_params,
        cost_estimate=effort(3.5),
    )(*ins)


def attend_back_kernel(count, first, flagged, *refs):
    flag_ref = refs[0] if flagged else None
    refs = refs[flagged:]
    query_ref, grad_ref, log_ref, mixed_ref = refs[:4]
    pairs = refs[4 : 4 + count]
    refs = refs[4 + count :]
    if not first:
        grad_query_in, refs = refs[0], refs[1:]
    grad_query_out, grad_pairs = refs[0], refs[1 : 1 + count]
    held, sems = refs[1 + count :]
    hbm_pairs, pairs = pairs, [held.at[i] for i in range(count)]

    def one_head(head, carry):
        key_rows = pl.ds(pl.multiple_of(head * HEAD_DIM, HEAD_DIM), HEAD_DIM)
        value_rows = pl.ds(pl.multiple_of(HEAD_COLS + head * HEAD_DIM, HEAD_DIM), HEAD_DIM)
        query, grad = query_ref[key_rows, :], grad_ref[key_rows, :]
        log_row = log_ref[head][0:1]
        inner = jnp.sum(
            mixed_ref[key_rows, :].astype(jnp.float32) * grad.astype(jnp.float32),
            axis=0,
            keepdims=True,
        )
        if first:
            grad_query = jnp.zeros((HEAD_DIM, query.shape[1]), jnp.float32)
        else:
            grad_query = grad_query_in[key_rows, :]
        for pair, grad_pair in zip(pairs, grad_pairs):
            keys = pair[key_rows, :]
            probs = jnp.exp(product32(keys, query, rows_first) - log_row)
            grad_probs = product32(pair[value_rows, :], grad, rows_first)
            grad_scores = (probs * (grad_probs - inner)).astype(jnp.bfloat16)
            grad_query = grad_query + product32(keys, grad_scores, plain_contract)
            grad_pair[key_rows, :] = product32(query, grad_scores, lanes_both).astype(jnp.bfloat16)
            grad_pair[value_rows, :] = product32(
                grad, probs.astype(jnp.bfloat16), lanes_both
            ).astype(jnp.bfloat16)
        grad_query_out[key_rows, :] = grad_query
        return carry

    def run():
        copies = [
            pltpu.make_async_copy(hbm, held.at[i], sems.at[i]) for i, hbm in enumerate(hbm_pairs)
        ]
        for copy in copies:
            copy.start()
        for copy in copies:
            copy.wait()
        lax.fori_loop(0, HEADS_HERE, one_head, 0)

    def idle():
        for ref in (grad_query_out, *grad_pairs):
            ref[...] = jnp.zeros_like(ref)

    when_flag(flag_ref, run, idle)


def attend_back_call(query, grad, log_rows, mixed, pairs, grad_query=None, flag=None):
    outs = [jax.ShapeDtypeStruct(query.shape, jnp.float32)]
    outs += [jax.ShapeDtypeStruct(pair.shape, jnp.bfloat16) for pair in pairs]
    ins = [query, grad, log_rows, mixed, *pairs, *(() if grad_query is None else (grad_query,))]
    specs = [pl.BlockSpec(memory_space=pltpu.VMEM)] * len(ins)
    specs[4 : 4 + len(pairs)] = [pl.BlockSpec(memory_space=pl.ANY)] * len(pairs)
    if flag is not None:
        ins, specs = [flag, *ins], [pl.BlockSpec(memory_space=pltpu.SMEM), *specs]
    return pl.pallas_call(
        functools.partial(
            attend_back_kernel, len(pairs), grad_query is None, int(flag is not None)
        ),
        out_shape=outs,
        in_specs=specs,
        scratch_shapes=[
            pltpu.VMEM((len(pairs), *pairs[0].shape), jnp.bfloat16),
            pltpu.SemaphoreType.DMA((len(pairs),)),
        ],
        compiler_params=kernel_params,
        cost_estimate=effort(10.0),
    )(*ins)


def pack_kernel(me_ref, *refs):
    given, (rows_ref, keep_ref, send_ref, in_keep, in_send) = refs[:4], refs[4:9]
    held, sems = refs[9:13], refs[13]
    copies = [
        pltpu.make_async_copy(source, target, sems.at[i])
        for i, (source, target) in enumerate(zip(given, held))
    ]
    for copy in copies:
        copy.start()
    for copy in copies:
        copy.wait()
    y_low, core_low = (me_ref[0] & 2) == 0, (me_ref[0] & 1) == 0
    for i, ref in enumerate(held[:3]):
        low, high = ref[:, :192], ref[:, 192:]
        keep_ref[0:48, 192 * i : 192 * (i + 1)] = jnp.where(y_low, low, high)
        send_ref[0:48, 192 * i : 192 * (i + 1)] = jnp.where(y_low, high, low)
    keep_ref[48:56, :] = rows_ref[...]
    send_ref[48:56, :] = rows_ref[...]
    for k in range(4):
        even = held[3][:, 384 * k : 384 * k + 192]
        odd = held[3][:, 384 * k + 192 : 384 * (k + 1)]
        in_keep[:, 192 * k : 192 * (k + 1)] = jnp.where(core_low, even, odd)
        in_send[:, 192 * k : 192 * (k + 1)] = jnp.where(core_low, odd, even)


def pack_call(me, weights, rows):
    return pl.pallas_call(
        pack_kernel,
        out_shape=[
            jax.ShapeDtypeStruct(shape, jnp.bfloat16)
            for shape in ((56, 576), (56, 576), (48, 768), (48, 768))
        ],
        in_specs=[
            pl.BlockSpec(memory_space=pltpu.SMEM),
            *[pl.BlockSpec(memory_space=pl.ANY)] * 4,
            pl.BlockSpec(memory_space=pltpu.VMEM),
        ],
        scratch_shapes=[
            *(pltpu.VMEM(weight.shape, jnp.bfloat16) for weight in weights),
            pltpu.SemaphoreType.DMA((4,)),
        ],
        compiler_params=kernel_params,
        cost_estimate=effort(400.0),
    )(me, *weights, rows)


def place_qkv_kernel(me_ref, own_ref, far_ref, mats_ref, wide_ref, heads_ref, hidden_ref, vecs_ref):
    for core, stack in enumerate((own_ref, far_ref)):
        for z in range(4):
            for y in range(2):
                owner = jnp.bitwise_xor(me_ref[0], z * 4 + y * 2 + core)
                mats_ref[owner] = stack[z, y, 0:48]
                vecs_ref[owner] = stack[z, y, 48:56].astype(jnp.float32)
    core_low = (me_ref[0] & 1) == 0
    for i in range(16):
        wide_ref[:, 48 * i : 48 * (i + 1)] = vecs_ref[i, :, 0:48]
    for i in range(8):
        hidden_ref[:, 192 * i : 192 * (i + 1)] = jnp.where(
            core_low, vecs_ref[2 * i, :, 128:320], vecs_ref[2 * i + 1, :, 128:320]
        )
    column = 2 * me_ref[1] + ((me_ref[0] >> 1) & 1)
    for i in range(4):

        @pl.when(column == i)
        def _():
            heads_ref[...] = wide_ref[:, 192 * i : 192 * (i + 1)]


def place_in_kernel(me_ref, one_own, one_far, two_own, two_far, in_ref, out_ref):
    zy_at, x_low = me_ref[0] >> 1, me_ref[1] == 0
    for y, stack in enumerate((two_own, two_far)):
        for z in range(4):
            owner = jnp.bitwise_xor(zy_at, z * 2 + y)
            own, far = one_own[4 * y + z], one_far[4 * y + z]
            low, high = jnp.where(x_low, own, far), jnp.where(x_low, far, own)
            in_ref[owner, :, 0:384], in_ref[owner, :, 768:1152] = low[0:96], high[0:96]
            out_ref[owner, :, 0:384], out_ref[owner, :, 384:768] = low[96:144], high[96:144]
            own, far = stack[0, z], stack[1, z]
            in_ref[owner, :, 384:768] = jnp.where(x_low, own, far)
            in_ref[owner, :, 1152:1536] = jnp.where(x_low, far, own)


def place_down_kernel(me_ref, one_own, one_far, two_own, two_far, down_ref):
    zy_at, x_low = me_ref[0] >> 1, me_ref[1] == 0
    for y, stack in enumerate((two_own, two_far)):
        for z in range(4):
            owner = jnp.bitwise_xor(zy_at, z * 2 + y)
            own, far = one_own[4 * y + z], one_far[4 * y + z]
            down_ref[owner, 0:96, 0:384] = jnp.where(x_low, own, far)
            down_ref[owner, 0:96, 384:768] = jnp.where(x_low, far, own)
            own, far = stack[0, z], stack[1, z]
            down_ref[owner, 96:192, 0:384] = jnp.where(x_low, own, far)
            down_ref[owner, 96:192, 384:768] = jnp.where(x_low, far, own)


def vectors_kernel(me_ref, *refs):
    rows, (query_ref, hidden_ref), moments, out_ref = refs[:7], refs[7:9], refs[9:13], refs[13]
    out_ref[...] = jnp.zeros_like(out_ref)
    core = me_ref[0] & 1
    column = 2 * me_ref[1] + ((me_ref[0] >> 1) & 1)
    totals = [jnp.sum(ref[...], axis=1, keepdims=True) for ref in moments]
    for i in range(16):
        for row, ref in enumerate(rows):
            out_ref[i, row : row + 1, 0:48] = ref[0:1, 48 * i : 48 * (i + 1)]
        part = query_ref[0:1, 48 * (i % 4) : 48 * (i % 4 + 1)]
        out_ref[i, 7:8, 0:48] = jnp.where(column == i // 4, part, 0.0)
        part = hidden_ref[0:1, 192 * (i // 2) : 192 * (i // 2 + 1)]
        out_ref[i, 0:1, 128:320] = jnp.where(core == i % 2, part, 0.0)
        for row, total in enumerate(totals):
            out_ref[i, row + 1 : row + 2, 128:256] = jnp.broadcast_to(total, (1, 128))


def place_call(kernel, me, stacks, shapes, more=(), scratch=(), cost=2.0):
    return pl.pallas_call(
        kernel,
        out_shape=[jax.ShapeDtypeStruct(shape, jnp.bfloat16) for shape in shapes]
        + [jax.ShapeDtypeStruct(shape, jnp.float32) for shape in more],
        scratch_shapes=[pltpu.VMEM(shape, jnp.float32) for shape in scratch],
        in_specs=[pl.BlockSpec(memory_space=pltpu.SMEM)]
        + [pl.BlockSpec(memory_space=pltpu.VMEM)] * len(stacks),
        compiler_params=kernel_params,
        cost_estimate=effort(cost),
    )(me, *stacks)


def fast_body(
    tokens,
    lengths,
    cotangent,
    query_weight,
    key_weight,
    value_weight,
    out_weight,
    in_weight,
    down_weight,
    query_bias,
    value_bias,
    out_bias,
    attn_norm_gain,
    attn_norm_bias,
    in_bias,
    down_bias,
    ffn_norm_gain,
    ffn_norm_bias,
):
    slot_count, width = tokens.shape[1:]
    me = lax.axis_index("ctx")
    x_at = lax.axis_index("fsdp")
    z_at, y_at, core_at = me >> 2, (me >> 1) & 1, me & 1
    y_low, x_low, core_low = y_at == 0, x_at == 0, core_at == 0
    own_long = lengths[0] == slot_count * lax.axis_size("ctx")
    short_flag = (z_at == 0).astype(jnp.int32).reshape(1)

    half = HEAD_COLS
    vector_rows = sum(
        lax.pad(piece[None, :], jnp.asarray(0, jnp.bfloat16), ((row, 7 - row, 0), (at, 576 - at - piece.shape[0], 0)))
        for row, at, piece in (
            (0, 0, query_bias),
            (1, 0, value_bias),
            (2, 0, out_bias),
            (3, 0, attn_norm_gain),
            (4, 0, attn_norm_bias),
            (5, 0, down_bias),
            (6, 0, ffn_norm_gain),
            (7, 0, ffn_norm_bias),
            (0, 128, in_bias),
        )
    )
    where_me = jnp.stack([me, x_at]).astype(jnp.int32)
    keep_cols, send_cols, in_keep, in_send = pack_call(
        where_me, (query_weight, key_weight, value_weight, in_weight), vector_rows
    )
    token_rows = tokens[0]
    in_got = core_swap(in_send)
    in_block = jnp.concatenate(
        [jnp.where(core_low, in_keep, in_got), jnp.where(core_low, in_got, in_keep)], axis=0
    )
    ffn_block = jnp.concatenate([in_block[:, :384], out_weight, in_block[:, 384:], down_weight])
    other_rows = x_swap(token_rows)
    long_own = jnp.where(own_long, token_rows, other_rows)
    short_own = jnp.where(own_long, other_rows, token_rows)
    got_cols, ffn_one, long_own, short_own = hold(
        y_swap(send_cols), ctx_move(ffn_block, 4), long_own, short_own
    )
    own_block = jnp.stack([keep_cols, got_cols])
    ffn_two = ctx_move(ffn_block, 8)
    z_one, z_two, long_far, short_own = hold(
        ctx_move(own_block, 4), ctx_move(own_block, 8), y_swap(long_own), short_own
    )
    z_three = ctx_move(z_two, 4)
    ffn_three = ctx_move(ffn_two, 4)
    z_stack = jnp.stack([own_block, z_one, z_two, z_three])
    qkv_weight, wide, heads, hidden = place_call(
        place_qkv_kernel,
        where_me,
        (z_stack, core_swap(z_stack)),
        ((16, 48, 576),),
        ((8, 768), (8, half), (8, 1536)),
        ((16, 8, 576),),
    )
    qkv_weight = qkv_weight.reshape(768, 576)
    out_vec, gain_one, bias_one, down_vec, gain_two, bias_two = (
        wide[row : row + 1] for row in range(2, 8)
    )
    in_vec = hidden[:1]
    columns = heads.T
    query_add, value_add = columns[:, 0:1], columns[:, 1:2]
    pair_add = jnp.concatenate([jnp.zeros_like(value_add), value_add], axis=0)

    long_rows = jnp.concatenate([long_own, long_far], axis=0)
    def project(rows):
        query = product32(qkv_weight[:, :half], rows, (((0,), (1,)), ((), ()))) + query_add
        pair = product32(qkv_weight[:, half:], rows, (((0,), (1,)), ((), ()))) + pair_add
        scale = jnp.asarray(score_scale, jnp.bfloat16)
        return query.astype(jnp.bfloat16) * scale, pair.astype(jnp.bfloat16)

    long_query, long_pair = project(long_rows)
    short_own, _ = hold(short_own, z_three)
    short_far = y_swap(short_own)
    long_pair, ffn_three, short_far = hold(long_pair, ffn_three, short_far)
    kv_two, kv_one = ctx_move(long_pair, 8), ctx_move(long_pair, 4)
    long_pair_far = core_swap(long_pair)
    state = attend_call(long_query, (long_pair, long_pair_far))
    short_rows = jnp.concatenate([short_own, short_far], axis=0)
    short_query, short_pair = project(short_rows)
    short_pairs = (short_pair, core_swap(short_pair))
    short_mixed, short_log = attend_call(short_query, short_pairs, last=True, flag=short_flag)
    ffn_stack = jnp.stack([ffn_block, ffn_one, ffn_two, ffn_three])
    in_one, in_two = ffn_stack[:, :144], ffn_stack[:, 144:240]
    in_one_y, in_two_x = y_swap(in_one), x_swap(in_two)
    kv_one, kv_two, in_one_y, in_two_x, short_mixed, *state = hold(
        kv_one, kv_two, in_one_y, in_two_x, short_mixed, *state
    )
    kv_three = ctx_move(kv_two, 4)
    in_one, in_two = jnp.concatenate([in_one, in_one_y], axis=0), jnp.stack([in_two, in_two_x])
    in_one_far, in_two_far = x_swap(in_one), y_swap(in_two)
    kv_one_far, kv_two_far = core_swap(kv_one), core_swap(kv_two)
    state = attend_call(long_query, (kv_one, kv_one_far), state)
    state = attend_call(long_query, (kv_two, kv_two_far), state)
    kv_three, *state = hold(kv_three, *state)
    kv_three_far = core_swap(kv_three)
    long_mixed, long_log = attend_call(long_query, (kv_three, kv_three_far), state, last=True)
    pairs = (
        (long_pair, long_pair_far),
        (kv_one, kv_one_far),
        (kv_two, kv_two_far),
        (kv_three, kv_three_far),
    )

    rows_here = slot_count
    sent = jnp.concatenate([long_mixed[:, rows_here:], short_mixed[:, rows_here:]], axis=0)
    sent, in_one_far, in_two_far = hold(sent, in_one_far, in_two_far)
    got = y_swap(sent)
    def by_y(mine, theirs):
        return jnp.concatenate(
            [jnp.where(y_low, mine, theirs), jnp.where(y_low, theirs, mine)], axis=0
        )

    long_heads = by_y(long_mixed[:, :rows_here], got[:half])
    short_heads = by_y(short_mixed[:, :rows_here], got[half:])
    own_heads = jnp.where(own_long, long_heads, short_heads)
    sent = jnp.where(own_long, short_heads, long_heads)
    far_heads = x_swap(sent)
    in_all, out_core = place_call(
        place_in_kernel,
        where_me,
        (in_one, in_one_far, in_two, in_two_far),
        ((8, 96, 1536), (8, 48, 768)),
    )
    down_one, down_two = ffn_stack[:, 240:336], ffn_stack[:, 336:]
    down_one, down_two, _ = hold(down_one, down_two, sent)
    down_one_y, down_two_x = hold(y_swap(down_one), x_swap(down_two))
    down_one = jnp.concatenate([down_one, down_one_y], axis=0)
    down_two = jnp.stack([down_two, down_two_x])
    (down_all,) = place_call(
        place_down_kernel,
        where_me,
        (down_one, x_swap(down_one), down_two, y_swap(down_two)),
        ((8, 192, 768),),
    )
    in_all, down_all = in_all.reshape(768, 1536), down_all.reshape(1536, 768)
    out_far = core_swap(out_core)
    out_all = jnp.stack(
        [jnp.where(core_low, out_core, out_far), jnp.where(core_low, out_far, out_core)], axis=1
    ).reshape(768, 768)

    mixed_t = jnp.concatenate(
        [jnp.where(x_low, own_heads, far_heads), jnp.where(x_low, far_heads, own_heads)], axis=0
    )

    local_slots = me * slot_count + jnp.arange(slot_count)
    valid_col = (local_slots < lengths[0]).astype(jnp.float32)[:, None]
    attn_branch = product32(mixed_t, out_all, rows_first) + out_vec
    stream = token_rows.astype(jnp.float32) + attn_branch
    norm_one, norm_one_back = jax.vjp(layer_norm, stream, gain_one, bias_one)
    norm_one_b = norm_one.astype(jnp.bfloat16)
    chip_norm = jnp.concatenate([norm_one_b, core_swap(norm_one_b)], axis=0)
    act_out, gelu_back = jax.vjp(gelu_exact, plain_product(chip_norm, in_all) + in_vec)
    act_b = act_out.astype(jnp.bfloat16)
    ffn_got = core_swap(plain_product(act_b[rows_here:], down_all).astype(jnp.bfloat16))
    ffn_part = plain_product(act_b[:rows_here], down_all)
    ffn_branch = ffn_part + ffn_got.astype(jnp.float32) + down_vec
    stream_two = norm_one + ffn_branch
    final_out, norm_two_back = jax.vjp(layer_norm, stream_two, gain_two, bias_two)
    layer_out = (valid_col * final_out).astype(jnp.bfloat16)[None]
    grad_final = valid_col * cotangent[0].astype(jnp.float32)
    grad_stream_two, grad_gain_two, grad_bias_two = norm_two_back(grad_final)
    grad_ffn_b = grad_stream_two.astype(jnp.bfloat16)
    grad_down_vec = row_sums(grad_ffn_b)
    chip_grad = jnp.concatenate([grad_ffn_b, core_swap(grad_ffn_b)], axis=0)
    grad_inner_b = gelu_back(column_product(chip_grad, down_all))[0].astype(jnp.bfloat16)
    grad_in_vec = row_sums(grad_inner_b)
    norm_got = core_swap(column_product(grad_inner_b[rows_here:], in_all).astype(jnp.bfloat16))
    norm_part = column_product(grad_inner_b[:rows_here], in_all)
    grad_norm_one = grad_stream_two + norm_part + norm_got.astype(jnp.float32)
    grad_stream, grad_gain_one, grad_bias_one = norm_one_back(grad_norm_one)
    grad_attn_b = grad_stream.astype(jnp.bfloat16)
    grad_out_vec = row_sums(grad_attn_b)
    grad_mixed_t = product32(out_all, grad_attn_b, lanes_both).astype(jnp.bfloat16)
    ones = jnp.ones((8, slot_count), jnp.bfloat16)
    grad_value_vec = product32(ones, grad_mixed_t, lanes_both)[:1]

    chip_norm, act_b, grad_inner_b, mixed_w, _ = lax.optimization_barrier(
        (chip_norm, act_b, grad_inner_b, mixed_t, grad_mixed_t)
    )
    inner_send = jnp.where(x_low, grad_inner_b[:, 768:], grad_inner_b[:, :768])
    inner_keep = jnp.where(x_low, grad_inner_b[:, :768], grad_inner_b[:, 768:])
    def with_out(in_part, out_part):
        in_part = in_part.astype(jnp.bfloat16).reshape(4, 2, 96, 768)
        return jnp.concatenate([in_part[..., :384], in_part[..., 384:], out_part], axis=2)

    grad_out = plain_product(mixed_w, grad_attn_b).astype(jnp.bfloat16).reshape(4, 2, 2, 48, 768)
    out_sum = add_b(
        jnp.where(core_low, grad_out[:, :, 0], grad_out[:, :, 1]),
        core_swap(jnp.where(core_low, grad_out[:, :, 1], grad_out[:, :, 0])),
    )
    in_send = with_out(
        row_product(chip_norm, inner_send),
        jnp.where(x_low, out_sum[..., 384:], out_sum[..., :384]),
    )
    in_keep_grad = with_out(
        row_product(chip_norm, inner_keep),
        jnp.where(x_low, out_sum[..., :384], out_sum[..., 384:]),
    )
    grad_down = row_product(act_b, chip_grad).astype(jnp.bfloat16).reshape(4, 2, 192, 768)
    down_send = jnp.where(y_low, grad_down[:, 1], grad_down[:, 0])
    down_keep = jnp.where(y_low, grad_down[:, 0], grad_down[:, 1])
    keep_x = jnp.where(x_low, grad_mixed_t[:384], grad_mixed_t[384:])
    got_x = x_swap(jnp.where(x_low, grad_mixed_t[384:], grad_mixed_t[:384]))
    long_x = jnp.where(own_long, keep_x, got_x)
    short_x = jnp.where(own_long, got_x, keep_x)
    both_keep = jnp.where(y_low, long_x[:half], long_x[half:])
    short_keep = jnp.where(y_low, short_x[:half], short_x[half:])
    sent = jnp.concatenate(
        [
            jnp.where(y_low, long_x[half:], long_x[:half]),
            jnp.where(y_low, short_x[half:], short_x[:half]),
        ],
        axis=0,
    )
    got = y_swap(sent)
    long_grad = jnp.concatenate([both_keep, got[:half]], axis=1)
    short_grad = jnp.concatenate([short_keep, got[half:]], axis=1)
    in_send, down_send, long_grad, _ = hold(in_send, down_send, long_grad, got)
    in_x, down_y = x_swap(in_send), y_swap(down_send)


    grad_query, *grads = attend_back_call(
        long_query, long_grad, long_log, long_mixed, sum(pairs[::-1], ())
    )
    near, far = grads[::2], grads[1::2]
    *far, grad_query, in_x, down_y = hold(
        *(core_swap(part) for part in far), grad_query, in_x, down_y
    )
    three, two, one = (add_b(near[i], far[i]) for i in range(3))
    near_own, far_own = near[3], far[3]
    in_sum = add_b(in_keep_grad, in_x)
    down_sum = add_b(down_keep, down_y)
    three_hop = ctx_move(three, 4)
    in_send = jnp.where(y_low, in_sum[:, 1], in_sum[:, 0])
    down_send = jnp.where(x_low, down_sum[..., 384:], down_sum[..., :384])
    in_send, down_send, two = hold(in_send, down_send, two)
    short_query_b, three_hop = hold(short_query, three_hop)
    in_y, down_x = y_swap(in_send), x_swap(down_send)
    one, three_hop = hold(one, three_hop)
    two_got = ctx_move(add_b(two, three_hop), 8)
    one_got = ctx_move(one, 4)
    short_back = attend_back_call(
        short_query_b,
        short_grad,
        short_log,
        short_mixed,
        short_pairs,
        flag=short_flag,
    )
    short_query_g, short_near, short_far = short_back
    short_pair_grad = add_b(short_near, core_swap(short_far))
    stream, attn_branch, ffn_branch, in_y = hold(stream, attn_branch, ffn_branch, in_y)
    (
        grad_value_vec,
        grad_out_vec,
        grad_gain_one,
        grad_bias_one,
        grad_down_vec,
        grad_gain_two,
        grad_bias_two,
        grad_in_vec,
        in_y,
    ) = hold(
        grad_value_vec,
        grad_out_vec,
        grad_gain_one,
        grad_bias_one,
        grad_down_vec,
        grad_gain_two,
        grad_bias_two,
        grad_in_vec,
        in_y,
    )
    long_query_grad = (grad_query * score_scale).astype(jnp.bfloat16)
    short_query_grad = (short_query_g * score_scale).astype(jnp.bfloat16)
    ones_wide = jnp.ones((8, 2 * slot_count), jnp.bfloat16)
    query_sums = product32(ones_wide, long_query_grad, lanes_both) + product32(
        ones_wide, short_query_grad, lanes_both
    )
    (owner_sums,) = place_call(
        vectors_kernel,
        where_me,
        (
            grad_value_vec,
            grad_out_vec,
            grad_gain_one,
            grad_bias_one,
            grad_down_vec,
            grad_gain_two,
            grad_bias_two,
            query_sums,
            grad_in_vec,
            jnp.sum(valid_col * stream * stream, axis=0, keepdims=True),
            jnp.sum(valid_col * attn_branch * attn_branch, axis=0, keepdims=True),
            jnp.sum(valid_col * ffn_branch * ffn_branch, axis=0, keepdims=True),
            jnp.broadcast_to(jnp.sum(valid_col, axis=0, keepdims=True) / 128, (1, 128)),
        ),
        (),
        ((16, 8, 384),),
    )
    owner_sums = owner_sums.astype(jnp.bfloat16)
    owner_sums = add_b(owner_sums, x_swap(owner_sums)).reshape(4, 2, 2, 8, 384)
    owner_sums = jnp.pad(owner_sums, ((0, 0), (0, 0), (0, 0), (0, 0), (0, 192)))

    def back_rows(grads):
        return product32(grads, qkv_weight, (((0,), (1,)), ((), ())))

    short_all = jnp.concatenate([short_query_grad, short_pair_grad], axis=0)
    short_rows_back = back_rows(short_all)
    short_got = y_swap(short_rows_back[rows_here:].astype(jnp.bfloat16))
    in_sum = add_b(jnp.where(y_low, in_sum[:, 0], in_sum[:, 1]), in_y)
    down_sum = add_b(jnp.where(x_low, down_sum[..., :384], down_sum[..., 384:]), down_x)
    ffn_sum = jnp.concatenate([in_sum, down_sum], axis=1)
    def by_z(stack):
        return [
            lax.dynamic_index_in_dim(stack, z_at ^ mask, 0, keepdims=False) for mask in range(4)
        ]

    ffn_own, ffn_first, ffn_second, ffn_third = by_z(ffn_sum)
    ffn_third = ctx_move(ffn_third, 4)
    two_got, one_got, ffn_own, ffn_first, ffn_second, ffn_third = hold(
        two_got, one_got, ffn_own, ffn_first, ffn_second, ffn_third
    )
    two_got, owner_sums, short_got, short_rows_back = hold(
        two_got, owner_sums, short_got, short_rows_back
    )
    ffn_second = add_b(ffn_second, ffn_third)
    long_pair_grad = near_own.astype(jnp.float32)
    for got_part in (far_own, one_got, two_got):
        long_pair_grad = long_pair_grad + got_part.astype(jnp.float32)
    long_pair_grad = long_pair_grad.astype(jnp.bfloat16)
    long_all = jnp.concatenate([long_query_grad, long_pair_grad], axis=0)
    long_back = back_rows(long_all)
    long_back, long_all = hold(long_back, long_all)
    long_got = y_swap(long_back[rows_here:].astype(jnp.bfloat16)).astype(jnp.float32)

    grad_qkv = product32(long_rows, long_all, (((0,), (1,)), ((), ()))) + product32(
        short_rows, short_all, (((0,), (1,)), ((), ()))
    )
    grad_qkv = grad_qkv.astype(jnp.bfloat16).reshape(4, 2, 2, 48, 576)
    grad_qkv = jnp.concatenate([grad_qkv, owner_sums], axis=3)
    core_keep = jnp.where(core_low, grad_qkv[:, :, 0], grad_qkv[:, :, 1])
    core_send = jnp.where(core_low, grad_qkv[:, :, 1], grad_qkv[:, :, 0])
    core_sum = add_b(core_keep, core_swap(core_send))

    own_sum, one_part, two_part, three_part = by_z(core_sum)
    one_part, three_part = ctx_move(one_part, 4), ctx_move(three_part, 4)
    two_part, qkv_hop = hold(add_b(two_part, three_part), three_part)
    two_part = ctx_move(two_part, 8)
    own_sum = sum(part.astype(jnp.float32) for part in (own_sum, one_part, two_part))
    y_keep = jnp.where(y_low, own_sum[0], own_sum[1])
    y_got = y_swap(jnp.where(y_low, own_sum[1], own_sum[0]).astype(jnp.bfloat16))
    own_part = ffn_own
    ffn_first, _ = hold(ffn_first, qkv_hop)
    one_part, two_part = ctx_move(ffn_first, 4), ctx_move(ffn_second, 8)
    one_part, two_part, y_keep = hold(one_part, two_part, y_keep)
    ffn_owned = sum(part.astype(jnp.float32) for part in (own_part, one_part, two_part))
    y_got = y_got.astype(jnp.float32)
    vector_sums = y_keep[48:] + y_got[48:]
    y_keep, y_got = y_keep[:48], y_got[:48]
    low_part, high_part = jnp.where(y_low, y_keep, y_got), jnp.where(y_low, y_got, y_keep)
    owned_qkv = [
        jnp.concatenate(
            [low_part[:, half * i : half * (i + 1)], high_part[:, half * i : half * (i + 1)]],
            axis=1,
        )
        for i in range(3)
    ]

    in_owned = jnp.concatenate([ffn_owned[:96], ffn_owned[96:192]], axis=1)
    in_owned = in_owned.astype(jnp.bfloat16).reshape(2, 48, 768)
    in_mine = jnp.where(core_low, in_owned[0], in_owned[1])
    in_other = core_swap(jnp.where(core_low, in_owned[1], in_owned[0]))
    in_even = jnp.where(core_low, in_mine, in_other).astype(jnp.float32)
    in_odd = jnp.where(core_low, in_other, in_mine).astype(jnp.float32)
    owned_in = jnp.concatenate(
        [
            part[:, 192 * k : 192 * (k + 1)]
            for k in range(4)
            for part in (in_even, in_odd)
        ],
        axis=1,
    )
    owned_out, owned_down = ffn_owned[192:240], ffn_owned[240:]

    short_part = short_rows_back[:rows_here] + short_got.astype(jnp.float32)
    long_part = long_back[:rows_here] + long_got
    own_part = jnp.where(own_long, long_part, short_part)
    far_part = x_swap(jnp.where(own_long, short_part, long_part).astype(jnp.bfloat16))
    tokens_grad = (grad_stream + own_part + far_part.astype(jnp.float32)).astype(jnp.bfloat16)

    def own_piece(row):
        return vector_sums[row, :48]

    rms_values = jnp.sqrt(vector_sums[1:4, 128] / (vector_sums[4, 128] * width))
    return (
        layer_out,
        tokens_grad[None],
        owned_qkv[0],
        owned_qkv[1],
        owned_qkv[2],
        owned_out,
        owned_in,
        owned_down,
        vector_sums[7, :48],
        own_piece(0),
        own_piece(1),
        own_piece(2),
        own_piece(3),
        vector_sums[0, 128:320],
        own_piece(4),
        own_piece(5),
        own_piece(6),
        rms_values,
    )


def layer_body(tokens, *others):
    fits = lax.axis_size("ctx") == 16 and lax.axis_size("fsdp") == 2
    if fits and tokens.shape == (1, 256, 768):
        return fast_body(tokens, *others)
    return body(tokens, *others)


def solution(mesh):
    in_specs = (
        P("fsdp", "ctx", None),
        P("fsdp"),
        P("fsdp", "ctx", None),
        P("ctx", "fsdp"),
        P("ctx", "fsdp"),
        P("ctx", "fsdp"),
        P("ctx", "fsdp"),
        P("ctx", "fsdp"),
        P("ctx", "fsdp"),
        P("ctx"),
        P("ctx"),
        P("ctx"),
        P("ctx"),
        P("ctx"),
        P("ctx"),
        P("ctx"),
        P("ctx"),
        P("ctx"),
    )
    out_specs = (
        P("fsdp", "ctx", None),
        P("fsdp", "ctx", None),
        P("ctx", "fsdp"),
        P("ctx", "fsdp"),
        P("ctx", "fsdp"),
        P("ctx", "fsdp"),
        P("ctx", "fsdp"),
        P("ctx", "fsdp"),
        P("ctx"),
        P("ctx"),
        P("ctx"),
        P("ctx"),
        P("ctx"),
        P("ctx"),
        P("ctx"),
        P("ctx"),
        P("ctx"),
        P(),
    )
    return jax.shard_map(layer_body, mesh=mesh, in_specs=in_specs, out_specs=out_specs, check_vma=False)
```
